512 devices in a mesh: dom: 64 (over x, z, core), cls: 8 (over y).
Axes of the slice: x: 4, y: 8, z: 8, core: 2. Of those that a mesh axis runs over, the one named last changes fastest.
Arguments:
- images: bfloat16 [2048, 9216], P(('dom', 'cls')), may hold values from -64 to 64
- ctf: float32 [2048, 64], P(('dom', 'cls')), may hold values from 0.2 to 1
- inv_noise: float32 [64], replicated, may hold values from 0.5 to 2
- classes: bfloat16 [400, 9216], P('cls'), may hold values from -0.25 to 0.25
- candidates: int32 [2048, 2], P(('dom', 'cls')), may hold values from 0 to 399, as said below
Outputs:
- class_sums: float32 [9216, 400], P('dom', 'cls')
- weight_sums: float32 [400, 64], P('cls')
- evidence: float32 [2048], P(('dom', 'cls'))
The draws below stay inside these ranges and needn't reach their ends.
Inputs may be any that keep to these rules, and one draw needn't show every extreme that they name: `candidates`: each row names 2 different classes. Among the 4 particles of one device, at most 2 name a class of any one block b (classes b * 50 to (b + 1) * 50 - 1); for each index along dom, the 8 devices that share it have one common block that exactly 2 particles of each of them name.
All inputs are finite; a program needn't handle non-finite values.
Results may differ from the reference program's by a relative error of at most 0.0053.
Values may be sent and summed in bfloat16 or wider, within the bound.
No kernel may reach another device: no remote copies, remote signals or barrier semaphores. Data moves between devices by JAX's collectives and lax.ppermute only.
A program may use at most 64 MiB of HBM per device.

```python
import math
import jax
import jax.numpy as jnp
from jax import lax

CYCLES = 64
ANGLES = 72
ROTATIONS = 36
CLASSES = 400
TOP_CAND = 2
PART_DEV = 4
FEATURES = 9216
CLASS_BLOCK = 50
CAPACITY = 2
PARTICLES = 2048
N_CLS = 8


def class_values(key):
    scale_key, shell_key, value_key = jax.random.split(jax.random.fold_in(key, 11), 3)
    overall = jnp.exp(jax.random.uniform(scale_key, (CLASSES, 1, 1, 1), jnp.float32, math.log(0.5), math.log(2.0)))
    shells = jnp.exp(jax.random.uniform(shell_key, (CLASSES, 1, 1, CYCLES), jnp.float32, math.log(0.5), math.log(2.0)))
    raw_values = jnp.clip(jax.random.normal(value_key, (CLASSES, ANGLES, 2, CYCLES), jnp.float32), -6.0, 6.0)
    values = raw_values * overall * shells / math.sqrt(FEATURES)
    return values.reshape(CLASSES, FEATURES)


def candidate_ids(key):
    device_total = PARTICLES // PART_DEV

    def one_device(device):
        device_key = jax.random.fold_in(jax.random.fold_in(key, 23), device)
        group_key = jax.random.fold_in(jax.random.fold_in(key, 29), device // N_CLS)
        hot_block = jax.random.randint(group_key, (), 0, N_CLS)
        order_key, slot_key, base_key, extra_key, swap_key = jax.random.split(device_key, 5)
        shuffled = jax.random.permutation(order_key, PART_DEV)
        chosen = jnp.zeros((PART_DEV,), jnp.int32).at[shuffled[:CAPACITY]].set(1)
        pair_index = jnp.arange(PART_DEV * TOP_CAND, dtype=jnp.int32)
        pair_part = pair_index // TOP_CAND
        pair_slot = pair_index % TOP_CAND
        first_hot = (pair_slot == 0) & (chosen[pair_part] == 1)
        remaining = 1 - first_hot.astype(jnp.int32)
        ranking = jnp.clip(jnp.cumsum(remaining) - 1, 0, (N_CLS - 1) * CAPACITY - 1)
        slot_order = jax.random.permutation(slot_key, (N_CLS - 1) * CAPACITY)
        other_block = slot_order[ranking] // CAPACITY
        other_block = other_block + (other_block >= hot_block).astype(jnp.int32)
        owner_block = jnp.where(first_hot, hot_block, other_block)
        base_offset = jax.random.randint(base_key, (PART_DEV,), 0, CLASS_BLOCK)
        extra_offset = jax.random.randint(extra_key, (PART_DEV,), 0, CLASS_BLOCK - 1)
        offsets = jnp.where(pair_slot == 0, base_offset[pair_part], (base_offset[pair_part] + 1 + extra_offset[pair_part]) % CLASS_BLOCK)
        class_ids = (owner_block * CLASS_BLOCK + offsets).reshape(PART_DEV, TOP_CAND)
        swap_flag = jax.random.randint(swap_key, (PART_DEV, 1), 0, 2)
        return jnp.where(swap_flag == 1, class_ids[:, ::-1], class_ids)
    device_ids = jax.vmap(one_device)(jnp.arange(device_total, dtype=jnp.int32))
    return device_ids.reshape(PARTICLES, TOP_CAND).astype(jnp.int32)


def draw_classes(key, part):
    return class_values(key).astype(jnp.bfloat16)


def draw_candidates(key, part):
    return candidate_ids(key)


def draw_images(key, part):
    values = jax.random.normal(jax.random.fold_in(key, 41), (PARTICLES, FEATURES), jnp.float32)
    return jnp.clip(values, -8.0, 8.0).astype(jnp.bfloat16)


def steps_of(stream_key, extent, cuts, low, largest):
    gain = 1.0
    for position, blocks in cuts:
        draws = jax.random.uniform(jax.random.fold_in(jax.random.fold_in(stream_key, 6), position), (blocks,), jnp.float32, low / len(cuts), largest / len(cuts))
        gain = gain * jnp.repeat(jnp.exp(draws), extent[position] // blocks).reshape((-1,) + (1,) * (len(extent) - 1 - position))
    return gain


def setup_inputs(seed: int = 0) -> dict:
    key_list = jax.random.split(jax.random.key(seed), 6)
    return {
        "images": draw_images(jax.random.fold_in(key_list[5], 71), 0),
        "ctf": jnp.clip(0.2 + 0.8 * jax.random.uniform(key_list[1], (PARTICLES, CYCLES), jnp.float32) ** steps_of(key_list[1], (PARTICLES, CYCLES), ((0, 512),), -0.2, 0.2), 0.2, 1.0),
        "inv_noise": jnp.clip(jnp.exp(jax.random.uniform(key_list[2], (CYCLES,), jnp.float32, math.log(0.5), math.log(2.0))), 0.5, 2.0),
        "classes": draw_classes(jax.random.fold_in(key_list[5], 71), 0),
        "candidates": draw_candidates(jax.random.fold_in(key_list[5], 71), 0),
    }


def class_frame(data, rotation):
    shaped = data.reshape(data.shape[0], ANGLES, 2 * CYCLES)
    doubled = jnp.concatenate([shaped, shaped], axis=1)
    start_angle = (rotation * (ANGLES // ROTATIONS)).astype(jnp.int32)
    moved = lax.dynamic_slice_in_dim(doubled, start_angle, ANGLES, 1)
    return moved.reshape(data.shape[0], 2 * CYCLES * ANGLES)


def reference(images, ctf, inv_noise, classes, candidates):
    ctf_noise = ctf * inv_noise[None, :]
    factor = jnp.tile(ctf_noise, (1, 2 * ANGLES))
    weighted = (images.astype(jnp.float32) * factor).astype(jnp.bfloat16)
    quadratic = (ctf * ctf * inv_noise[None, :]).astype(jnp.bfloat16)
    quad_wide = quadratic.astype(jnp.float32)
    class_wide = classes.astype(jnp.float32)
    energy = jnp.sum(jnp.square(class_wide).reshape(CLASSES, 2 * ANGLES, CYCLES), axis=1)
    picked = classes[candidates].astype(jnp.float32)
    norm_term = jnp.einsum("nr,njr->nj", quad_wide, energy[candidates], precision=lax.Precision.HIGHEST)

    def correlate(rotation):
        framed = class_frame(weighted, rotation).astype(jnp.float32)
        return jnp.einsum("nf,njf->nj", framed, picked, precision=lax.Precision.HIGHEST)

    cross = lax.map(correlate, jnp.arange(ROTATIONS, dtype=jnp.int32))
    logits = jnp.transpose(cross, (1, 2, 0)) - 0.5 * norm_term[:, :, None]
    highest = jnp.max(logits, axis=(1, 2))
    totals = jnp.sum(jnp.exp(logits - highest[:, None, None]), axis=(1, 2))
    evidence = highest + jnp.log(totals)
    posterior = jnp.exp(logits - evidence[:, None, None]).astype(jnp.bfloat16)
    post_wide = posterior.astype(jnp.float32)

    def accumulate(carry, rotation):
        framed = class_frame(weighted, rotation).astype(jnp.float32)
        weight_now = lax.dynamic_index_in_dim(post_wide, rotation, 2, keepdims=False)
        return carry + weight_now[:, :, None] * framed[:, None, :], rotation

    start_sums = jnp.zeros((PARTICLES, TOP_CAND, FEATURES), jnp.float32)
    contrib, unused = lax.scan(accumulate, start_sums, jnp.arange(ROTATIONS, dtype=jnp.int32))
    flat_ids = candidates.reshape(-1)
    sums = jax.ops.segment_sum(contrib.reshape(PARTICLES * TOP_CAND, FEATURES), flat_ids, num_segments=CLASSES)
    weight_total = jnp.sum(post_wide, axis=2)
    ctf_terms = weight_total[:, :, None] * quad_wide[:, None, :]
    weight_sums = jax.ops.segment_sum(ctf_terms.reshape(PARTICLES * TOP_CAND, CYCLES), flat_ids, num_segments=CLASSES)
    return (sums.T, weight_sums, evidence)
```

```python
import jax
import jax.numpy as jnp
from jax import lax
from jax.experimental import pallas as pl
from jax.experimental.pallas import tpu as pltpu
from jax.sharding import Mesh, PartitionSpec as P

CYCLES = 64
ROTATIONS = 36
BLOCK = 256
FEATURES = ROTATIONS * BLOCK
LANES = 128
HALF = 64
ROWS = 16
GROUPS = 64
SLICE = FEATURES // GROUPS
CHUNKS = SLICE // 16
PAY_ROWS = SLICE // 2
NEGATIVE = -1e30
P_LANE = 120
F32 = jnp.float32
BF16 = jnp.bfloat16
HIGH = lax.Precision.HIGHEST


def lanes_of(shape):
    return lax.broadcasted_iota(jnp.int32, shape, len(shape) - 1)


def rows_of(shape):
    return lax.broadcasted_iota(jnp.int32, shape, len(shape) - 2)


def call(body, outs, *args):
    return pl.pallas_call(
        body,
        out_shape=outs,
        compiler_params=pltpu.CompilerParams(vmem_limit_bytes=48 * 1024 * 1024),
    )(*args)


def pack_body(class_block, images_ref, ctf_ref, noise_ref, cands_ref, out_ref):
    part = images_ref.shape[0]
    ctf = ctf_ref[...]
    noise = noise_ref[...]
    ctf_noise = ctf * noise
    factor = jnp.concatenate([ctf_noise, ctf_noise], axis=1)
    quad = (ctf * ctf * noise).astype(BF16)
    quad = jnp.concatenate([quad, quad], axis=1)
    cands = cands_ref[...]
    first = jnp.broadcast_to(cands[0:1, :], (ROWS, part))
    second = jnp.broadcast_to(cands[1:2, :], (ROWS, part))
    row = rows_of((ROWS, part))
    low = (row // 2) * class_block
    hit = ((first >= low) & (first < low + class_block)) | (
        (second >= low) & (second < low + class_block)
    )
    hit = hit.astype(F32)
    taken = jnp.zeros((ROWS, 1), F32)
    columns = []
    slot = (rows_of((ROWS, 1)) % 2).astype(F32)
    for p in range(part):
        now = hit[:, p : p + 1]
        columns.append(now * (taken == slot).astype(F32))
        taken = taken + now
    packing = jnp.concatenate(columns, axis=1)
    valid = jnp.sum(packing, axis=1, keepdims=True)
    own = jnp.sum(packing * lanes_of((ROWS, part)).astype(F32), axis=1, keepdims=True)
    base = low[:, 0:1].astype(F32)
    id_a = jnp.sum(packing * first.astype(F32), axis=1, keepdims=True) - base
    id_b = jnp.sum(packing * second.astype(F32), axis=1, keepdims=True) - base
    lane = lanes_of((ROWS, LANES))
    klane = (lane - HALF).astype(F32)
    in_block = (lane >= HALF) & (lane < HALF + class_block)
    flags = (in_block & ((klane == id_a) | (klane == id_b))) | (
        (lane - P_LANE).astype(F32) == own
    )
    flags = flags.astype(F32) * (valid > 0.5).astype(F32)
    packing = packing.astype(BF16)
    quad_rows = jnp.dot(packing, quad, preferred_element_type=F32)
    out_ref[:, FEATURES : FEATURES + LANES] = jnp.where(lane < HALF, quad_rows, flags).astype(BF16)
    wide = jnp.concatenate([factor] * 4, axis=1)
    step = 4 * LANES
    for t in range(FEATURES // step):
        part_w = (images_ref[:, t * step : (t + 1) * step].astype(F32) * wide).astype(BF16)
        out_ref[:, t * step : (t + 1) * step] = jnp.dot(
            packing, part_w, preferred_element_type=F32
        ).astype(BF16)


def prep_body(classes_ref, table_ref, energy_ref):
    count = classes_ref.shape[0]
    acc = jnp.zeros((count, LANES), F32)
    for b in range(ROTATIONS):
        block = classes_ref[:, b * BLOCK : (b + 1) * BLOCK]
        table_ref[b * HALF : b * HALF + count, :] = block
        table_ref[b * HALF + count : (b + 1) * HALF, :] = jnp.zeros((HALF - count, BLOCK), BF16)
        wide = block.astype(F32)
        square = wide * wide
        acc = acc + square[:, :LANES] + square[:, LANES:]
    acc = acc + pltpu.roll(acc, HALF, 1)
    energy_ref[...] = jnp.zeros((LANES, LANES), F32)
    energy_ref[0:count, :] = acc
    energy_ref[HALF : HALF + count, :] = acc


def row_facts(meta):
    lane = lanes_of(meta.shape)
    flags = jnp.where((lane >= HALF) & (lane < P_LANE), meta, 0.0)
    live = (flags + pltpu.roll(flags, HALF, 1)) > 0.5
    marks = jnp.where(lane >= P_LANE, meta, 0.0)
    valid = jnp.sum(marks, axis=1, keepdims=True)
    own = jnp.sum(marks * (lane - P_LANE).astype(F32), axis=1, keepdims=True)
    source = (rows_of(meta.shape) // 2 * 4).astype(F32)
    spot = (lane.astype(F32) == source + own) & (valid > 0.5)
    return live, spot


def cross_body(rows_ref, table_ref, energy_ref, logits_ref, stats_ref, blocks_ref, acc_ref):
    total_rows = ROTATIONS * ROWS
    for b in range(ROTATIONS):
        blocks_ref[b * ROWS : (b + 1) * ROWS, :] = rows_ref[:, b * BLOCK : (b + 1) * BLOCK]
    for m in range(ROTATIONS // 4):
        g = lax.dot_general(
            blocks_ref[...],
            table_ref[m * BLOCK : (m + 1) * BLOCK, :],
            (((1,), (1,)), ((), ())),
            preferred_element_type=F32,
        )
        for h in range(2):
            tile = g[:, h * LANES : (h + 1) * LANES]
            shift = (2 * m + h) * 2 * ROWS
            if shift == 0:
                acc_ref[...] = tile
            else:
                acc_ref[0 : total_rows - shift, :] += tile[shift:, :]
                acc_ref[total_rows - shift :, :] += tile[:shift, :]
    meta = rows_ref[:, FEATURES : FEATURES + LANES].astype(F32)
    lane = lanes_of((ROWS, LANES))
    live, spot = row_facts(meta)
    quad = jnp.where(lane < HALF, meta, 0.0)
    norm = 0.5 * lax.dot_general(
        quad, energy_ref[...], (((1,), (1,)), ((), ())), precision=HIGH, preferred_element_type=F32
    )
    left = live & (lane < HALF)
    best = jnp.full((ROWS, LANES), NEGATIVE, F32)
    for r in range(ROTATIONS):
        nxt = (r + 1) % ROTATIONS
        mixed = jnp.where(
            lane < HALF,
            acc_ref[r * ROWS : (r + 1) * ROWS, :],
            acc_ref[nxt * ROWS : (nxt + 1) * ROWS, :],
        )
        value = mixed + pltpu.roll(mixed, HALF, 1) - norm
        logits_ref[r * ROWS : (r + 1) * ROWS, :] = value
        best = jnp.maximum(best, jnp.where(left, value, NEGATIVE))
    peak = jnp.max(best, axis=1, keepdims=True)
    total = jnp.zeros((ROWS, LANES), F32)
    for r in range(ROTATIONS):
        value = logits_ref[r * ROWS : (r + 1) * ROWS, :]
        total = total + jnp.where(left, jnp.exp(value - peak), 0.0)
    total = jnp.sum(total, axis=1, keepdims=True)
    stats_ref[0:1, :] = jnp.max(jnp.where(spot, peak, NEGATIVE), axis=0, keepdims=True)
    stats_ref[1:2, :] = jnp.sum(jnp.where(spot, total, 0.0), axis=0, keepdims=True)


def turn_body(blocks_ref, out_ref):
    out_ref[...] = blocks_ref[...].astype(F32).T.astype(BF16)


def sums_body(stats_ref, logits_ref, meta_ref, turned_ref, pay_ref, evid_ref, left_ref, right_ref):
    total_rows = ROTATIONS * ROWS
    peaks = stats_ref[:, 0, :]
    totals = stats_ref[:, 1, :]
    highest = jnp.max(peaks, axis=0, keepdims=True)
    total = jnp.sum(totals * jnp.exp(peaks - highest), axis=0, keepdims=True)
    evidence = highest + jnp.log(total)
    evid_ref[...] = evidence
    meta = meta_ref[...].astype(F32)
    live, spot = row_facts(meta)
    lane = lanes_of((ROWS, LANES))
    row_evidence = jnp.sum(jnp.where(spot, evidence, 0.0), axis=1, keepdims=True)
    weight = jnp.zeros((ROWS, LANES), F32)
    for r in range(ROTATIONS):
        value = logits_ref[r * ROWS : (r + 1) * ROWS, :]
        post = jnp.where(live, jnp.exp(value - row_evidence), 0.0).astype(BF16).astype(F32)
        weight = weight + post
        one = jnp.where(lane < HALF, post, 0.0).astype(BF16)
        two = jnp.where(lane < HALF, 0.0, post).astype(BF16)
        left_ref[r * ROWS : (r + 1) * ROWS, :] = one
        left_ref[total_rows + r * ROWS : total_rows + (r + 1) * ROWS, :] = one
        right_ref[r * ROWS : (r + 1) * ROWS, :] = two
        right_ref[total_rows + r * ROWS : total_rows + (r + 1) * ROWS, :] = two
    quad = jnp.where(lane < HALF, meta, 0.0)
    quad = quad + pltpu.roll(quad, HALF, 1)
    filters = jnp.dot(weight.T, quad, precision=HIGH, preferred_element_type=F32)
    pair = jnp.where(lanes_of((32, LANES)) < HALF, filters[0:32, :], filters[32:64, :]).astype(BF16)
    base = GROUPS // 2 * PAY_ROWS
    pay_ref[0, base : base + 32, :] = pair
    pay_ref[1, base : base + 32, :] = pair

    def turned_posterior(b):
        start = (ROTATIONS - b) * ROWS
        return (
            left_ref[start : start + total_rows, :]
            + right_ref[start - ROWS : start - ROWS + total_rows, :]
        )

    for m in range(ROTATIONS // 4):
        mixed = jnp.concatenate([turned_posterior(4 * m), turned_posterior(4 * m + 2)], axis=1)
        out = jnp.dot(turned_ref[...], mixed, preferred_element_type=F32).astype(BF16)
        for e in range(4):
            for i in range(16):
                q = (4 * m + e) * 16 + i
                group, j = q // CHUNKS, q % CHUNKS
                core, spot_at = group % 2, group // 2 * PAY_ROWS
                piece = out[i * 16 : (i + 1) * 16, e * HALF : (e + 1) * HALF]
                if j < CHUNKS - 1:
                    at = spot_at + j // 2 * 16
                    lo = j % 2 * HALF
                    pay_ref[core, at : at + 16, lo : lo + HALF] = piece
                else:
                    at = spot_at + PAY_ROWS - 8
                    pay_ref[core, at : at + 8, 0:HALF] = piece[0:8, :]
                    pay_ref[core, at : at + 8, HALF:LANES] = piece[8:16, :]


def combine_body(pay_ref, out_ref):
    half = GROUPS // 2
    base = half * PAY_ROWS
    weights = (pay_ref[0, base : base + 32, :].astype(F32) + pay_ref[1, base : base + 32, :].astype(F32)).astype(BF16)
    for g in range(half):
        at = g * PAY_ROWS
        out_ref[g, 0:PAY_ROWS, :] = (
            pay_ref[0, at : at + PAY_ROWS, :].astype(F32) + pay_ref[1, at : at + PAY_ROWS, :].astype(F32)
        ).astype(BF16)
        out_ref[g, PAY_ROWS : PAY_ROWS + 32, :] = weights


def final_body(parts_ref, sums_ref, weights_ref):
    count = weights_ref.shape[0]
    acc = parts_ref[0, :, :].astype(F32)
    for g in range(1, GROUPS // 2):
        acc = acc + parts_ref[g, :, :].astype(F32)
    pieces = []
    for j in range(CHUNKS - 1):
        lo = j % 2 * HALF
        pieces.append(acc[j // 2 * 16 : j // 2 * 16 + 16, lo : lo + HALF])
    pieces.append(acc[PAY_ROWS - 8 : PAY_ROWS, 0:HALF])
    pieces.append(acc[PAY_ROWS - 8 : PAY_ROWS, HALF:LANES])
    full = jnp.concatenate(pieces, axis=0)
    sums_ref[...] = full.T[0:count, :]
    weights_ref[0:32, :] = acc[PAY_ROWS : PAY_ROWS + 32, 0:HALF]
    weights_ref[32:count, :] = acc[PAY_ROWS : PAY_ROWS + count - 32, HALF:LANES]


def shards(images, ctf, inv_noise, classes, candidates):
    class_block = classes.shape[0]
    my_index = lax.axis_index("cls")
    total_rows = ROTATIONS * ROWS
    width = FEATURES + LANES
    shape = jax.ShapeDtypeStruct

    def swap(value, axes):
        return lax.all_to_all(value, axes, split_axis=0, concat_axis=0, tiled=True)

    def pack(*refs):
        pack_body(class_block, *refs)

    packed = call(
        pack, shape((ROWS, width), BF16), images, ctf, inv_noise.reshape(1, CYCLES), candidates.T
    )
    rows = swap(packed.reshape(8, 2, width), "cls").reshape(ROWS, width)
    table, energy = call(
        prep_body,
        (shape((ROTATIONS * HALF, BLOCK), BF16), shape((LANES, LANES), F32)),
        classes,
    )
    logits, stats, blocks = pl.pallas_call(
        cross_body,
        out_shape=(
            shape((total_rows, LANES), F32),
            shape((2, LANES), F32),
            shape((total_rows, BLOCK), BF16),
        ),
        scratch_shapes=[pltpu.VMEM((total_rows, LANES), F32)],
        compiler_params=pltpu.CompilerParams(vmem_limit_bytes=48 * 1024 * 1024),
    )(rows, table, energy)
    group_stats = swap(jnp.broadcast_to(stats[None], (8, 2, LANES)), "cls")
    turned = call(turn_body, shape((BLOCK, total_rows), BF16), blocks)
    meta = rows[:, FEATURES:]
    pay_total = GROUPS // 2 * PAY_ROWS + 32
    pay, evidence = pl.pallas_call(
        sums_body,
        out_shape=(shape((2, pay_total, LANES), BF16), shape((1, LANES), F32)),
        scratch_shapes=[
            pltpu.VMEM((2 * total_rows, LANES), BF16),
            pltpu.VMEM((2 * total_rows, LANES), BF16),
        ],
        compiler_params=pltpu.CompilerParams(vmem_limit_bytes=48 * 1024 * 1024),
    )(group_stats, logits, meta, turned)
    both = swap(pay, "core")
    merged = call(combine_body, shape((GROUPS // 2, PAY_ROWS + 32, LANES), BF16), both)
    parts = swap(merged, ("x", "z"))
    sums, weight_sums = call(
        final_body, (shape((class_block, SLICE), F32), shape((class_block, CYCLES), F32)), parts
    )
    own = lax.dynamic_slice(evidence.reshape(LANES), (my_index * 4,), (4,))
    return sums.T, weight_sums, own


def solution(mesh):
    fine = Mesh(mesh.devices.reshape(4, 8, 2, 8), ("x", "z", "core", "cls"))
    dom = ("x", "z", "core")
    every = dom + ("cls",)
    in_specs = (P(every, None), P(every, None), P(), P("cls", None), P(every, None))
    out_specs = (P(dom, "cls"), P("cls", None), P(every))
    return jax.shard_map(shards, mesh=fine, in_specs=in_specs, out_specs=out_specs, check_vma=False)
```

```python
import jax
import jax.numpy as jnp
from jax import lax
from jax.experimental import pallas as pl
from jax.experimental.pallas import tpu as pltpu
from jax.sharding import Mesh, PartitionSpec as P

CYCLES = 64
ROTATIONS = 36
BLOCK = 256
FEATURES = ROTATIONS * BLOCK
LANES = 128
HALF = 64
ROWS = 16
GROUPS = 64
CLASSES = 50
SLICE = FEATURES // GROUPS
CHUNKS = SLICE // 16
PAY_ROWS = SLICE // 2
NEGATIVE = -1e30
P_LANE = 120
F32 = jnp.float32
BF16 = jnp.bfloat16
HIGH = lax.Precision.HIGHEST


def lanes_of(shape):
    return lax.broadcasted_iota(jnp.int32, shape, len(shape) - 1)


def rows_of(shape):
    return lax.broadcasted_iota(jnp.int32, shape, len(shape) - 2)


def call(body, outs, *args, in_specs=None, scratch=(), micros=0):
    more = {} if in_specs is None else {"in_specs": in_specs}
    if micros:
        more["cost_estimate"] = pl.CostEstimate(
            flops=0, transcendentals=0, bytes_accessed=micros * 3_000_000
        )
    return pl.pallas_call(
        body,
        out_shape=outs,
        scratch_shapes=list(scratch),
        compiler_params=pltpu.CompilerParams(vmem_limit_bytes=48 * 1024 * 1024),
        **more,
    )(*args)


def pack_body(class_block, images_any, ctf_any, noise_any, cands_any, out_ref, images_ref, ctf_ref, noise_ref, cands_ref, sems):
    copies = [
        pltpu.make_async_copy(source, target, sems.at[i])
        for i, (source, target) in enumerate(
            (
                (cands_any, cands_ref),
                (ctf_any, ctf_ref),
                (noise_any, noise_ref),
                (images_any, images_ref),
            )
        )
    ]
    for copy in copies:
        copy.start()
    for copy in copies:
        copy.wait()
    part = images_ref.shape[0]
    ctf = ctf_ref[...]
    noise = noise_ref[...]
    ctf_noise = ctf * noise
    factor = jnp.concatenate([ctf_noise, ctf_noise], axis=1)
    quad = (ctf * ctf * noise).astype(BF16)
    quad = jnp.concatenate([quad, quad], axis=1)
    cands = cands_ref[...]
    first = jnp.broadcast_to(cands[0:1, :], (ROWS, part))
    second = jnp.broadcast_to(cands[1:2, :], (ROWS, part))
    row = rows_of((ROWS, part))
    low = (row // 2) * class_block
    hit = ((first >= low) & (first < low + class_block)) | (
        (second >= low) & (second < low + class_block)
    )
    hit = hit.astype(F32)
    taken = jnp.zeros((ROWS, 1), F32)
    columns = []
    slot = (rows_of((ROWS, 1)) % 2).astype(F32)
    for p in range(part):
        now = hit[:, p : p + 1]
        columns.append(now * (taken == slot).astype(F32))
        taken = taken + now
    packing = jnp.concatenate(columns, axis=1)
    valid = jnp.sum(packing, axis=1, keepdims=True)
    own = jnp.sum(packing * lanes_of((ROWS, part)).astype(F32), axis=1, keepdims=True)
    base = low[:, 0:1].astype(F32)
    id_a = jnp.sum(packing * first.astype(F32), axis=1, keepdims=True) - base
    id_b = jnp.sum(packing * second.astype(F32), axis=1, keepdims=True) - base
    lane = lanes_of((ROWS, LANES))
    klane = (lane - HALF).astype(F32)
    in_block = (lane >= HALF) & (lane < HALF + class_block)
    flags = (in_block & ((klane == id_a) | (klane == id_b))) | (
        (lane - P_LANE).astype(F32) == own
    )
    flags = flags.astype(F32) * (valid > 0.5).astype(F32)
    packing = packing.astype(BF16)

    def put(value, start, size):
        value = value.astype(BF16)
        for owner in range(ROWS // 2):
            out_ref[owner, :, start : start + size] = value[2 * owner : 2 * owner + 2, :]

    quad_rows = jnp.dot(packing, quad, preferred_element_type=F32)
    put(jnp.where(lane < HALF, quad_rows, flags), FEATURES, LANES)
    wide = jnp.concatenate([factor] * 4, axis=1)
    step = 4 * LANES
    for t in range(FEATURES // step):
        part_w = (images_ref[:, t * step : (t + 1) * step].astype(F32) * wide).astype(BF16)
        put(jnp.dot(packing, part_w, preferred_element_type=F32), t * step, step)


def prep_body(classes_ref, table_ref, energy_ref):
    count = classes_ref.shape[0]
    acc = jnp.zeros((count, LANES), F32)
    for b in range(ROTATIONS):
        block = classes_ref[:, b * BLOCK : (b + 1) * BLOCK]
        table_ref[b * HALF : b * HALF + count, :] = block
        table_ref[b * HALF + count : (b + 1) * HALF, :] = jnp.zeros((HALF - count, BLOCK), BF16)
        wide = block.astype(F32)
        square = wide * wide
        acc = acc + square[:, :LANES] + square[:, LANES:]
    acc = acc + pltpu.roll(acc, HALF, 1)
    energy_ref[...] = jnp.zeros((LANES, LANES), F32)
    energy_ref[0:count, :] = acc
    energy_ref[HALF : HALF + count, :] = acc


def row_facts(meta):
    lane = lanes_of(meta.shape)
    flags = jnp.where((lane >= HALF) & (lane < P_LANE), meta, 0.0)
    live = (flags + pltpu.roll(flags, HALF, 1)) > 0.5
    marks = jnp.where(lane >= P_LANE, meta, 0.0)
    valid = jnp.sum(marks, axis=1, keepdims=True)
    own = jnp.sum(marks * (lane - P_LANE).astype(F32), axis=1, keepdims=True)
    source = (rows_of(meta.shape) // 2 * 4).astype(F32)
    spot = (lane.astype(F32) == source + own) & (valid > 0.5)
    return live, spot


def cross_body(rows_ref, table_ref, energy_ref, logits_ref, stats_ref, blocks_ref, acc_ref):
    total_rows = ROTATIONS * ROWS
    for b in range(ROTATIONS):
        blocks_ref[b * ROWS : (b + 1) * ROWS, :] = rows_ref[:, b * BLOCK : (b + 1) * BLOCK]
    for m in range(ROTATIONS // 4):
        g = lax.dot_general(
            blocks_ref[0:total_rows, :],
            table_ref[m * BLOCK : (m + 1) * BLOCK, :],
            (((1,), (1,)), ((), ())),
            preferred_element_type=F32,
        )
        for h in range(2):
            tile = g[:, h * LANES : (h + 1) * LANES]
            shift = (2 * m + h) * 2 * ROWS
            if shift == 0:
                acc_ref[...] = tile
            else:
                acc_ref[0 : total_rows - shift, :] += tile[shift:, :]
                acc_ref[total_rows - shift :, :] += tile[:shift, :]
    raw = rows_ref[:, FEATURES : FEATURES + LANES]
    blocks_ref[total_rows:, 0:LANES] = raw
    blocks_ref[total_rows:, LANES:] = jnp.zeros((ROWS, LANES), BF16)
    meta = raw.astype(F32)
    lane = lanes_of((ROWS, LANES))
    live, spot = row_facts(meta)
    quad = jnp.where(lane < HALF, meta, 0.0)
    norm = 0.5 * lax.dot_general(
        quad, energy_ref[...], (((1,), (1,)), ((), ())), precision=HIGH, preferred_element_type=F32
    )
    left = live & (lane < HALF)
    best = jnp.full((ROWS, LANES), NEGATIVE, F32)
    for r in range(ROTATIONS):
        nxt = (r + 1) % ROTATIONS
        mixed = jnp.where(
            lane < HALF,
            acc_ref[r * ROWS : (r + 1) * ROWS, :],
            acc_ref[nxt * ROWS : (nxt + 1) * ROWS, :],
        )
        value = mixed + pltpu.roll(mixed, HALF, 1) - norm
        logits_ref[r * ROWS : (r + 1) * ROWS, :] = value
        best = jnp.maximum(best, jnp.where(left, value, NEGATIVE))
    peak = jnp.max(best, axis=1, keepdims=True)
    total = jnp.zeros((ROWS, LANES), F32)
    for r in range(ROTATIONS):
        value = logits_ref[r * ROWS : (r + 1) * ROWS, :]
        total = total + jnp.where(left, jnp.exp(value - peak), 0.0)
    total = jnp.sum(total, axis=1, keepdims=True)
    peak_row = jnp.max(jnp.where(spot, peak, NEGATIVE), axis=0, keepdims=True)
    total_row = jnp.sum(jnp.where(spot, total, 0.0), axis=0, keepdims=True)
    for d in range(stats_ref.shape[0]):
        stats_ref[d, 0:1, :] = peak_row
        stats_ref[d, 1:2, :] = total_row


def turn_body(core_ref, blocks_ref, logits_ref, mine_ref, theirs_ref, logits_out_ref):
    total_rows = ROTATIONS * ROWS
    second = core_ref[0] == 1
    value = blocks_ref[0:total_rows, :].astype(F32)
    rolled = pltpu.roll(value, BLOCK - SLICE, 1)
    after = jnp.concatenate([rolled[ROWS:, :], rolled[:ROWS, :]], axis=0)
    moved = jnp.where(lanes_of(value.shape) < BLOCK - SLICE, rolled, after)
    mine_ref[...] = jnp.where(second, moved, value).T.astype(BF16)
    theirs_ref[0:BLOCK, :] = jnp.where(second, value, moved).T.astype(BF16)
    theirs_ref[BLOCK:, 0:LANES] = blocks_ref[total_rows:, 0:LANES]
    theirs_ref[BLOCK:, LANES:] = jnp.zeros((ROWS, total_rows - LANES), BF16)
    logits_out_ref[...] = logits_ref[...]


def sums_body(
    core_ref,
    stats_ref,
    mine_logits_ref,
    sibling_logits_ref,
    mine_meta_ref,
    sibling_meta_ref,
    mine_turned_ref,
    sibling_turned_ref,
    pay_ref,
    evid_ref,
    *tables,
):
    total_rows = ROTATIONS * ROWS
    core = core_ref[0]
    lane = lanes_of((ROWS, LANES))
    weights, quads = [], []
    for g, (logits_ref, meta_ref) in enumerate(
        ((mine_logits_ref, mine_meta_ref), (sibling_logits_ref, sibling_meta_ref))
    ):
        left_ref, right_ref = tables[2 * g], tables[2 * g + 1]
        place = (core if g == 0 else 1 - core) * 8
        stats = stats_ref[pl.ds(place, 8), :, :]
        peaks = stats[:, 0, :]
        totals = stats[:, 1, :]
        highest = jnp.max(peaks, axis=0, keepdims=True)
        total = jnp.sum(totals * jnp.exp(peaks - highest), axis=0, keepdims=True)
        evidence = highest + jnp.log(total)
        if g == 0:
            evid_ref[...] = evidence
        meta = meta_ref[...].astype(F32)
        live, spot = row_facts(meta)
        row_evidence = jnp.sum(jnp.where(spot, evidence, 0.0), axis=1, keepdims=True)
        weight = jnp.zeros((ROWS, LANES), F32)
        for r in range(ROTATIONS):
            value = logits_ref[r * ROWS : (r + 1) * ROWS, :]
            post = jnp.where(live, jnp.exp(value - row_evidence), 0.0).astype(BF16).astype(F32)
            weight = weight + post
            one = jnp.where(lane < HALF, post, 0.0).astype(BF16)
            two = jnp.where(lane < HALF, 0.0, post).astype(BF16)
            left_ref[r * ROWS : (r + 1) * ROWS, :] = one
            left_ref[total_rows + r * ROWS : total_rows + (r + 1) * ROWS, :] = one
            right_ref[r * ROWS : (r + 1) * ROWS, :] = two
            right_ref[total_rows + r * ROWS : total_rows + (r + 1) * ROWS, :] = two
        quad = jnp.where(lane < HALF, meta, 0.0)
        quads.append(quad + pltpu.roll(quad, HALF, 1))
        weights.append(weight)
    weight = jnp.concatenate(weights, axis=0)
    quad = jnp.concatenate(quads, axis=0)
    by_class = jnp.dot(weight.T, quad, precision=HIGH, preferred_element_type=F32)
    by_shell = jnp.dot(quad.T, weight, precision=HIGH, preferred_element_type=F32)[0:HALF, :]
    tail = jnp.where(lane < HALF, by_class[0:16, :], by_class[16:32, :]).astype(BF16)
    wide = lanes_of((HALF, LANES))
    spare = jnp.where(
        (wide >= CLASSES) & (wide < HALF),
        pltpu.roll(by_shell, CLASSES - 32, 1),
        jnp.where(wide >= HALF + CLASSES, pltpu.roll(by_shell, CLASSES - 46, 1), 0.0),
    ).astype(BF16)
    for xz in range(GROUPS // 2):
        pay_ref[xz, 0:HALF, :] = spare
        pay_ref[xz, PAY_ROWS : PAY_ROWS + 16, :] = tail

    def turned_posterior(g, b, c):
        first = (ROTATIONS - b) * ROWS
        second = (ROTATIONS - c) * ROWS
        return (
            tables[2 * g][first : first + total_rows, :]
            + tables[2 * g + 1][second : second + total_rows, :]
        )

    for b in range(CHUNKS):
        kept = [i for i in range(16) if (16 * b + i) // CHUNKS % 2 == 0]
        bands = []
        for i in kept:
            if bands and bands[-1][1] == i:
                bands[-1][1] = i + 1
            else:
                bands.append([i, i + 1])
        out = jnp.zeros((16 * len(kept), BLOCK), F32)
        for g, turned_ref in enumerate((mine_turned_ref, sibling_turned_ref)):
            left = jnp.concatenate([turned_ref[16 * lo : 16 * hi, :] for lo, hi in bands], axis=0)
            mixed = jnp.concatenate(
                [turned_posterior(g, b, b + 9), turned_posterior(g, b + 18, b + 27)], axis=1
            )
            out = out + jnp.dot(left, mixed, preferred_element_type=F32)
        out = out.astype(BF16)
        for e in range(4):
            for n, i in enumerate(kept):
                q = (b + 9 * e) * 16 + i
                xz, j = q // CHUNKS // 2, q % CHUNKS
                piece = out[n * 16 : (n + 1) * 16, e * HALF : e * HALF + CLASSES]
                if j < CHUNKS - 1:
                    at = j // 2 * 16
                    lo = j % 2 * HALF
                    pay_ref[xz, at : at + 16, lo : lo + CLASSES] = piece
                else:
                    pay_ref[xz, PAY_ROWS - 8 : PAY_ROWS, 0:CLASSES] = piece[0:8, :]
                    pay_ref[xz, PAY_ROWS - 8 : PAY_ROWS, HALF : HALF + CLASSES] = piece[8:16, :]


def final_body(parts_ref, sums_ref, weights_ref):
    acc = parts_ref[0, :, :].astype(F32)
    for g in range(1, GROUPS // 2):
        acc = acc + parts_ref[g, :, :].astype(F32)
    pieces = []
    for j in range(CHUNKS - 1):
        lo = j % 2 * HALF
        pieces.append(acc[j // 2 * 16 : j // 2 * 16 + 16, lo : lo + HALF])
    pieces.append(acc[PAY_ROWS - 8 : PAY_ROWS, 0:HALF])
    pieces.append(acc[PAY_ROWS - 8 : PAY_ROWS, HALF:LANES])
    full = jnp.concatenate(pieces, axis=0)
    sums_ref[...] = full.T[0:CLASSES, :]
    weights_ref[0:16, :] = acc[PAY_ROWS : PAY_ROWS + 16, 0:HALF]
    weights_ref[16:32, :] = acc[PAY_ROWS : PAY_ROWS + 16, HALF:LANES]
    rest = acc[0:HALF, :].T
    weights_ref[32:46, :] = rest[CLASSES:HALF, :]
    weights_ref[46:CLASSES, :] = rest[HALF + CLASSES : HALF + CLASSES + 4, :]


def shards(images, ctf, inv_noise, classes, candidates):
    class_block = classes.shape[0]
    part = images.shape[0]
    my_index = lax.axis_index("cls")
    core = lax.axis_index("core").astype(jnp.int32).reshape(1)
    total_rows = ROTATIONS * ROWS
    width = FEATURES + LANES
    shape = jax.ShapeDtypeStruct
    vmem = pl.BlockSpec(memory_space=pltpu.VMEM)
    smem = pl.BlockSpec(memory_space=pltpu.SMEM)
    raw = pl.BlockSpec(memory_space=pltpu.HBM)

    def swap(value, axes):
        return lax.all_to_all(value, axes, split_axis=0, concat_axis=0, tiled=True)

    def cross_core(value):
        return lax.ppermute(value, "core", [(0, 1), (1, 0)])

    def pack(*refs):
        pack_body(class_block, *refs)

    hbm = [
        pltpu.with_memory_space_constraint(value, pltpu.HBM)
        for value in (images, ctf, inv_noise.reshape(1, CYCLES), candidates.T)
    ]
    packed = call(
        pack,
        shape((8, 2, width), BF16),
        *hbm,
        in_specs=[raw] * 4,
        scratch=[
            pltpu.VMEM((part, FEATURES), BF16),
            pltpu.VMEM((part, CYCLES), F32),
            pltpu.VMEM((1, CYCLES), F32),
            pltpu.VMEM((2, part), jnp.int32),
            pltpu.SemaphoreType.DMA((4,)),
        ],
    )
    rows = swap(packed, "cls").reshape(ROWS, width)
    table, energy = call(
        prep_body,
        (shape((ROTATIONS * HALF, BLOCK), BF16), shape((LANES, LANES), F32)),
        classes,
    )
    logits, stats, blocks = call(
        cross_body,
        (
            shape((total_rows, LANES), F32),
            shape((16, 2, LANES), F32),
            shape((total_rows + ROWS, BLOCK), BF16),
        ),
        rows,
        table,
        energy,
        scratch=[pltpu.VMEM((total_rows, LANES), F32)],
    )
    group_stats = swap(stats, ("core", "cls"))
    turned, turned_out, logits_out = call(
        turn_body,
        (
            shape((BLOCK, total_rows), BF16),
            shape((BLOCK + ROWS, total_rows), BF16),
            shape((total_rows, LANES), F32),
        ),
        core,
        blocks,
        logits,
        in_specs=[smem, vmem, vmem],
        micros=10,
    )
    other_turned = cross_core(turned_out)
    other_logits = cross_core(logits_out)
    pay, evidence = call(
        sums_body,
        (shape((GROUPS // 2, PAY_ROWS + 16, LANES), BF16), shape((1, LANES), F32)),
        core,
        group_stats,
        logits,
        other_logits,
        blocks[total_rows:, :LANES],
        other_turned[BLOCK:, :LANES],
        turned,
        other_turned,
        in_specs=[smem] + [vmem] * 7,
        scratch=[pltpu.VMEM((2 * total_rows, LANES), BF16)] * 4,
    )
    parts = swap(pay, ("x", "z"))
    sums, weight_sums = call(
        final_body, (shape((CLASSES, SLICE), F32), shape((CLASSES, CYCLES), F32)), parts
    )
    own = lax.dynamic_slice(evidence.reshape(LANES), (my_index * 4,), (4,))
    return sums.T, weight_sums, own


def solution(mesh):
    fine = Mesh(mesh.devices.reshape(4, 8, 2, 8), ("x", "z", "core", "cls"))
    dom = ("x", "z", "core")
    every = dom + ("cls",)
    in_specs = (P(every, None), P(every, None), P(), P("cls", None), P(every, None))
    out_specs = (P(dom, "cls"), P("cls", None), P(every))
    return jax.shard_map(shards, mesh=fine, in_specs=in_specs, out_specs=out_specs, check_vma=False)
```

```python
import jax
import jax.numpy as jnp
from jax import lax
from jax.experimental import pallas as pl
from jax.experimental.pallas import tpu as pltpu
from jax.sharding import Mesh, PartitionSpec as P

CYCLES = 64
ROTATIONS = 36
BLOCK = 256
FEATURES = ROTATIONS * BLOCK
LANES = 128
HALF = 64
ROWS = 16
MICROS = 5
GROUPS = 64
TARGETS = GROUPS // 4
CLASSES = 50
SLICE = FEATURES // GROUPS
CHUNKS = SLICE // 16
PAY_ROWS = SLICE // 2
NEGATIVE = -1e30
P_LANE = 120
F32 = jnp.float32
BF16 = jnp.bfloat16
HIGH = lax.Precision.HIGHEST


def lanes_of(shape):
    return lax.broadcasted_iota(jnp.int32, shape, len(shape) - 1)


def rows_of(shape):
    return lax.broadcasted_iota(jnp.int32, shape, len(shape) - 2)


def call(body, outs, *args, in_specs=None, scratch=(), micros=0):
    more = {} if in_specs is None else {"in_specs": in_specs}
    if micros:
        more["cost_estimate"] = pl.CostEstimate(
            flops=0, transcendentals=0, bytes_accessed=micros * 3_000_000
        )
    return pl.pallas_call(
        body,
        out_shape=outs,
        scratch_shapes=list(scratch),
        compiler_params=pltpu.CompilerParams(vmem_limit_bytes=48 * 1024 * 1024),
        **more,
    )(*args)


def pack_body(class_block, images_any, ctf_any, noise_any, cands_any, out_ref, images_ref, ctf_ref, noise_ref, cands_ref, sems):
    copies = [
        pltpu.make_async_copy(source, target, sems.at[i])
        for i, (source, target) in enumerate(
            (
                (cands_any, cands_ref),
                (ctf_any, ctf_ref),
                (noise_any, noise_ref),
                (images_any, images_ref),
            )
        )
    ]
    for copy in copies:
        copy.start()
    for copy in copies:
        copy.wait()
    part = images_ref.shape[0]
    ctf = ctf_ref[...]
    noise = noise_ref[...]
    ctf_noise = ctf * noise
    factor = jnp.concatenate([ctf_noise, ctf_noise], axis=1)
    quad = (ctf * ctf * noise).astype(BF16)
    quad = jnp.concatenate([quad, quad], axis=1)
    cands = cands_ref[...]
    first = jnp.broadcast_to(cands[0:1, :], (ROWS, part))
    second = jnp.broadcast_to(cands[1:2, :], (ROWS, part))
    row = rows_of((ROWS, part))
    low = (row // 2) * class_block
    hit = ((first >= low) & (first < low + class_block)) | (
        (second >= low) & (second < low + class_block)
    )
    hit = hit.astype(F32)
    taken = jnp.zeros((ROWS, 1), F32)
    columns = []
    slot = (rows_of((ROWS, 1)) % 2).astype(F32)
    for p in range(part):
        now = hit[:, p : p + 1]
        columns.append(now * (taken == slot).astype(F32))
        taken = taken + now
    packing = jnp.concatenate(columns, axis=1)
    valid = jnp.sum(packing, axis=1, keepdims=True)
    own = jnp.sum(packing * lanes_of((ROWS, part)).astype(F32), axis=1, keepdims=True)
    base = low[:, 0:1].astype(F32)
    id_a = jnp.sum(packing * first.astype(F32), axis=1, keepdims=True) - base
    id_b = jnp.sum(packing * second.astype(F32), axis=1, keepdims=True) - base
    lane = lanes_of((ROWS, LANES))
    klane = (lane - HALF).astype(F32)
    in_block = (lane >= HALF) & (lane < HALF + class_block)
    flags = (in_block & ((klane == id_a) | (klane == id_b))) | (
        (lane - P_LANE).astype(F32) == own
    )
    flags = flags.astype(F32) * (valid > 0.5).astype(F32)
    packing = packing.astype(BF16)

    def put(value, start, size):
        value = value.astype(BF16)
        for owner in range(ROWS // 2):
            out_ref[owner, :, start : start + size] = value[2 * owner : 2 * owner + 2, :]

    quad_rows = jnp.dot(packing, quad, preferred_element_type=F32)
    put(jnp.where(lane < HALF, quad_rows, flags), FEATURES, LANES)
    wide = jnp.concatenate([factor] * 4, axis=1)
    step = 4 * LANES
    for t in range(FEATURES // step):
        part_w = (images_ref[:, t * step : (t + 1) * step].astype(F32) * wide).astype(BF16)
        put(jnp.dot(packing, part_w, preferred_element_type=F32), t * step, step)


def prep_body(classes_ref, table_ref, energy_ref):
    count = classes_ref.shape[0]
    acc = jnp.zeros((count, LANES), F32)
    for b in range(ROTATIONS):
        block = classes_ref[:, b * BLOCK : (b + 1) * BLOCK]
        table_ref[b * HALF : b * HALF + count, :] = block
        table_ref[b * HALF + count : (b + 1) * HALF, :] = jnp.zeros((HALF - count, BLOCK), BF16)
        wide = block.astype(F32)
        square = wide * wide
        acc = acc + square[:, :LANES] + square[:, LANES:]
    acc = acc + pltpu.roll(acc, HALF, 1)
    energy_ref[...] = jnp.zeros((LANES, LANES), F32)
    energy_ref[0:count, :] = acc
    energy_ref[HALF : HALF + count, :] = acc


def row_facts(meta):
    lane = lanes_of(meta.shape)
    flags = jnp.where((lane >= HALF) & (lane < P_LANE), meta, 0.0)
    flags = (flags + pltpu.roll(flags, HALF, 1)) > 0.5
    marks = jnp.where(lane >= P_LANE, meta, 0.0)
    valid = jnp.sum(marks, axis=1, keepdims=True)
    own = jnp.sum(marks * (lane - P_LANE).astype(F32), axis=1, keepdims=True)
    source = (rows_of(meta.shape) // 2 * 4).astype(F32)
    spot = (lane.astype(F32) == source + own) & (valid > 0.5)
    return flags, spot


def slots_of(live):
    lane = lanes_of(live.shape)
    ids = (lane % HALF).astype(F32)
    low = jnp.min(jnp.where(live, ids, 1000.0), axis=1, keepdims=True)
    high = jnp.max(jnp.where(live, ids, -1.0), axis=1, keepdims=True)
    high = jnp.where(high > low, high, -1.0)
    return ids == low, ids == high, low < 999.0, high > -0.5


def cross_body(rows_ref, table_ref, energy_ref, logits_ref, stats_ref, blocks_ref, acc_ref):
    total_rows = ROTATIONS * ROWS
    for b in range(ROTATIONS):
        blocks_ref[b * ROWS : (b + 1) * ROWS, :] = rows_ref[:, b * BLOCK : (b + 1) * BLOCK]
    for m in range(ROTATIONS // 4):
        g = lax.dot_general(
            blocks_ref[...],
            table_ref[m * BLOCK : (m + 1) * BLOCK, :],
            (((1,), (1,)), ((), ())),
            preferred_element_type=F32,
        )
        for h in range(2):
            tile = g[:, h * LANES : (h + 1) * LANES]
            shift = (2 * m + h) * 2 * ROWS
            if shift == 0:
                acc_ref[...] = tile
            else:
                acc_ref[0 : total_rows - shift, :] += tile[shift:, :]
                acc_ref[total_rows - shift :, :] += tile[:shift, :]
    meta = rows_ref[:, FEATURES : FEATURES + LANES].astype(F32)
    lane = lanes_of((ROWS, LANES))
    live, spot = row_facts(meta)
    quad = jnp.where(lane < HALF, meta, 0.0)
    norm = 0.5 * lax.dot_general(
        quad, energy_ref[...], (((1,), (1,)), ((), ())), precision=HIGH, preferred_element_type=F32
    )
    left = live & (lane < HALF)
    best = jnp.full((ROWS, LANES), NEGATIVE, F32)
    for r in range(ROTATIONS):
        nxt = (r + 1) % ROTATIONS
        mixed = jnp.where(
            lane < HALF,
            acc_ref[r * ROWS : (r + 1) * ROWS, :],
            acc_ref[nxt * ROWS : (nxt + 1) * ROWS, :],
        )
        value = mixed + pltpu.roll(mixed, HALF, 1) - norm
        logits_ref[r * ROWS : (r + 1) * ROWS, :] = value
        best = jnp.maximum(best, jnp.where(left, value, NEGATIVE))
    peak = jnp.max(best, axis=1, keepdims=True)
    total = jnp.zeros((ROWS, LANES), F32)
    for r in range(ROTATIONS):
        value = logits_ref[r * ROWS : (r + 1) * ROWS, :]
        total = total + jnp.where(left, jnp.exp(value - peak), 0.0)
    total = jnp.sum(total, axis=1, keepdims=True)
    peak_row = jnp.max(jnp.where(spot, peak, NEGATIVE), axis=0, keepdims=True)
    total_row = jnp.sum(jnp.where(spot, total, 0.0), axis=0, keepdims=True)
    for d in range(stats_ref.shape[0]):
        stats_ref[d, 0:1, :] = peak_row
        stats_ref[d, 1:2, :] = total_row


def bundle_body(rows_ref, logits_ref, out_ref):
    total_rows = ROTATIONS * ROWS
    for b in range(ROTATIONS):
        out_ref[b * ROWS : (b + 1) * ROWS, :] = rows_ref[:, b * BLOCK : (b + 1) * BLOCK]
    raw = rows_ref[:, FEATURES : FEATURES + LANES]
    live, _ = row_facts(raw.astype(F32))
    lane = lanes_of((ROWS, LANES))
    first, second, _, _ = slots_of(live & (lane < HALF))
    first = first & (lane < HALF)
    second = second & (lane < HALF)
    compact = jnp.zeros((ROWS, LANES), F32)
    for r in range(ROTATIONS):
        value = logits_ref[r * ROWS : (r + 1) * ROWS, :]
        one = jnp.sum(jnp.where(first, value, 0.0), axis=1, keepdims=True)
        two = jnp.sum(jnp.where(second, value, 0.0), axis=1, keepdims=True)
        compact = jnp.where(lane == r, one, jnp.where(lane == ROTATIONS + r, two, compact))
    high = compact.astype(BF16)
    rest = compact - high.astype(F32)
    middle = rest.astype(BF16)
    rest = rest - middle.astype(F32)
    out_ref[total_rows : total_rows + ROWS, 0:LANES] = raw
    out_ref[total_rows : total_rows + ROWS, LANES:] = high
    out_ref[total_rows + ROWS :, 0:LANES] = middle
    out_ref[total_rows + ROWS :, LANES:] = rest.astype(BF16)


def turn_body(place_ref, one_ref, two_ref, out_ref):
    total_rows = ROTATIONS * ROWS
    second = place_ref[0] == 1
    for g, blocks_ref in enumerate((one_ref, two_ref)):
        value = blocks_ref[0:total_rows, :].astype(F32)
        rolled = pltpu.roll(value, BLOCK - SLICE, 1)
        after = jnp.concatenate([rolled[ROWS:, :], rolled[:ROWS, :]], axis=0)
        moved = jnp.where(lanes_of(value.shape) < BLOCK - SLICE, rolled, after)
        value = jnp.where(second, moved, value)
        out_ref[:, g * total_rows : (g + 1) * total_rows] = value.T.astype(BF16)


def evidence_body(place_ref, stats_ref, out_ref):
    core, near = place_ref[0], place_ref[1]
    for g in range(4):
        at_core = core if g % 2 == 0 else 1 - core
        at_near = near if g < 2 else 1 - near
        stats = stats_ref[pl.ds((at_near * 2 + at_core) * 8, 8), :, :]
        peaks = stats[:, 0, :]
        totals = stats[:, 1, :]
        highest = jnp.max(peaks, axis=0, keepdims=True)
        total = jnp.sum(totals * jnp.exp(peaks - highest), axis=0, keepdims=True)
        out_ref[g : g + 1, :] = highest + jnp.log(total)


def sums_body(
    place_ref, evid_ref, tail_a, tail_b, tail_c, tail_d, turned_a, turned_b, pay_ref, *tables
):
    total_rows = ROTATIONS * ROWS
    near = place_ref[1]
    lane = lanes_of((ROWS, LANES))
    on_left = lane < HALF
    weights, quads = [], []
    for g, tail_ref in enumerate((tail_a, tail_b, tail_c, tail_d)):
        table_ref = tables[g]
        evidence = evid_ref[g : g + 1, :]
        meta = tail_ref[0:ROWS, 0:LANES].astype(F32)
        logits = tail_ref[0:ROWS, LANES:].astype(F32) + (
            tail_ref[ROWS:, 0:LANES].astype(F32) + tail_ref[ROWS:, LANES:].astype(F32)
        )
        live, spot = row_facts(meta)
        first, second, has_first, has_second = slots_of(live)
        row_evidence = jnp.sum(jnp.where(spot, evidence, 0.0), axis=1, keepdims=True)
        known = ((lane < ROTATIONS) & has_first) | (
            (lane >= ROTATIONS) & (lane < 2 * ROTATIONS) & has_second
        )
        post = jnp.where(known, jnp.exp(logits - row_evidence), 0.0).astype(BF16).astype(F32)
        first = first.astype(F32)
        second = second.astype(F32)
        total_one = jnp.sum(jnp.where(lane < ROTATIONS, post, 0.0), axis=1, keepdims=True)
        total_two = jnp.sum(jnp.where(lane < ROTATIONS, 0.0, post), axis=1, keepdims=True)
        weights.append(total_one * first + total_two * second)
        half = ROTATIONS // 2

        def spread(r):
            return (
                post[:, r : r + 1] * first + post[:, ROTATIONS + r : ROTATIONS + r + 1] * second
            )

        for r in range(half):
            here, there = spread(r), spread(r + half)
            for row, value in (
                (r, jnp.where(on_left, here, there)),
                (r + half, jnp.where(on_left, there, here)),
            ):
                value = value.astype(BF16)
                table_ref[row * ROWS : (row + 1) * ROWS, :] = value
                table_ref[total_rows + row * ROWS : total_rows + (row + 1) * ROWS, :] = value
        quad = jnp.where(on_left, meta, 0.0)
        quads.append(quad + pltpu.roll(quad, HALF, 1))
    weight = jnp.concatenate(weights, axis=0)
    quad = jnp.concatenate(quads, axis=0)
    by_class = jnp.dot(weight.T, quad, precision=HIGH, preferred_element_type=F32)
    by_shell = jnp.dot(quad.T, weight, precision=HIGH, preferred_element_type=F32)[0:HALF, :]
    tail = jnp.where(on_left, by_class[0:16, :], by_class[16:32, :]).astype(BF16)
    wide = lanes_of((HALF, LANES))
    spare = jnp.where(
        (wide >= CLASSES) & (wide < HALF),
        pltpu.roll(by_shell, CLASSES - 32, 1),
        jnp.where(wide >= HALF + CLASSES, pltpu.roll(by_shell, CLASSES - 46, 1), 0.0),
    ).astype(BF16)
    for d in range(TARGETS):
        pay_ref[d, 0:HALF, :] = spare
        pay_ref[d, PAY_ROWS : PAY_ROWS + 16, :] = tail
    base = (ROTATIONS - CHUNKS * near) * ROWS
    for b in range(CHUNKS):
        kept = [i for i in range(16) if (16 * b + i) // CHUNKS % 2 == 0]
        bands = []
        for i in kept:
            if bands and bands[-1][1] == i:
                bands[-1][1] = i + 1
            else:
                bands.append([i, i + 1])
        start = pl.multiple_of(base - b * ROWS, ROWS)
        out = jnp.zeros((16 * len(kept), LANES), F32)
        for g, turned_ref in enumerate((turned_a, turned_b)):
            left = jnp.concatenate([turned_ref[16 * lo : 16 * hi, :] for lo, hi in bands], axis=0)
            right = jnp.concatenate(
                [
                    tables[2 * g][pl.ds(start, total_rows), :],
                    tables[2 * g + 1][pl.ds(start, total_rows), :],
                ],
                axis=0,
            )
            out = out + jnp.dot(left, right, preferred_element_type=F32)
        out = out.astype(BF16)
        for e in range(2):
            for n, i in enumerate(kept):
                q = b * 16 + i
                d, j = e * 8 + q // CHUNKS // 2, q % CHUNKS
                piece = out[n * 16 : (n + 1) * 16, e * HALF : e * HALF + CLASSES]
                if j < CHUNKS - 1:
                    at = j // 2 * 16
                    lo = j % 2 * HALF
                    pay_ref[d, at : at + 16, lo : lo + CLASSES] = piece
                else:
                    pay_ref[d, PAY_ROWS - 8 : PAY_ROWS, 0:CLASSES] = piece[0:8, :]
                    pay_ref[d, PAY_ROWS - 8 : PAY_ROWS, HALF : HALF + CLASSES] = piece[8:16, :]


def final_body(parts_ref, sums_ref, weights_ref):
    acc = parts_ref[0, :, :].astype(F32)
    for g in range(1, TARGETS):
        acc = acc + parts_ref[g, :, :].astype(F32)
    pieces = []
    for j in range(CHUNKS - 1):
        lo = j % 2 * HALF
        pieces.append(acc[j // 2 * 16 : j // 2 * 16 + 16, lo : lo + HALF])
    pieces.append(acc[PAY_ROWS - 8 : PAY_ROWS, 0:HALF])
    pieces.append(acc[PAY_ROWS - 8 : PAY_ROWS, HALF:LANES])
    full = jnp.concatenate(pieces, axis=0)
    sums_ref[...] = full.T[0:CLASSES, :]
    weights_ref[0:16, :] = acc[PAY_ROWS : PAY_ROWS + 16, 0:HALF]
    weights_ref[16:32, :] = acc[PAY_ROWS : PAY_ROWS + 16, HALF:LANES]
    rest = acc[0:HALF, :].T
    weights_ref[32:46, :] = rest[CLASSES:HALF, :]
    weights_ref[46:CLASSES, :] = rest[HALF + CLASSES : HALF + CLASSES + 4, :]


def shards(images, ctf, inv_noise, classes, candidates):
    class_block = classes.shape[0]
    part = images.shape[0]
    my_index = lax.axis_index("cls")
    place = jnp.stack([lax.axis_index("core"), lax.axis_index("xl")]).astype(jnp.int32)
    total_rows = ROTATIONS * ROWS
    width = FEATURES + LANES
    shape = jax.ShapeDtypeStruct
    vmem = pl.BlockSpec(memory_space=pltpu.VMEM)
    smem = pl.BlockSpec(memory_space=pltpu.SMEM)
    raw = pl.BlockSpec(memory_space=pltpu.HBM)

    def swap(value, axes):
        return lax.all_to_all(value, axes, split_axis=0, concat_axis=0, tiled=True)

    def flip(value, axis):
        return lax.ppermute(value, axis, [(0, 1), (1, 0)])

    def pack(*refs):
        pack_body(class_block, *refs)

    hbm = [
        pltpu.with_memory_space_constraint(value, pltpu.HBM)
        for value in (images, ctf, inv_noise.reshape(1, CYCLES), candidates.T)
    ]
    packed = call(
        pack,
        shape((8, 2, width), BF16),
        *hbm,
        in_specs=[raw] * 4,
        scratch=[
            pltpu.VMEM((part, FEATURES), BF16),
            pltpu.VMEM((part, CYCLES), F32),
            pltpu.VMEM((1, CYCLES), F32),
            pltpu.VMEM((2, part), jnp.int32),
            pltpu.SemaphoreType.DMA((4,)),
        ],
    )
    rows = swap(packed, "cls").reshape(ROWS, width)
    table, energy = call(
        prep_body,
        (shape((ROTATIONS * HALF, BLOCK), BF16), shape((LANES, LANES), F32)),
        classes,
    )
    logits, stats = call(
        cross_body,
        (shape((total_rows, LANES), F32), shape((32, 2, LANES), F32)),
        rows,
        table,
        energy,
        scratch=[pltpu.VMEM((total_rows, BLOCK), BF16), pltpu.VMEM((total_rows, LANES), F32)],
    )
    group_stats = swap(stats, ("xl", "core", "cls"))
    mine = call(bundle_body, shape((total_rows + 2 * ROWS, BLOCK), BF16), rows, logits)
    beside = flip(mine, "xl")
    sibling = flip(mine, "core")
    across = lax.ppermute(mine, ("xl", "core"), [(0, 3), (1, 2), (2, 1), (3, 0)])

    def turn(one, two):
        return call(
            turn_body,
            shape((BLOCK, 2 * total_rows), BF16),
            place,
            one,
            two,
            in_specs=[smem, vmem, vmem],
        )

    evidence = call(
        evidence_body,
        shape((4, LANES), F32),
        place,
        group_stats,
        in_specs=[smem, vmem],
        micros=MICROS,
    )
    pay = call(
        sums_body,
        shape((TARGETS, PAY_ROWS + 16, LANES), BF16),
        place,
        evidence,
        *(value[total_rows:, :] for value in (mine, sibling, beside, across)),
        turn(mine, sibling),
        turn(beside, across),
        in_specs=[smem] + [vmem] * 7,
        scratch=[pltpu.VMEM((2 * total_rows, LANES), BF16)] * 4,
    )
    parts = swap(pay, ("xh", "z"))
    sums, weight_sums = call(
        final_body, (shape((CLASSES, SLICE), F32), shape((CLASSES, CYCLES), F32)), parts
    )
    own = lax.dynamic_slice(evidence, (0, my_index * 4), (1, 4)).reshape(4)
    return sums.T, weight_sums, own


def solution(mesh):
    dom = ("xh", "xl", "z", "core")
    fine = Mesh(mesh.devices.reshape(2, 2, 8, 2, 8), dom + ("cls",))
    every = dom + ("cls",)
    in_specs = (P(every, None), P(every, None), P(), P("cls", None), P(every, None))
    out_specs = (P(dom, "cls"), P("cls", None), P(every))
    return jax.shard_map(shards, mesh=fine, in_specs=in_specs, out_specs=out_specs, check_vma=False)
```

```python
import jax
import jax.numpy as jnp
from jax import lax
from jax.experimental import pallas as pl
from jax.experimental.pallas import tpu as pltpu
from jax.sharding import Mesh, PartitionSpec as P

CYCLES = 64
ROTATIONS = 36
BLOCK = 256
FEATURES = ROTATIONS * BLOCK
LANES = 128
HALF = 64
ROWS = 16
GROUPS = 64
TARGETS = GROUPS // 4
DEPTH = 640
CLASSES = 50
SLICE = FEATURES // GROUPS
CHUNKS = SLICE // 16
PAY_ROWS = SLICE // 2
NEGATIVE = -1e30
P_LANE = 120
F32 = jnp.float32
BF16 = jnp.bfloat16
HIGH = lax.Precision.HIGHEST


def lanes_of(shape):
    return lax.broadcasted_iota(jnp.int32, shape, len(shape) - 1)


def rows_of(shape):
    return lax.broadcasted_iota(jnp.int32, shape, len(shape) - 2)


def call(body, outs, *args, in_specs=None, out_specs=None, scratch=()):
    more = {} if in_specs is None else {"in_specs": in_specs}
    if out_specs is not None:
        more["out_specs"] = out_specs
    return pl.pallas_call(
        body,
        out_shape=outs,
        scratch_shapes=list(scratch),
        compiler_params=pltpu.CompilerParams(vmem_limit_bytes=48 * 1024 * 1024),
        **more,
    )(*args)


def pack_body(class_block, images_any, ctf_any, noise_any, cands_any, out_ref, images_ref, ctf_ref, noise_ref, cands_ref, sems):
    copies = [
        pltpu.make_async_copy(source, target, sems.at[i])
        for i, (source, target) in enumerate(
            (
                (cands_any, cands_ref),
                (ctf_any, ctf_ref),
                (noise_any, noise_ref),
                (images_any, images_ref),
            )
        )
    ]
    for copy in copies:
        copy.start()
    for copy in copies:
        copy.wait()
    part = images_ref.shape[0]
    ctf = ctf_ref[...]
    noise = noise_ref[...]
    ctf_noise = ctf * noise
    factor = jnp.concatenate([ctf_noise, ctf_noise], axis=1)
    quad = (ctf * ctf * noise).astype(BF16)
    quad = jnp.concatenate([quad, quad], axis=1)
    cands = cands_ref[...]
    first = jnp.broadcast_to(cands[0:1, :], (ROWS, part))
    second = jnp.broadcast_to(cands[1:2, :], (ROWS, part))
    row = rows_of((ROWS, part))
    low = (row // 2) * class_block
    hit = ((first >= low) & (first < low + class_block)) | (
        (second >= low) & (second < low + class_block)
    )
    hit = hit.astype(F32)
    taken = jnp.zeros((ROWS, 1), F32)
    columns = []
    slot = (rows_of((ROWS, 1)) % 2).astype(F32)
    for p in range(part):
        now = hit[:, p : p + 1]
        columns.append(now * (taken == slot).astype(F32))
        taken = taken + now
    packing = jnp.concatenate(columns, axis=1)
    valid = jnp.sum(packing, axis=1, keepdims=True)
    own = jnp.sum(packing * lanes_of((ROWS, part)).astype(F32), axis=1, keepdims=True)
    base = low[:, 0:1].astype(F32)
    id_a = jnp.sum(packing * first.astype(F32), axis=1, keepdims=True) - base
    id_b = jnp.sum(packing * second.astype(F32), axis=1, keepdims=True) - base
    lane = lanes_of((ROWS, LANES))
    klane = (lane - HALF).astype(F32)
    in_block = (lane >= HALF) & (lane < HALF + class_block)
    flags = (in_block & ((klane == id_a) | (klane == id_b))) | (
        (lane - P_LANE).astype(F32) == own
    )
    flags = flags.astype(F32) * (valid > 0.5).astype(F32)
    packing = packing.astype(BF16)

    def put(value, start, size):
        value = value.astype(BF16)
        for owner in range(ROWS // 2):
            out_ref[owner, :, start : start + size] = value[2 * owner : 2 * owner + 2, :]

    quad_rows = jnp.dot(packing, quad, preferred_element_type=F32)
    put(jnp.where(lane < HALF, quad_rows, flags), FEATURES, LANES)
    wide = jnp.concatenate([factor] * 4, axis=1)
    step = 4 * LANES
    for t in range(FEATURES // step):
        part_w = (images_ref[:, t * step : (t + 1) * step].astype(F32) * wide).astype(BF16)
        put(jnp.dot(packing, part_w, preferred_element_type=F32), t * step, step)


def prep_body(classes_ref, table_ref, energy_ref):
    count = classes_ref.shape[0]
    acc = jnp.zeros((count, LANES), F32)
    for b in range(ROTATIONS):
        block = classes_ref[:, b * BLOCK : (b + 1) * BLOCK]
        table_ref[b * HALF : b * HALF + count, :] = block
        table_ref[b * HALF + count : (b + 1) * HALF, :] = jnp.zeros((HALF - count, BLOCK), BF16)
        wide = block.astype(F32)
        square = wide * wide
        acc = acc + square[:, :LANES] + square[:, LANES:]
    acc = acc + pltpu.roll(acc, HALF, 1)
    energy_ref[...] = jnp.zeros((LANES, LANES), F32)
    energy_ref[0:count, :] = acc
    energy_ref[HALF : HALF + count, :] = acc


def row_facts(meta):
    lane = lanes_of(meta.shape)
    flags = jnp.where((lane >= HALF) & (lane < P_LANE), meta, 0.0)
    flags = (flags + pltpu.roll(flags, HALF, 1)) > 0.5
    marks = jnp.where(lane >= P_LANE, meta, 0.0)
    valid = jnp.sum(marks, axis=1, keepdims=True)
    own = jnp.sum(marks * (lane - P_LANE).astype(F32), axis=1, keepdims=True)
    source = (rows_of(meta.shape) // 2 * 4).astype(F32)
    spot = (lane.astype(F32) == source + own) & (valid > 0.5)
    return flags, spot


def slots_of(live):
    lane = lanes_of(live.shape)
    ids = (lane % HALF).astype(F32)
    low = jnp.min(jnp.where(live, ids, 1000.0), axis=1, keepdims=True)
    high = jnp.max(jnp.where(live, ids, -1.0), axis=1, keepdims=True)
    high = jnp.where(high > low, high, -1.0)
    return ids == low, ids == high, low < 999.0, high > -0.5


def cross_body(rows_ref, table_ref, energy_ref, logits_ref, stats_ref, blocks_ref, acc_ref):
    total_rows = ROTATIONS * ROWS
    for b in range(ROTATIONS):
        blocks_ref[b * ROWS : (b + 1) * ROWS, :] = rows_ref[:, b * BLOCK : (b + 1) * BLOCK]
    for m in range(ROTATIONS // 4):
        g = lax.dot_general(
            blocks_ref[...],
            table_ref[m * BLOCK : (m + 1) * BLOCK, :],
            (((1,), (1,)), ((), ())),
            preferred_element_type=F32,
        )
        for h in range(2):
            tile = g[:, h * LANES : (h + 1) * LANES]
            shift = (2 * m + h) * 2 * ROWS
            if shift == 0:
                acc_ref[...] = tile
            else:
                acc_ref[0 : total_rows - shift, :] += tile[shift:, :]
                acc_ref[total_rows - shift :, :] += tile[:shift, :]
    meta = rows_ref[:, FEATURES : FEATURES + LANES].astype(F32)
    lane = lanes_of((ROWS, LANES))
    live, spot = row_facts(meta)
    quad = jnp.where(lane < HALF, meta, 0.0)
    norm = 0.5 * lax.dot_general(
        quad, energy_ref[...], (((1,), (1,)), ((), ())), precision=HIGH, preferred_element_type=F32
    )
    left = live & (lane < HALF)
    best = jnp.full((ROWS, LANES), NEGATIVE, F32)
    for r in range(ROTATIONS):
        nxt = (r + 1) % ROTATIONS
        mixed = jnp.where(
            lane < HALF,
            acc_ref[r * ROWS : (r + 1) * ROWS, :],
            acc_ref[nxt * ROWS : (nxt + 1) * ROWS, :],
        )
        value = mixed + pltpu.roll(mixed, HALF, 1) - norm
        logits_ref[r * ROWS : (r + 1) * ROWS, :] = value
        best = jnp.maximum(best, jnp.where(left, value, NEGATIVE))
    peak = jnp.max(best, axis=1, keepdims=True)
    total = jnp.zeros((ROWS, LANES), F32)
    for r in range(ROTATIONS):
        value = logits_ref[r * ROWS : (r + 1) * ROWS, :]
        total = total + jnp.where(left, jnp.exp(value - peak), 0.0)
    total = jnp.sum(total, axis=1, keepdims=True)
    peak_row = jnp.max(jnp.where(spot, peak, NEGATIVE), axis=0, keepdims=True)
    total_row = jnp.sum(jnp.where(spot, total, 0.0), axis=0, keepdims=True)
    for d in range(stats_ref.shape[0]):
        stats_ref[d, 0:1, :] = peak_row
        stats_ref[d, 1:2, :] = total_row


def bundle_body(rows_ref, logits_ref, out_ref):
    total_rows = ROTATIONS * ROWS
    for b in range(ROTATIONS):
        out_ref[b * ROWS : (b + 1) * ROWS, :] = rows_ref[:, b * BLOCK : (b + 1) * BLOCK]
    raw = rows_ref[:, FEATURES : FEATURES + LANES]
    live, _ = row_facts(raw.astype(F32))
    lane = lanes_of((ROWS, LANES))
    first, second, _, _ = slots_of(live & (lane < HALF))
    first = first & (lane < HALF)
    second = second & (lane < HALF)
    compact = jnp.zeros((ROWS, LANES), F32)
    for r in range(ROTATIONS):
        value = logits_ref[r * ROWS : (r + 1) * ROWS, :]
        one = jnp.sum(jnp.where(first, value, 0.0), axis=1, keepdims=True)
        two = jnp.sum(jnp.where(second, value, 0.0), axis=1, keepdims=True)
        compact = jnp.where(lane == r, one, jnp.where(lane == ROTATIONS + r, two, compact))
    high = compact.astype(BF16)
    rest = compact - high.astype(F32)
    middle = rest.astype(BF16)
    rest = rest - middle.astype(F32)
    out_ref[total_rows : total_rows + ROWS, 0:LANES] = raw
    out_ref[total_rows : total_rows + ROWS, LANES:] = high
    out_ref[total_rows + ROWS :, 0:LANES] = middle
    out_ref[total_rows + ROWS :, LANES:] = rest.astype(BF16)


def turn_body(place_ref, blocks_ref, turned_ref, facts_ref):
    total_rows = ROTATIONS * ROWS
    second = place_ref[0] == 1
    value = blocks_ref[0:total_rows, :].astype(F32)
    rolled = pltpu.roll(value, BLOCK - SLICE, 1)
    after = jnp.concatenate([rolled[ROWS:, :], rolled[:ROWS, :]], axis=0)
    moved = jnp.where(lanes_of(value.shape) < BLOCK - SLICE, rolled, after)
    value = jnp.where(second, moved, value)
    turned_ref[:, 0:total_rows] = value.T.astype(BF16)
    turned_ref[:, total_rows:] = jnp.zeros((BLOCK, DEPTH - total_rows), BF16)
    lane = lanes_of((ROWS, LANES))
    meta = blocks_ref[total_rows : total_rows + ROWS, 0:LANES].astype(F32)
    logits = blocks_ref[total_rows : total_rows + ROWS, LANES:].astype(F32) + (
        blocks_ref[total_rows + ROWS :, 0:LANES].astype(F32)
        + blocks_ref[total_rows + ROWS :, LANES:].astype(F32)
    )
    live, spot = row_facts(meta)
    first, second, has_first, has_second = slots_of(live)
    known = ((lane < ROTATIONS) & has_first) | (
        (lane >= ROTATIONS) & (lane < 2 * ROTATIONS) & has_second
    )
    quad = jnp.where(lane < HALF, meta, 0.0)
    quad = quad + pltpu.roll(quad, HALF, 1)
    for i, fact in enumerate((first, second, spot, known, logits, quad)):
        facts_ref[i, :, :] = fact.astype(F32)


def sums_body(
    place_ref,
    stats_ref,
    facts_a,
    facts_b,
    facts_c,
    facts_d,
    turned_a,
    turned_b,
    turned_c,
    turned_d,
    out_any,
    evid_ref,
    pay_ref,
    table_a,
    table_b,
    table_c,
    table_d,
    sems,
):
    total_rows = ROTATIONS * ROWS
    core, near = place_ref[0], place_ref[1]
    all_facts = (facts_a, facts_b, facts_c, facts_d)
    all_turned = (turned_a, turned_b, turned_c, turned_d)
    tables = (table_a, table_b, table_c, table_d)
    lane = lanes_of((ROWS, LANES))
    on_left = lane < HALF
    weights, quads = [], []
    for g, (facts_ref, table_ref) in enumerate(zip(all_facts, tables)):
        at_core = core if g % 2 == 0 else 1 - core
        at_near = near if g < 2 else 1 - near
        stats = stats_ref[pl.ds((at_near * 2 + at_core) * 8, 8), :, :]
        peaks = stats[:, 0, :]
        totals = stats[:, 1, :]
        highest = jnp.max(peaks, axis=0, keepdims=True)
        total = jnp.sum(totals * jnp.exp(peaks - highest), axis=0, keepdims=True)
        evidence = highest + jnp.log(total)
        if g == 0:
            evid_ref[...] = evidence
        first, second = facts_ref[0, :, :], facts_ref[1, :, :]
        row_evidence = jnp.sum(
            jnp.where(facts_ref[2, :, :] > 0.5, evidence, 0.0), axis=1, keepdims=True
        )
        post = jnp.where(
            facts_ref[3, :, :] > 0.5, jnp.exp(facts_ref[4, :, :] - row_evidence), 0.0
        )
        post = post.astype(BF16).astype(F32)
        total_one = jnp.sum(jnp.where(lane < ROTATIONS, post, 0.0), axis=1, keepdims=True)
        total_two = jnp.sum(jnp.where(lane < ROTATIONS, 0.0, post), axis=1, keepdims=True)
        weights.append(total_one * first + total_two * second)
        quads.append(facts_ref[5, :, :])
        half = ROTATIONS // 2

        def spread(r):
            return (
                post[:, r : r + 1] * first + post[:, ROTATIONS + r : ROTATIONS + r + 1] * second
            )

        for r in range(half):
            here, there = spread(r), spread(r + half)
            for row, value in (
                (r, jnp.where(on_left, here, there)),
                (r + half, jnp.where(on_left, there, here)),
            ):
                value = value.astype(BF16)
                for turn in range(3):
                    at = (turn * ROTATIONS + row) * ROWS
                    if at + ROWS <= total_rows + DEPTH:
                        table_ref[at : at + ROWS, :] = value
    weight = jnp.concatenate(weights, axis=0)
    quad = jnp.concatenate(quads, axis=0)
    by_class = jnp.dot(weight.T, quad, precision=HIGH, preferred_element_type=F32)
    by_shell = jnp.dot(quad.T, weight, precision=HIGH, preferred_element_type=F32)[0:HALF, :]
    tail = jnp.where(on_left, by_class[0:16, :], by_class[16:32, :]).astype(BF16)
    wide = lanes_of((HALF, LANES))
    spare = jnp.where(
        (wide >= CLASSES) & (wide < HALF),
        pltpu.roll(by_shell, CLASSES - 32, 1),
        jnp.where(wide >= HALF + CLASSES, pltpu.roll(by_shell, CLASSES - 46, 1), 0.0),
    ).astype(BF16)
    for d in range(TARGETS):
        pay_ref[d, 0:HALF, :] = spare
        pay_ref[d, PAY_ROWS : PAY_ROWS + 16, :] = tail
    copies = [
        pltpu.make_async_copy(pay_ref.at[d], out_any.at[d], sems.at[d]) for d in range(TARGETS)
    ]
    started = 0
    base = (ROTATIONS - CHUNKS * near) * ROWS
    for b in range(CHUNKS):
        kept = [i for i in range(16) if (16 * b + i) // CHUNKS % 2 == 0]
        bands = []
        for i in kept:
            if bands and bands[-1][1] == i:
                bands[-1][1] = i + 1
            else:
                bands.append([i, i + 1])
        start = pl.multiple_of(base - b * ROWS, ROWS)
        left = jnp.concatenate(
            [
                jnp.concatenate([ref[16 * lo : 16 * hi, :] for lo, hi in bands], axis=0)
                for ref in all_turned
            ],
            axis=1,
        )
        right = jnp.concatenate([ref[pl.ds(start, DEPTH), :] for ref in tables], axis=0)
        out = jnp.dot(left, right, preferred_element_type=F32).astype(BF16)
        for e in range(2):
            for n, i in enumerate(kept):
                q = b * 16 + i
                d, j = e * 8 + q // CHUNKS // 2, q % CHUNKS
                piece = out[n * 16 : (n + 1) * 16, e * HALF : e * HALF + CLASSES]
                if j < CHUNKS - 1:
                    at = j // 2 * 16
                    lo = j % 2 * HALF
                    pay_ref[d, at : at + 16, lo : lo + CLASSES] = piece
                else:
                    pay_ref[d, PAY_ROWS - 8 : PAY_ROWS, 0:CLASSES] = piece[0:8, :]
                    pay_ref[d, PAY_ROWS - 8 : PAY_ROWS, HALF : HALF + CLASSES] = piece[8:16, :]
        finished = (16 * b + 16 + CHUNKS) // (2 * CHUNKS)
        for z in range(started, finished):
            copies[z].start()
            copies[8 + z].start()
        started = finished
    for copy in copies:
        copy.wait()


def final_body(parts_ref, sums_ref, weights_ref):
    acc = parts_ref[0, :, :].astype(F32)
    for g in range(1, TARGETS):
        acc = acc + parts_ref[g, :, :].astype(F32)
    pieces = []
    for j in range(CHUNKS - 1):
        lo = j % 2 * HALF
        pieces.append(acc[j // 2 * 16 : j // 2 * 16 + 16, lo : lo + HALF])
    pieces.append(acc[PAY_ROWS - 8 : PAY_ROWS, 0:HALF])
    pieces.append(acc[PAY_ROWS - 8 : PAY_ROWS, HALF:LANES])
    full = jnp.concatenate(pieces, axis=0)
    sums_ref[...] = full.T[0:CLASSES, :]
    weights_ref[0:16, :] = acc[PAY_ROWS : PAY_ROWS + 16, 0:HALF]
    weights_ref[16:32, :] = acc[PAY_ROWS : PAY_ROWS + 16, HALF:LANES]
    rest = acc[0:HALF, :].T
    weights_ref[32:46, :] = rest[CLASSES:HALF, :]
    weights_ref[46:CLASSES, :] = rest[HALF + CLASSES : HALF + CLASSES + 4, :]


def shards(images, ctf, inv_noise, classes, candidates):
    class_block = classes.shape[0]
    part = images.shape[0]
    my_index = lax.axis_index("cls")
    place = jnp.stack([lax.axis_index("core"), lax.axis_index("xl")]).astype(jnp.int32)
    total_rows = ROTATIONS * ROWS
    width = FEATURES + LANES
    shape = jax.ShapeDtypeStruct
    vmem = pl.BlockSpec(memory_space=pltpu.VMEM)
    smem = pl.BlockSpec(memory_space=pltpu.SMEM)
    raw = pl.BlockSpec(memory_space=pltpu.HBM)

    def swap(value, axes):
        return lax.all_to_all(value, axes, split_axis=0, concat_axis=0, tiled=True)

    def flip(value, axis):
        return lax.ppermute(value, axis, [(0, 1), (1, 0)])

    def pack(*refs):
        pack_body(class_block, *refs)

    hbm = [
        pltpu.with_memory_space_constraint(value, pltpu.HBM)
        for value in (images, ctf, inv_noise.reshape(1, CYCLES), candidates.T)
    ]
    packed = call(
        pack,
        shape((8, 2, width), BF16),
        *hbm,
        in_specs=[raw] * 4,
        scratch=[
            pltpu.VMEM((part, FEATURES), BF16),
            pltpu.VMEM((part, CYCLES), F32),
            pltpu.VMEM((1, CYCLES), F32),
            pltpu.VMEM((2, part), jnp.int32),
            pltpu.SemaphoreType.DMA((4,)),
        ],
    )
    rows = swap(packed, "cls").reshape(ROWS, width)
    table, energy = call(
        prep_body,
        (shape((ROTATIONS * HALF, BLOCK), BF16), shape((LANES, LANES), F32)),
        classes,
    )
    logits, stats = call(
        cross_body,
        (shape((total_rows, LANES), F32), shape((32, 2, LANES), F32)),
        rows,
        table,
        energy,
        scratch=[pltpu.VMEM((total_rows, BLOCK), BF16), pltpu.VMEM((total_rows, LANES), F32)],
    )
    group_stats = swap(stats, ("xl", "core", "cls"))
    mine = call(bundle_body, shape((total_rows + 2 * ROWS, BLOCK), BF16), rows, logits)

    def turn(value):
        return call(
            turn_body,
            (shape((BLOCK, DEPTH), BF16), shape((6, ROWS, LANES), F32)),
            place,
            value,
            in_specs=[smem, vmem],
        )

    def trade(value):
        beside = flip(value, "xl")
        sibling = flip(value, "core")
        across = flip(beside, "core")
        return turn(value), turn(sibling), turn(beside), turn(across)

    def alone(value):
        return (turn(value),) * 4

    turned, facts = zip(*lax.cond(place[0] < 2, trade, alone, mine))
    pay, evidence = call(
        sums_body,
        (shape((TARGETS, PAY_ROWS + 16, LANES), BF16), shape((1, LANES), F32)),
        place,
        group_stats,
        *facts,
        *turned,
        in_specs=[smem] + [vmem] * 9,
        out_specs=(raw, vmem),
        scratch=[pltpu.VMEM((TARGETS, PAY_ROWS + 16, LANES), BF16)]
        + [pltpu.VMEM((total_rows + DEPTH, LANES), BF16)] * 4
        + [pltpu.SemaphoreType.DMA((TARGETS,))],
    )
    parts = swap(pay, ("xh", "z"))
    sums, weight_sums = call(
        final_body, (shape((CLASSES, SLICE), F32), shape((CLASSES, CYCLES), F32)), parts
    )
    own = lax.dynamic_slice(evidence, (0, my_index * 4), (1, 4)).reshape(4)
    return sums.T, weight_sums, own


def solution(mesh):
    dom = ("xh", "xl", "z", "core")
    fine = Mesh(mesh.devices.reshape(2, 2, 8, 2, 8), dom + ("cls",))
    every = dom + ("cls",)
    in_specs = (P(every, None), P(every, None), P(), P("cls", None), P(every, None))
    out_specs = (P(dom, "cls"), P("cls", None), P(every))
    return jax.shard_map(shards, mesh=fine, in_specs=in_specs, out_specs=out_specs, check_vma=False)
```

```python
import jax
import jax.numpy as jnp
from jax import lax
from jax.experimental import pallas as pl
from jax.experimental.pallas import tpu as pltpu
from jax.sharding import Mesh, PartitionSpec as P

CYCLES = 64
ROTATIONS = 36
BLOCK = 256
FEATURES = ROTATIONS * BLOCK
LANES = 128
HALF = 64
ROWS = 16
GROUPS = 64
TARGETS = GROUPS // 4
DEPTH = 2 * ROTATIONS * ROWS
CLASSES = 50
SLICE = FEATURES // GROUPS
CHUNKS = SLICE // 16
PAY_ROWS = SLICE // 2
NEGATIVE = -1e30
P_LANE = 120
F32 = jnp.float32
BF16 = jnp.bfloat16
HIGH = lax.Precision.HIGHEST


def lanes_of(shape):
    return lax.broadcasted_iota(jnp.int32, shape, len(shape) - 1)


def rows_of(shape):
    return lax.broadcasted_iota(jnp.int32, shape, len(shape) - 2)


def call(body, outs, *args, in_specs=None, out_specs=None, scratch=()):
    more = {} if in_specs is None else {"in_specs": in_specs}
    if out_specs is not None:
        more["out_specs"] = out_specs
    return pl.pallas_call(
        body,
        out_shape=outs,
        scratch_shapes=list(scratch),
        compiler_params=pltpu.CompilerParams(vmem_limit_bytes=48 * 1024 * 1024),
        **more,
    )(*args)


def pack_body(class_block, images_any, ctf_any, noise_any, cands_any, out_ref, images_ref, ctf_ref, noise_ref, cands_ref, sems):
    copies = [
        pltpu.make_async_copy(source, target, sems.at[i])
        for i, (source, target) in enumerate(
            (
                (cands_any, cands_ref),
                (ctf_any, ctf_ref),
                (noise_any, noise_ref),
                (images_any, images_ref),
            )
        )
    ]
    for copy in copies:
        copy.start()
    for copy in copies:
        copy.wait()
    part = images_ref.shape[0]
    ctf = ctf_ref[...]
    noise = noise_ref[...]
    ctf_noise = ctf * noise
    factor = jnp.concatenate([ctf_noise, ctf_noise], axis=1)
    quad = (ctf * ctf * noise).astype(BF16)
    quad = jnp.concatenate([quad, quad], axis=1)
    cands = cands_ref[...]
    first = jnp.broadcast_to(cands[0:1, :], (ROWS, part))
    second = jnp.broadcast_to(cands[1:2, :], (ROWS, part))
    row = rows_of((ROWS, part))
    low = (row // 2) * class_block
    hit = ((first >= low) & (first < low + class_block)) | (
        (second >= low) & (second < low + class_block)
    )
    hit = hit.astype(F32)
    taken = jnp.zeros((ROWS, 1), F32)
    columns = []
    slot = (rows_of((ROWS, 1)) % 2).astype(F32)
    for p in range(part):
        now = hit[:, p : p + 1]
        columns.append(now * (taken == slot).astype(F32))
        taken = taken + now
    packing = jnp.concatenate(columns, axis=1)
    valid = jnp.sum(packing, axis=1, keepdims=True)
    own = jnp.sum(packing * lanes_of((ROWS, part)).astype(F32), axis=1, keepdims=True)
    base = low[:, 0:1].astype(F32)
    id_a = jnp.sum(packing * first.astype(F32), axis=1, keepdims=True) - base
    id_b = jnp.sum(packing * second.astype(F32), axis=1, keepdims=True) - base
    lane = lanes_of((ROWS, LANES))
    klane = (lane - HALF).astype(F32)
    in_block = (lane >= HALF) & (lane < HALF + class_block)
    flags = (in_block & ((klane == id_a) | (klane == id_b))) | (
        (lane - P_LANE).astype(F32) == own
    )
    flags = flags.astype(F32) * (valid > 0.5).astype(F32)
    packing = packing.astype(BF16)

    def put(value, start, size):
        value = value.astype(BF16)
        for owner in range(ROWS // 2):
            out_ref[owner, :, start : start + size] = value[2 * owner : 2 * owner + 2, :]

    quad_rows = jnp.dot(packing, quad, preferred_element_type=F32)
    put(jnp.where(lane < HALF, quad_rows, flags), FEATURES, LANES)
    wide = jnp.concatenate([factor] * 4, axis=1)
    step = 4 * LANES
    for t in range(FEATURES // step):
        part_w = (images_ref[:, t * step : (t + 1) * step].astype(F32) * wide).astype(BF16)
        put(jnp.dot(packing, part_w, preferred_element_type=F32), t * step, step)


def prep_body(classes_ref, table_ref, energy_ref):
    count = classes_ref.shape[0]
    acc = jnp.zeros((count, LANES), F32)
    for b in range(ROTATIONS):
        block = classes_ref[:, b * BLOCK : (b + 1) * BLOCK]
        table_ref[b * HALF : b * HALF + count, :] = block
        table_ref[b * HALF + count : (b + 1) * HALF, :] = jnp.zeros((HALF - count, BLOCK), BF16)
        wide = block.astype(F32)
        square = wide * wide
        acc = acc + square[:, :LANES] + square[:, LANES:]
    acc = acc + pltpu.roll(acc, HALF, 1)
    energy_ref[...] = jnp.zeros((LANES, LANES), F32)
    energy_ref[0:count, :] = acc
    energy_ref[HALF : HALF + count, :] = acc


def row_facts(meta):
    lane = lanes_of(meta.shape)
    flags = jnp.where((lane >= HALF) & (lane < P_LANE), meta, 0.0)
    flags = (flags + pltpu.roll(flags, HALF, 1)) > 0.5
    marks = jnp.where(lane >= P_LANE, meta, 0.0)
    valid = jnp.sum(marks, axis=1, keepdims=True)
    own = jnp.sum(marks * (lane - P_LANE).astype(F32), axis=1, keepdims=True)
    source = (rows_of(meta.shape) % ROWS // 2 * 4).astype(F32)
    spot = (lane.astype(F32) == source + own) & (valid > 0.5)
    return flags, spot


def slots_of(live):
    lane = lanes_of(live.shape)
    ids = (lane % HALF).astype(F32)
    low = jnp.min(jnp.where(live, ids, 1000.0), axis=1, keepdims=True)
    high = jnp.max(jnp.where(live, ids, -1.0), axis=1, keepdims=True)
    high = jnp.where(high > low, high, -1.0)
    return ids == low, ids == high, low < 999.0, high > -0.5


def correlate(rows_ref, table_ref, energy_ref, logits_ref, blocks_ref, acc_ref):
    total_rows = ROTATIONS * ROWS
    for b in range(ROTATIONS):
        blocks_ref[b * ROWS : (b + 1) * ROWS, :] = rows_ref[:, b * BLOCK : (b + 1) * BLOCK]
    for m in range(ROTATIONS // 4):
        g = lax.dot_general(
            blocks_ref[...],
            table_ref[m * BLOCK : (m + 1) * BLOCK, :],
            (((1,), (1,)), ((), ())),
            preferred_element_type=F32,
        )
        for h in range(2):
            tile = g[:, h * LANES : (h + 1) * LANES]
            shift = (2 * m + h) * 2 * ROWS
            if shift == 0:
                acc_ref[...] = tile
            else:
                acc_ref[0 : total_rows - shift, :] += tile[shift:, :]
                acc_ref[total_rows - shift :, :] += tile[:shift, :]
    meta = rows_ref[:, FEATURES : FEATURES + LANES].astype(F32)
    lane = lanes_of((ROWS, LANES))
    quad = jnp.where(lane < HALF, meta, 0.0)
    norm = 0.5 * lax.dot_general(
        quad, energy_ref[...], (((1,), (1,)), ((), ())), precision=HIGH, preferred_element_type=F32
    )
    for r in range(ROTATIONS):
        nxt = (r + 1) % ROTATIONS
        mixed = jnp.where(
            lane < HALF,
            acc_ref[r * ROWS : (r + 1) * ROWS, :],
            acc_ref[nxt * ROWS : (nxt + 1) * ROWS, :],
        )
        logits_ref[r * ROWS : (r + 1) * ROWS, :] = mixed + pltpu.roll(mixed, HALF, 1) - norm


def cross_body(rows_ref, table_ref, energy_ref, logits_ref, stats_ref, blocks_ref, acc_ref):
    correlate(rows_ref, table_ref, energy_ref, logits_ref, blocks_ref, acc_ref)
    meta = rows_ref[:, FEATURES : FEATURES + LANES].astype(F32)
    lane = lanes_of((ROWS, LANES))
    live, spot = row_facts(meta)
    left = live & (lane < HALF)
    best = jnp.full((ROWS, LANES), NEGATIVE, F32)
    for r in range(ROTATIONS):
        value = logits_ref[r * ROWS : (r + 1) * ROWS, :]
        best = jnp.maximum(best, jnp.where(left, value, NEGATIVE))
    peak = jnp.max(best, axis=1, keepdims=True)
    total = jnp.zeros((ROWS, LANES), F32)
    for r in range(ROTATIONS):
        value = logits_ref[r * ROWS : (r + 1) * ROWS, :]
        total = total + jnp.where(left, jnp.exp(value - peak), 0.0)
    total = jnp.sum(total, axis=1, keepdims=True)
    peak_row = jnp.max(jnp.where(spot, peak, NEGATIVE), axis=0, keepdims=True)
    total_row = jnp.sum(jnp.where(spot, total, 0.0), axis=0, keepdims=True)
    for d in range(stats_ref.shape[0]):
        stats_ref[d, 0:1, :] = peak_row
        stats_ref[d, 1:2, :] = total_row


def share_body(place_ref, one_ref, two_ref, one_logits_ref, two_logits_ref, mine_ref, theirs_ref):
    second = place_ref[0] == 1
    pieces = []
    for b in range(ROTATIONS):
        for ref in (one_ref, two_ref):
            pieces.append(ref[:, b * BLOCK : (b + 1) * BLOCK])
    value = jnp.concatenate(pieces, axis=0).astype(F32)
    rolled = pltpu.roll(value, BLOCK - SLICE, 1)
    after = jnp.concatenate([rolled[2 * ROWS :, :], rolled[: 2 * ROWS, :]], axis=0)
    moved = jnp.where(lanes_of(value.shape) < BLOCK - SLICE, rolled, after)
    mine_ref[0:BLOCK, :] = jnp.where(second, moved, value).T.astype(BF16)
    theirs_ref[0:BLOCK, :] = jnp.where(second, value, moved).T.astype(BF16)
    columns = slice(FEATURES, FEATURES + LANES)
    meta = jnp.concatenate([one_ref[:, columns], two_ref[:, columns]], axis=0).astype(F32)
    lane = lanes_of(meta.shape)
    live, spot = row_facts(meta)
    first, other, has_first, has_other = slots_of(live)
    known = ((lane < ROTATIONS) & has_first) | (
        (lane >= ROTATIONS) & (lane < 2 * ROTATIONS) & has_other
    )
    quad = jnp.where(lane < HALF, meta, 0.0)
    quad = quad + pltpu.roll(quad, HALF, 1)
    one_mask = first & (lane < HALF)
    two_mask = other & (lane < HALF)
    compact = jnp.zeros(meta.shape, F32)
    for r in range(ROTATIONS):
        own = slice(r * ROWS, (r + 1) * ROWS)
        level = jnp.concatenate([one_logits_ref[own, :], two_logits_ref[own, :]], axis=0)
        one = jnp.sum(jnp.where(one_mask, level, 0.0), axis=1, keepdims=True)
        two = jnp.sum(jnp.where(two_mask, level, 0.0), axis=1, keepdims=True)
        compact = jnp.where(lane == r, one, jnp.where(lane == ROTATIONS + r, two, compact))
    high = compact.astype(BF16)
    left = compact - high.astype(F32)
    middle = left.astype(BF16)
    left = left - middle.astype(F32)
    for i, fact in enumerate((first, other, spot, known, quad, high, middle, left)):
        fact = fact.astype(F32).astype(BF16)
        for ref in (mine_ref, theirs_ref):
            ref[BLOCK:, i * LANES : (i + 1) * LANES] = fact
    for ref in (mine_ref, theirs_ref):
        ref[BLOCK:, 8 * LANES :] = jnp.zeros((2 * ROWS, DEPTH - 8 * LANES), BF16)


def sums_body(
    place_ref, stats_ref, mine_ref, other_any, out_any, evid_ref, pay_ref, other_ref, table_a, table_b, sems
):
    fetch_facts = pltpu.make_async_copy(
        other_any.at[pl.ds(BLOCK, 2 * ROWS), :], other_ref.at[pl.ds(BLOCK, 2 * ROWS), :], sems.at[TARGETS]
    )
    fetch_turned = pltpu.make_async_copy(
        other_any.at[pl.ds(0, BLOCK), :], other_ref.at[pl.ds(0, BLOCK), :], sems.at[TARGETS + 1]
    )
    fetch_facts.start()
    fetch_turned.start()
    core, near = place_ref[0], place_ref[1]
    tables = (table_a, table_b)
    lane = lanes_of((ROWS, LANES))
    on_left = lane < HALF
    weights, quads = [], []
    for g in range(4):
        if g == 2:
            fetch_facts.wait()
        facts_ref, table_ref = (mine_ref, other_ref)[g // 2], tables[g // 2]

        def fact(i):
            at = BLOCK + g % 2 * ROWS
            return facts_ref[at : at + ROWS, i * LANES : (i + 1) * LANES].astype(F32)

        at_core = core if g < 2 else 1 - core
        at_near = near if g % 2 == 0 else 1 - near
        stats = stats_ref[pl.ds((at_near * 2 + at_core) * 8, 8), :, :]
        peaks = stats[:, 0, :]
        totals = stats[:, 1, :]
        highest = jnp.max(peaks, axis=0, keepdims=True)
        total = jnp.sum(totals * jnp.exp(peaks - highest), axis=0, keepdims=True)
        evidence = highest + jnp.log(total)
        if g == 0:
            evid_ref[...] = evidence
        first, second = fact(0), fact(1)
        row_evidence = jnp.sum(
            jnp.where(fact(2) > 0.5, evidence, 0.0), axis=1, keepdims=True
        )
        logits = fact(5) + (fact(6) + fact(7))
        post = jnp.where(fact(3) > 0.5, jnp.exp(logits - row_evidence), 0.0)
        post = post.astype(BF16).astype(F32)
        total_one = jnp.sum(jnp.where(lane < ROTATIONS, post, 0.0), axis=1, keepdims=True)
        total_two = jnp.sum(jnp.where(lane < ROTATIONS, 0.0, post), axis=1, keepdims=True)
        weights.append(total_one * first + total_two * second)
        quads.append(fact(4))
        half = ROTATIONS // 2

        def spread(r):
            return (
                post[:, r : r + 1] * first + post[:, ROTATIONS + r : ROTATIONS + r + 1] * second
            )

        for r in range(half):
            here, there = spread(r), spread(r + half)
            for row, value in (
                (r, jnp.where(on_left, here, there)),
                (r + half, jnp.where(on_left, there, here)),
            ):
                value = value.astype(BF16)
                for turn in range(2):
                    at = ((turn * ROTATIONS + row) * 2 + g % 2) * ROWS
                    table_ref[at : at + ROWS, :] = value
    weight = jnp.concatenate(weights, axis=0)
    quad = jnp.concatenate(quads, axis=0)
    by_class = jnp.dot(weight.T, quad, precision=HIGH, preferred_element_type=F32)
    by_shell = jnp.dot(quad.T, weight, precision=HIGH, preferred_element_type=F32)[0:HALF, :]
    tail = jnp.where(on_left, by_class[0:16, :], by_class[16:32, :]).astype(BF16)
    wide = lanes_of((HALF, LANES))
    spare = jnp.where(
        (wide >= CLASSES) & (wide < HALF),
        pltpu.roll(by_shell, CLASSES - 32, 1),
        jnp.where(wide >= HALF + CLASSES, pltpu.roll(by_shell, CLASSES - 46, 1), 0.0),
    ).astype(BF16)
    for d in range(TARGETS):
        pay_ref[d, 0:HALF, :] = spare
        pay_ref[d, PAY_ROWS : PAY_ROWS + 16, :] = tail
    copies = [
        pltpu.make_async_copy(pay_ref.at[d], out_any.at[d], sems.at[d]) for d in range(TARGETS)
    ]
    started = 0
    fetch_turned.wait()
    base = (ROTATIONS - CHUNKS * near) * 2 * ROWS
    for group in ((0, 1), (2, 3), (4, 5), (6, 7), (8,)):
        kept = {b: [i for i in range(16) if (16 * b + i) // CHUNKS % 2 == 0] for b in group}
        used = sorted(set(i for b in group for i in kept[b]))
        bands = []
        for i in used:
            if bands and bands[-1][1] == i:
                bands[-1][1] = i + 1
            else:
                bands.append([i, i + 1])
        left = jnp.concatenate(
            [
                jnp.concatenate([ref[16 * lo : 16 * hi, :] for lo, hi in bands], axis=0)
                for ref in (mine_ref, other_ref)
            ],
            axis=1,
        )
        columns = []
        for b in group:
            start = pl.multiple_of(base - b * 2 * ROWS, 2 * ROWS)
            columns.append(jnp.concatenate([ref[pl.ds(start, DEPTH), :] for ref in tables], axis=0))
        right = jnp.concatenate(columns, axis=1)
        out = jnp.dot(left, right, preferred_element_type=F32).astype(BF16)
        for c, b in enumerate(group):
            for i in kept[b]:
                n = used.index(i)
                for e in range(2):
                    q = b * 16 + i
                    d, j = e * 8 + q // CHUNKS // 2, q % CHUNKS
                    from_lane = c * LANES + e * HALF
                    piece = out[n * 16 : (n + 1) * 16, from_lane : from_lane + CLASSES]
                    if j < CHUNKS - 1:
                        at = j // 2 * 16
                        lo = j % 2 * HALF
                        pay_ref[d, at : at + 16, lo : lo + CLASSES] = piece
                    else:
                        pay_ref[d, PAY_ROWS - 8 : PAY_ROWS, 0:CLASSES] = piece[0:8, :]
                        pay_ref[d, PAY_ROWS - 8 : PAY_ROWS, HALF : HALF + CLASSES] = piece[8:16, :]
        finished = (16 * group[-1] + 16 + CHUNKS) // (2 * CHUNKS)
        for z in range(started, finished):
            copies[z].start()
            copies[8 + z].start()
        started = finished
    for copy in copies:
        copy.wait()


def final_body(parts_ref, sums_ref, weights_ref):
    acc = parts_ref[0, :, :].astype(F32)
    for g in range(1, TARGETS):
        acc = acc + parts_ref[g, :, :].astype(F32)
    pieces = []
    for j in range(CHUNKS - 1):
        lo = j % 2 * HALF
        pieces.append(acc[j // 2 * 16 : j // 2 * 16 + 16, lo : lo + HALF])
    pieces.append(acc[PAY_ROWS - 8 : PAY_ROWS, 0:HALF])
    pieces.append(acc[PAY_ROWS - 8 : PAY_ROWS, HALF:LANES])
    full = jnp.concatenate(pieces, axis=0)
    sums_ref[...] = full.T[0:CLASSES, :]
    weights_ref[0:16, :] = acc[PAY_ROWS : PAY_ROWS + 16, 0:HALF]
    weights_ref[16:32, :] = acc[PAY_ROWS : PAY_ROWS + 16, HALF:LANES]
    rest = acc[0:HALF, :].T
    weights_ref[32:46, :] = rest[CLASSES:HALF, :]
    weights_ref[46:CLASSES, :] = rest[HALF + CLASSES : HALF + CLASSES + 4, :]


def shards(images, ctf, inv_noise, classes, candidates):
    class_block = classes.shape[0]
    part = images.shape[0]
    my_index = lax.axis_index("cls")
    place = jnp.stack([lax.axis_index("core"), lax.axis_index("xl")]).astype(jnp.int32)
    total_rows = ROTATIONS * ROWS
    width = FEATURES + LANES
    shape = jax.ShapeDtypeStruct
    vmem = pl.BlockSpec(memory_space=pltpu.VMEM)
    smem = pl.BlockSpec(memory_space=pltpu.SMEM)
    raw = pl.BlockSpec(memory_space=pltpu.HBM)

    def swap(value, axes):
        return lax.all_to_all(value, axes, split_axis=0, concat_axis=0, tiled=True)

    def flip(value, axis):
        return lax.ppermute(value, axis, [(0, 1), (1, 0)])

    def pack(*refs):
        pack_body(class_block, *refs)

    hbm = [
        pltpu.with_memory_space_constraint(value, pltpu.HBM)
        for value in (images, ctf, inv_noise.reshape(1, CYCLES), candidates.T)
    ]
    packed = call(
        pack,
        shape((8, 2, width), BF16),
        *hbm,
        in_specs=[raw] * 4,
        scratch=[
            pltpu.VMEM((part, FEATURES), BF16),
            pltpu.VMEM((part, CYCLES), F32),
            pltpu.VMEM((1, CYCLES), F32),
            pltpu.VMEM((2, part), jnp.int32),
            pltpu.SemaphoreType.DMA((4,)),
        ],
    )
    rows = swap(packed, "cls").reshape(ROWS, width)
    table, energy = call(
        prep_body,
        (shape((ROTATIONS * HALF, BLOCK), BF16), shape((LANES, LANES), F32)),
        classes,
    )
    rows, table, energy = lax.optimization_barrier((rows, table, energy))
    beside = flip(rows, "xl")
    logits, stats = call(
        cross_body,
        (shape((total_rows, LANES), F32), shape((32, 2, LANES), F32)),
        rows,
        table,
        energy,
        scratch=[pltpu.VMEM((total_rows, BLOCK), BF16), pltpu.VMEM((total_rows, LANES), F32)],
    )
    group_stats = swap(stats, ("xl", "core", "cls"))

    shared = shape((BLOCK + 2 * ROWS, DEPTH), BF16)

    def trade(one, two, one_logits):
        two_logits = call(
            correlate,
            shape((total_rows, LANES), F32),
            two,
            table,
            energy,
            scratch=[pltpu.VMEM((total_rows, BLOCK), BF16), pltpu.VMEM((total_rows, LANES), F32)],
        )
        own, theirs = call(
            share_body,
            (shared, shared),
            place,
            one,
            two,
            one_logits,
            two_logits,
            in_specs=[smem] + [vmem] * 4,
        )
        return own, flip(theirs, "core")

    def alone(one, two, one_logits):
        nothing = jnp.zeros(shared.shape, BF16)
        return nothing, nothing

    own_share, other_share = lax.cond(place[0] < 2, trade, alone, rows, beside, logits)
    pay, evidence = call(
        sums_body,
        (shape((TARGETS, PAY_ROWS + 16, LANES), BF16), shape((1, LANES), F32)),
        place,
        group_stats,
        own_share,
        pltpu.with_memory_space_constraint(other_share, pltpu.HBM),
        in_specs=[smem, vmem, vmem, raw],
        out_specs=(raw, vmem),
        scratch=[
            pltpu.VMEM((TARGETS, PAY_ROWS + 16, LANES), BF16),
            pltpu.VMEM(shared.shape, BF16),
            pltpu.VMEM((2 * DEPTH, LANES), BF16),
            pltpu.VMEM((2 * DEPTH, LANES), BF16),
            pltpu.SemaphoreType.DMA((TARGETS + 2,)),
        ],
    )
    parts = swap(pay, ("xh", "z"))
    sums, weight_sums = call(
        final_body, (shape((CLASSES, SLICE), F32), shape((CLASSES, CYCLES), F32)), parts
    )
    own = lax.dynamic_slice(evidence, (0, my_index * 4), (1, 4)).reshape(4)
    return sums.T, weight_sums, own


def solution(mesh):
    dom = ("xh", "xl", "z", "core")
    fine = Mesh(mesh.devices.reshape(2, 2, 8, 2, 8), dom + ("cls",))
    every = dom + ("cls",)
    in_specs = (P(every, None), P(every, None), P(), P("cls", None), P(every, None))
    out_specs = (P(dom, "cls"), P("cls", None), P(every))
    return jax.shard_map(shards, mesh=fine, in_specs=in_specs, out_specs=out_specs, check_vma=False)
```

```python
import jax
import jax.numpy as jnp
from jax import lax
from jax.experimental import pallas as pl
from jax.experimental.pallas import tpu as pltpu
from jax.sharding import Mesh, PartitionSpec as P

CYCLES = 64
ROTATIONS = 36
BLOCK = 256
FEATURES = ROTATIONS * BLOCK
LANES = 128
HALF = 64
ROWS = 16
TURNS = 2 * ROTATIONS - 4
GROUPS = 64
TARGETS = GROUPS // 4
DEPTH = 2 * ROTATIONS * ROWS
CLASSES = 50
SLICE = FEATURES // GROUPS
CHUNKS = SLICE // 16
PAY_ROWS = SLICE // 2
NEGATIVE = -1e30
P_LANE = 120
F32 = jnp.float32
BF16 = jnp.bfloat16
HIGH = lax.Precision.HIGHEST


def lanes_of(shape):
    return lax.broadcasted_iota(jnp.int32, shape, len(shape) - 1)


def rows_of(shape):
    return lax.broadcasted_iota(jnp.int32, shape, len(shape) - 2)


def call(body, outs, *args, in_specs=None, out_specs=None, scratch=()):
    more = {} if in_specs is None else {"in_specs": in_specs}
    if out_specs is not None:
        more["out_specs"] = out_specs
    return pl.pallas_call(
        body,
        out_shape=outs,
        scratch_shapes=list(scratch),
        compiler_params=pltpu.CompilerParams(vmem_limit_bytes=48 * 1024 * 1024),
        **more,
    )(*args)


def pack_body(class_block, images_any, ctf_any, noise_any, cands_any, out_any, images_ref, ctf_ref, noise_ref, cands_ref, out_ref, sems):
    copies = [
        pltpu.make_async_copy(source, target, sems.at[i])
        for i, (source, target) in enumerate(
            (
                (cands_any, cands_ref),
                (ctf_any, ctf_ref),
                (noise_any, noise_ref),
                (images_any, images_ref),
            )
        )
    ]
    for copy in copies:
        copy.start()
    for copy in copies[:3]:
        copy.wait()
    part = images_ref.shape[0]
    ctf = ctf_ref[...]
    noise = noise_ref[...]
    ctf_noise = ctf * noise
    factor = jnp.concatenate([ctf_noise, ctf_noise], axis=1)
    quad = (ctf * ctf * noise).astype(BF16)
    quad = jnp.concatenate([quad, quad], axis=1)
    cands = cands_ref[...]
    first = jnp.broadcast_to(cands[0:1, :], (ROWS, part))
    second = jnp.broadcast_to(cands[1:2, :], (ROWS, part))
    row = rows_of((ROWS, part))
    low = (row // 2) * class_block
    hit = ((first >= low) & (first < low + class_block)) | (
        (second >= low) & (second < low + class_block)
    )
    hit = hit.astype(F32)
    taken = jnp.zeros((ROWS, 1), F32)
    columns = []
    slot = (rows_of((ROWS, 1)) % 2).astype(F32)
    for p in range(part):
        now = hit[:, p : p + 1]
        columns.append(now * (taken == slot).astype(F32))
        taken = taken + now
    packing = jnp.concatenate(columns, axis=1)
    valid = jnp.sum(packing, axis=1, keepdims=True)
    own = jnp.sum(packing * lanes_of((ROWS, part)).astype(F32), axis=1, keepdims=True)
    base = low[:, 0:1].astype(F32)
    id_a = jnp.sum(packing * first.astype(F32), axis=1, keepdims=True) - base
    id_b = jnp.sum(packing * second.astype(F32), axis=1, keepdims=True) - base
    lane = lanes_of((ROWS, LANES))
    klane = (lane - HALF).astype(F32)
    in_block = (lane >= HALF) & (lane < HALF + class_block)
    flags = (in_block & ((klane == id_a) | (klane == id_b))) | (
        (lane - P_LANE).astype(F32) == own
    )
    flags = flags.astype(F32) * (valid > 0.5).astype(F32)
    packing = packing.astype(BF16)

    def put(value, start, size):
        value = value.astype(BF16)
        for owner in range(ROWS // 2):
            out_ref[owner, :, start : start + size] = value[2 * owner : 2 * owner + 2, :]

    quad_rows = jnp.dot(packing, quad, preferred_element_type=F32)
    put(jnp.where(lane < HALF, quad_rows, flags), FEATURES, LANES)
    wide = jnp.concatenate([factor] * 4, axis=1)
    step = 4 * LANES
    copies[3].wait()
    sent = []

    def leave(start, size):
        piece = pl.ds(start, size)
        copy = pltpu.make_async_copy(
            out_ref.at[:, :, piece], out_any.at[:, :, piece], sems.at[4 + len(sent)]
        )
        copy.start()
        sent.append(copy)

    leave(FEATURES, LANES)
    for t in range(FEATURES // step):
        part_w = (images_ref[:, t * step : (t + 1) * step].astype(F32) * wide).astype(BF16)
        put(jnp.dot(packing, part_w, preferred_element_type=F32), t * step, step)
        if t % 6 == 5:
            leave((t - 5) * step, 6 * step)
    for copy in sent:
        copy.wait()


def prep_body(classes_ref, table_ref, energy_ref):
    count = classes_ref.shape[0]
    acc = jnp.zeros((count, LANES), F32)
    for b in range(ROTATIONS):
        block = classes_ref[:, b * BLOCK : (b + 1) * BLOCK]
        m, c = b // 4, b % 4
        table_ref[c * HALF : c * HALF + count, m * BLOCK : (m + 1) * BLOCK] = block
        wide = block.astype(F32)
        square = wide * wide
        acc = acc + square[:, :LANES] + square[:, LANES:]
    for c in range(4):
        table_ref[c * HALF + count : (c + 1) * HALF, :] = jnp.zeros(
            (HALF - count, ROTATIONS // 4 * BLOCK), BF16
        )
    acc = acc + pltpu.roll(acc, HALF, 1)
    energy_ref[...] = jnp.zeros((LANES, LANES), F32)
    energy_ref[0:count, :] = acc
    energy_ref[HALF : HALF + count, :] = acc


def row_facts(meta):
    lane = lanes_of(meta.shape)
    flags = jnp.where((lane >= HALF) & (lane < P_LANE), meta, 0.0)
    flags = (flags + pltpu.roll(flags, HALF, 1)) > 0.5
    marks = jnp.where(lane >= P_LANE, meta, 0.0)
    valid = jnp.sum(marks, axis=1, keepdims=True)
    own = jnp.sum(marks * (lane - P_LANE).astype(F32), axis=1, keepdims=True)
    source = (rows_of(meta.shape) % ROWS // 2 * 4).astype(F32)
    spot = (lane.astype(F32) == source + own) & (valid > 0.5)
    return flags, spot


def slots_of(live):
    lane = lanes_of(live.shape)
    ids = (lane % HALF).astype(F32)
    low = jnp.min(jnp.where(live, ids, 1000.0), axis=1, keepdims=True)
    high = jnp.max(jnp.where(live, ids, -1.0), axis=1, keepdims=True)
    high = jnp.where(high > low, high, -1.0)
    return ids == low, ids == high, low < 999.0, high > -0.5


def correlate(rows_ref, table_ref, energy_ref, logits_ref, blocks_ref, acc_ref):
    total_rows = ROTATIONS * ROWS
    for b in range(TURNS):
        at = b % ROTATIONS * BLOCK
        blocks_ref[b * ROWS : (b + 1) * ROWS, :] = rows_ref[:, at : at + BLOCK]
    left = jnp.concatenate(
        [
            blocks_ref[4 * m * ROWS : 4 * m * ROWS + total_rows, :]
            for m in range(ROTATIONS // 4)
        ],
        axis=1,
    )
    acc_ref[...] = lax.dot_general(
        left, table_ref[...], (((1,), (1,)), ((), ())), preferred_element_type=F32
    )
    meta = rows_ref[:, FEATURES : FEATURES + LANES].astype(F32)
    lane = lanes_of((ROWS, LANES))
    quad = jnp.where(lane < HALF, meta, 0.0)
    norm = 0.5 * lax.dot_general(
        quad, energy_ref[...], (((1,), (1,)), ((), ())), precision=HIGH, preferred_element_type=F32
    )

    def tile(r, half):
        r = r % ROTATIONS
        return acc_ref[r * ROWS : (r + 1) * ROWS, half * LANES : (half + 1) * LANES]

    for r in range(ROTATIONS):
        mixed = jnp.where(lane < HALF, tile(r, 0), tile(r + 1, 0)) + jnp.where(
            lane < HALF, tile(r + 2, 1), tile(r + 3, 1)
        )
        logits_ref[r * ROWS : (r + 1) * ROWS, :] = mixed + pltpu.roll(mixed, HALF, 1) - norm


def cross_body(rows_ref, table_ref, energy_ref, logits_ref, stats_ref, blocks_ref, acc_ref):
    correlate(rows_ref, table_ref, energy_ref, logits_ref, blocks_ref, acc_ref)
    meta = rows_ref[:, FEATURES : FEATURES + LANES].astype(F32)
    lane = lanes_of((ROWS, LANES))
    live, spot = row_facts(meta)
    left = live & (lane < HALF)
    best = jnp.full((ROWS, LANES), NEGATIVE, F32)
    for r in range(ROTATIONS):
        value = logits_ref[r * ROWS : (r + 1) * ROWS, :]
        best = jnp.maximum(best, jnp.where(left, value, NEGATIVE))
    peak = jnp.max(best, axis=1, keepdims=True)
    total = jnp.zeros((ROWS, LANES), F32)
    for r in range(ROTATIONS):
        value = logits_ref[r * ROWS : (r + 1) * ROWS, :]
        total = total + jnp.where(left, jnp.exp(value - peak), 0.0)
    total = jnp.sum(total, axis=1, keepdims=True)
    peak_row = jnp.max(jnp.where(spot, peak, NEGATIVE), axis=0, keepdims=True)
    total_row = jnp.sum(jnp.where(spot, total, 0.0), axis=0, keepdims=True)
    for d in range(stats_ref.shape[0]):
        stats_ref[d, 0:1, :] = peak_row
        stats_ref[d, 1:2, :] = total_row


def share_body(place_ref, one_ref, two_ref, one_logits_ref, two_logits_ref, mine_ref, theirs_ref):
    second = place_ref[0] == 1
    pieces = []
    for b in range(ROTATIONS):
        for ref in (one_ref, two_ref):
            pieces.append(ref[:, b * BLOCK : (b + 1) * BLOCK])
    value = jnp.concatenate(pieces, axis=0).astype(F32)
    rolled = pltpu.roll(value, BLOCK - SLICE, 1)
    after = jnp.concatenate([rolled[2 * ROWS :, :], rolled[: 2 * ROWS, :]], axis=0)
    moved = jnp.where(lanes_of(value.shape) < BLOCK - SLICE, rolled, after)
    mine_ref[0:BLOCK, :] = jnp.where(second, moved, value).T.astype(BF16)
    theirs_ref[0:BLOCK, :] = jnp.where(second, value, moved).T.astype(BF16)
    columns = slice(FEATURES, FEATURES + LANES)
    meta = jnp.concatenate([one_ref[:, columns], two_ref[:, columns]], axis=0).astype(F32)
    lane = lanes_of(meta.shape)
    live, spot = row_facts(meta)
    first, other, has_first, has_other = slots_of(live)
    known = ((lane < ROTATIONS) & has_first) | (
        (lane >= ROTATIONS) & (lane < 2 * ROTATIONS) & has_other
    )
    quad = jnp.where(lane < HALF, meta, 0.0)
    quad = quad + pltpu.roll(quad, HALF, 1)
    one_mask = first & (lane < HALF)
    two_mask = other & (lane < HALF)
    compact = jnp.zeros(meta.shape, F32)
    for r in range(ROTATIONS):
        own = slice(r * ROWS, (r + 1) * ROWS)
        level = jnp.concatenate([one_logits_ref[own, :], two_logits_ref[own, :]], axis=0)
        one = jnp.sum(jnp.where(one_mask, level, 0.0), axis=1, keepdims=True)
        two = jnp.sum(jnp.where(two_mask, level, 0.0), axis=1, keepdims=True)
        compact = jnp.where(lane == r, one, jnp.where(lane == ROTATIONS + r, two, compact))
    high = compact.astype(BF16)
    left = compact - high.astype(F32)
    middle = left.astype(BF16)
    left = left - middle.astype(F32)
    for i, fact in enumerate((first, other, spot, known, quad, high, middle, left)):
        fact = fact.astype(F32).astype(BF16)
        for ref in (mine_ref, theirs_ref):
            ref[BLOCK:, i * LANES : (i + 1) * LANES] = fact
    for ref in (mine_ref, theirs_ref):
        ref[BLOCK:, 8 * LANES :] = jnp.zeros((2 * ROWS, DEPTH - 8 * LANES), BF16)


def sums_body(
    place_ref, stats_ref, mine_ref, other_any, out_any, evid_ref, pay_ref, other_ref, table_a, table_b, sems
):
    fetch_facts = pltpu.make_async_copy(
        other_any.at[pl.ds(BLOCK, 2 * ROWS), :], other_ref.at[pl.ds(BLOCK, 2 * ROWS), :], sems.at[TARGETS]
    )
    fetch_turned = pltpu.make_async_copy(
        other_any.at[pl.ds(0, BLOCK), :], other_ref.at[pl.ds(0, BLOCK), :], sems.at[TARGETS + 1]
    )
    fetch_facts.start()
    fetch_turned.start()
    core, near = place_ref[0], place_ref[1]
    tables = (table_a, table_b)
    lane = lanes_of((ROWS, LANES))
    on_left = lane < HALF
    weights, quads = [], []
    for g in range(4):
        if g == 2:
            fetch_facts.wait()
        facts_ref, table_ref = (mine_ref, other_ref)[g // 2], tables[g // 2]

        def fact(i):
            at = BLOCK + g % 2 * ROWS
            return facts_ref[at : at + ROWS, i * LANES : (i + 1) * LANES].astype(F32)

        at_core = core if g < 2 else 1 - core
        at_near = near if g % 2 == 0 else 1 - near
        stats = stats_ref[pl.ds((at_near * 2 + at_core) * 8, 8), :, :]
        peaks = stats[:, 0, :]
        totals = stats[:, 1, :]
        highest = jnp.max(peaks, axis=0, keepdims=True)
        total = jnp.sum(totals * jnp.exp(peaks - highest), axis=0, keepdims=True)
        evidence = highest + jnp.log(total)
        if g == 0:
            evid_ref[...] = evidence
        first, second = fact(0), fact(1)
        row_evidence = jnp.sum(
            jnp.where(fact(2) > 0.5, evidence, 0.0), axis=1, keepdims=True
        )
        logits = fact(5) + (fact(6) + fact(7))
        post = jnp.where(fact(3) > 0.5, jnp.exp(logits - row_evidence), 0.0)
        post = post.astype(BF16).astype(F32)
        total_one = jnp.sum(jnp.where(lane < ROTATIONS, post, 0.0), axis=1, keepdims=True)
        total_two = jnp.sum(jnp.where(lane < ROTATIONS, 0.0, post), axis=1, keepdims=True)
        weights.append(total_one * first + total_two * second)
        quads.append(fact(4))
        half = ROTATIONS // 2

        def spread(r):
            return (
                post[:, r : r + 1] * first + post[:, ROTATIONS + r : ROTATIONS + r + 1] * second
            )

        for r in range(half):
            here, there = spread(r), spread(r + half)
            for row, value in (
                (r, jnp.where(on_left, here, there)),
                (r + half, jnp.where(on_left, there, here)),
            ):
                value = value.astype(BF16)
                for turn in range(2):
                    at = ((turn * ROTATIONS + row) * 2 + g % 2) * ROWS
                    table_ref[at : at + ROWS, :] = value
    weight = jnp.concatenate(weights, axis=0)
    quad = jnp.concatenate(quads, axis=0)
    upper = weight.astype(BF16).astype(F32)
    parts = jnp.concatenate([upper, weight - upper], axis=0).T.astype(BF16)
    quad = jnp.concatenate([quad, quad], axis=0).astype(BF16)
    by_class = jnp.dot(parts, quad, preferred_element_type=F32)
    by_shell = by_class.T[0:HALF, :]
    tail = jnp.where(on_left, by_class[0:16, :], by_class[16:32, :]).astype(BF16)
    wide = lanes_of((HALF, LANES))
    spare = jnp.where(
        (wide >= CLASSES) & (wide < HALF),
        pltpu.roll(by_shell, CLASSES - 32, 1),
        jnp.where(wide >= HALF + CLASSES, pltpu.roll(by_shell, CLASSES - 46, 1), 0.0),
    ).astype(BF16)
    for d in range(TARGETS):
        pay_ref[d, 0:HALF, :] = spare
        pay_ref[d, PAY_ROWS : PAY_ROWS + 16, :] = tail
    copies = [
        pltpu.make_async_copy(pay_ref.at[d], out_any.at[d], sems.at[d]) for d in range(TARGETS)
    ]
    started = 0
    fetch_turned.wait()
    base = (ROTATIONS - CHUNKS * near) * 2 * ROWS
    for group in ((0, 1), (2, 3), (4, 5), (6, 7), (8,)):
        kept = {b: [i for i in range(16) if (16 * b + i) // CHUNKS % 2 == 0] for b in group}
        used = sorted(set(i for b in group for i in kept[b]))
        bands = []
        for i in used:
            if bands and bands[-1][1] == i:
                bands[-1][1] = i + 1
            else:
                bands.append([i, i + 1])
        left = jnp.concatenate(
            [
                jnp.concatenate([ref[16 * lo : 16 * hi, :] for lo, hi in bands], axis=0)
                for ref in (mine_ref, other_ref)
            ],
            axis=1,
        )
        columns = []
        for b in group:
            start = pl.multiple_of(base - b * 2 * ROWS, 2 * ROWS)
            columns.append(jnp.concatenate([ref[pl.ds(start, DEPTH), :] for ref in tables], axis=0))
        right = jnp.concatenate(columns, axis=1)
        out = jnp.dot(left, right, preferred_element_type=F32).astype(BF16)
        for c, b in enumerate(group):
            for i in kept[b]:
                n = used.index(i)
                for e in range(2):
                    q = b * 16 + i
                    d, j = e * 8 + q // CHUNKS // 2, q % CHUNKS
                    from_lane = c * LANES + e * HALF
                    piece = out[n * 16 : (n + 1) * 16, from_lane : from_lane + CLASSES]
                    if j < CHUNKS - 1:
                        at = j // 2 * 16
                        lo = j % 2 * HALF
                        pay_ref[d, at : at + 16, lo : lo + CLASSES] = piece
                    else:
                        pay_ref[d, PAY_ROWS - 8 : PAY_ROWS, 0:CLASSES] = piece[0:8, :]
                        pay_ref[d, PAY_ROWS - 8 : PAY_ROWS, HALF : HALF + CLASSES] = piece[8:16, :]
        finished = (16 * group[-1] + 16 + CHUNKS) // (2 * CHUNKS)
        for z in range(started, finished):
            copies[z].start()
            copies[8 + z].start()
        started = finished
    for copy in copies:
        copy.wait()


def final_body(parts_ref, sums_ref, weights_ref):
    acc = parts_ref[0, :, :].astype(F32)
    for g in range(1, TARGETS):
        acc = acc + parts_ref[g, :, :].astype(F32)
    pieces = []
    for j in range(CHUNKS - 1):
        lo = j % 2 * HALF
        pieces.append(acc[j // 2 * 16 : j // 2 * 16 + 16, lo : lo + HALF])
    pieces.append(acc[PAY_ROWS - 8 : PAY_ROWS, 0:HALF])
    pieces.append(acc[PAY_ROWS - 8 : PAY_ROWS, HALF:LANES])
    full = jnp.concatenate(pieces, axis=0)
    sums_ref[...] = full.T[0:CLASSES, :]
    weights_ref[0:16, :] = acc[PAY_ROWS : PAY_ROWS + 16, 0:HALF]
    weights_ref[16:32, :] = acc[PAY_ROWS : PAY_ROWS + 16, HALF:LANES]
    rest = acc[0:HALF, :].T
    weights_ref[32:46, :] = rest[CLASSES:HALF, :]
    weights_ref[46:CLASSES, :] = rest[HALF + CLASSES : HALF + CLASSES + 4, :]


def shards(images, ctf, inv_noise, classes, candidates):
    class_block = classes.shape[0]
    part = images.shape[0]
    my_index = lax.axis_index("cls")
    place = jnp.stack([lax.axis_index("core"), lax.axis_index("xl")]).astype(jnp.int32)
    total_rows = ROTATIONS * ROWS
    width = FEATURES + LANES
    shape = jax.ShapeDtypeStruct
    vmem = pl.BlockSpec(memory_space=pltpu.VMEM)
    smem = pl.BlockSpec(memory_space=pltpu.SMEM)
    raw = pl.BlockSpec(memory_space=pltpu.HBM)

    def swap(value, axes):
        return lax.all_to_all(value, axes, split_axis=0, concat_axis=0, tiled=True)

    def flip(value, axis):
        return lax.ppermute(value, axis, [(0, 1), (1, 0)])

    def pack(*refs):
        pack_body(class_block, *refs)

    hbm = [
        pltpu.with_memory_space_constraint(value, pltpu.HBM)
        for value in (images, ctf, inv_noise.reshape(1, CYCLES), candidates.T)
    ]
    packed = call(
        pack,
        shape((8, 2, width), BF16),
        *hbm,
        in_specs=[raw] * 4,
        out_specs=raw,
        scratch=[
            pltpu.VMEM((part, FEATURES), BF16),
            pltpu.VMEM((part, CYCLES), F32),
            pltpu.VMEM((1, CYCLES), F32),
            pltpu.VMEM((2, part), jnp.int32),
            pltpu.VMEM((8, 2, width), BF16),
            pltpu.SemaphoreType.DMA((8,)),
        ],
    )
    rows = swap(packed, "cls").reshape(ROWS, width)
    table, energy = call(
        prep_body,
        (shape((BLOCK, ROTATIONS // 4 * BLOCK), BF16), shape((LANES, LANES), F32)),
        classes,
    )
    rows, table, energy = lax.optimization_barrier((rows, table, energy))
    beside = flip(rows, "xl")
    logits, stats = call(
        cross_body,
        (shape((total_rows, LANES), F32), shape((32, 2, LANES), F32)),
        rows,
        table,
        energy,
        scratch=[pltpu.VMEM((TURNS * ROWS, BLOCK), BF16), pltpu.VMEM((total_rows, BLOCK), F32)],
    )
    group_stats = swap(stats, ("xl", "core", "cls"))

    shared = shape((BLOCK + 2 * ROWS, DEPTH), BF16)

    def trade(one, two, one_logits):
        two_logits = call(
            correlate,
            shape((total_rows, LANES), F32),
            two,
            table,
            energy,
            scratch=[pltpu.VMEM((TURNS * ROWS, BLOCK), BF16), pltpu.VMEM((total_rows, BLOCK), F32)],
        )
        own, theirs = call(
            share_body,
            (shared, shared),
            place,
            one,
            two,
            one_logits,
            two_logits,
            in_specs=[smem] + [vmem] * 4,
        )
        return own, flip(theirs, "core")

    def alone(one, two, one_logits):
        nothing = jnp.zeros(shared.shape, BF16)
        return nothing, nothing

    own_share, other_share = lax.cond(place[0] < 2, trade, alone, rows, beside, logits)
    pay, evidence = call(
        sums_body,
        (shape((TARGETS, PAY_ROWS + 16, LANES), BF16), shape((1, LANES), F32)),
        place,
        group_stats,
        own_share,
        pltpu.with_memory_space_constraint(other_share, pltpu.HBM),
        in_specs=[smem, vmem, vmem, raw],
        out_specs=(raw, vmem),
        scratch=[
            pltpu.VMEM((TARGETS, PAY_ROWS + 16, LANES), BF16),
            pltpu.VMEM(shared.shape, BF16),
            pltpu.VMEM((2 * DEPTH, LANES), BF16),
            pltpu.VMEM((2 * DEPTH, LANES), BF16),
            pltpu.SemaphoreType.DMA((TARGETS + 2,)),
        ],
    )
    parts = swap(pay, ("xh", "z"))
    sums, weight_sums = call(
        final_body, (shape((CLASSES, SLICE), F32), shape((CLASSES, CYCLES), F32)), parts
    )
    own = lax.dynamic_slice(evidence, (0, my_index * 4), (1, 4)).reshape(4)
    return sums.T, weight_sums, own


def solution(mesh):
    dom = ("xh", "xl", "z", "core")
    fine = Mesh(mesh.devices.reshape(2, 2, 8, 2, 8), dom + ("cls",))
    every = dom + ("cls",)
    in_specs = (P(every, None), P(every, None), P(), P("cls", None), P(every, None))
    out_specs = (P(dom, "cls"), P("cls", None), P(every))
    return jax.shard_map(shards, mesh=fine, in_specs=in_specs, out_specs=out_specs, check_vma=False)
```

```python
import jax
import jax.numpy as jnp
from jax import lax
from jax.experimental import pallas as pl
from jax.experimental.pallas import tpu as pltpu
from jax.sharding import Mesh, PartitionSpec as P

CYCLES = 64
ROTATIONS = 36
BLOCK = 256
FEATURES = ROTATIONS * BLOCK
LANES = 128
HALF = 64
ROWS = 16
TURNS = 2 * ROTATIONS - 4
GROUPS = 64
TARGETS = GROUPS // 4
DEPTH = 2 * ROTATIONS * ROWS
CLASSES = 50
SLICE = FEATURES // GROUPS
CHUNKS = SLICE // 16
PAY_ROWS = SLICE // 2
NEGATIVE = -1e30
P_LANE = 120
F32 = jnp.float32
BF16 = jnp.bfloat16
HIGH = lax.Precision.HIGHEST


def lanes_of(shape):
    return lax.broadcasted_iota(jnp.int32, shape, len(shape) - 1)


def rows_of(shape):
    return lax.broadcasted_iota(jnp.int32, shape, len(shape) - 2)


def call(body, outs, *args, in_specs=None, out_specs=None, scratch=()):
    more = {} if in_specs is None else {"in_specs": in_specs}
    if out_specs is not None:
        more["out_specs"] = out_specs
    return pl.pallas_call(
        body,
        out_shape=outs,
        scratch_shapes=list(scratch),
        compiler_params=pltpu.CompilerParams(vmem_limit_bytes=48 * 1024 * 1024),
        **more,
    )(*args)


def pack_body(class_block, images_any, ctf_any, noise_any, cands_any, out_any, images_ref, ctf_ref, noise_ref, cands_ref, out_ref, sems):
    copies = [
        pltpu.make_async_copy(source, target, sems.at[i])
        for i, (source, target) in enumerate(
            (
                (cands_any, cands_ref),
                (ctf_any, ctf_ref),
                (noise_any, noise_ref),
                (images_any, images_ref),
            )
        )
    ]
    for copy in copies:
        copy.start()
    for copy in copies[:3]:
        copy.wait()
    part = images_ref.shape[0]
    ctf = ctf_ref[...]
    noise = noise_ref[...]
    ctf_noise = ctf * noise
    factor = jnp.concatenate([ctf_noise, ctf_noise], axis=1)
    quad = (ctf * ctf * noise).astype(BF16)
    quad = jnp.concatenate([quad, quad], axis=1)
    cands = cands_ref[...]
    first = jnp.broadcast_to(cands[0:1, :], (ROWS, part))
    second = jnp.broadcast_to(cands[1:2, :], (ROWS, part))
    row = rows_of((ROWS, part))
    low = (row // 2) * class_block
    hit = ((first >= low) & (first < low + class_block)) | (
        (second >= low) & (second < low + class_block)
    )
    hit = hit.astype(F32)
    taken = jnp.zeros((ROWS, 1), F32)
    columns = []
    slot = (rows_of((ROWS, 1)) % 2).astype(F32)
    for p in range(part):
        now = hit[:, p : p + 1]
        columns.append(now * (taken == slot).astype(F32))
        taken = taken + now
    packing = jnp.concatenate(columns, axis=1)
    valid = jnp.sum(packing, axis=1, keepdims=True)
    own = jnp.sum(packing * lanes_of((ROWS, part)).astype(F32), axis=1, keepdims=True)
    base = low[:, 0:1].astype(F32)
    id_a = jnp.sum(packing * first.astype(F32), axis=1, keepdims=True) - base
    id_b = jnp.sum(packing * second.astype(F32), axis=1, keepdims=True) - base
    lane = lanes_of((ROWS, LANES))
    klane = (lane - HALF).astype(F32)
    in_block = (lane >= HALF) & (lane < HALF + class_block)
    flags = (in_block & ((klane == id_a) | (klane == id_b))) | (
        (lane - P_LANE).astype(F32) == own
    )
    flags = flags.astype(F32) * (valid > 0.5).astype(F32)
    packing = packing.astype(BF16)

    def put(value, start, size):
        value = value.astype(BF16)
        for owner in range(ROWS // 2):
            out_ref[owner, :, start : start + size] = value[2 * owner : 2 * owner + 2, :]

    quad_rows = jnp.dot(packing, quad, preferred_element_type=F32)
    put(jnp.where(lane < HALF, quad_rows, flags), FEATURES, LANES)
    wide = jnp.concatenate([factor] * 4, axis=1)
    step = 4 * LANES
    copies[3].wait()
    sent = []

    def leave(start, size):
        piece = pl.ds(start, size)
        copy = pltpu.make_async_copy(
            out_ref.at[:, :, piece], out_any.at[:, :, piece], sems.at[4 + len(sent)]
        )
        copy.start()
        sent.append(copy)

    leave(FEATURES, LANES)
    for t in range(FEATURES // step):
        part_w = (images_ref[:, t * step : (t + 1) * step].astype(F32) * wide).astype(BF16)
        put(jnp.dot(packing, part_w, preferred_element_type=F32), t * step, step)
        if t % 6 == 5:
            leave((t - 5) * step, 6 * step)
    for copy in sent:
        copy.wait()


def prep_body(classes_ref, table_ref, energy_ref):
    count = classes_ref.shape[0]
    acc = jnp.zeros((count, LANES), F32)
    for b in range(ROTATIONS):
        block = classes_ref[:, b * BLOCK : (b + 1) * BLOCK]
        m, c = b // 4, b % 4
        table_ref[c * HALF : c * HALF + count, m * BLOCK : (m + 1) * BLOCK] = block
        wide = block.astype(F32)
        square = wide * wide
        acc = acc + square[:, :LANES] + square[:, LANES:]
    for c in range(4):
        table_ref[c * HALF + count : (c + 1) * HALF, :] = jnp.zeros(
            (HALF - count, ROTATIONS // 4 * BLOCK), BF16
        )
    acc = acc + pltpu.roll(acc, HALF, 1)
    energy_ref[...] = jnp.zeros((LANES, LANES), F32)
    energy_ref[0:count, :] = acc
    energy_ref[HALF : HALF + count, :] = acc


def row_facts(meta):
    lane = lanes_of(meta.shape)
    flags = jnp.where((lane >= HALF) & (lane < P_LANE), meta, 0.0)
    flags = (flags + pltpu.roll(flags, HALF, 1)) > 0.5
    marks = jnp.where(lane >= P_LANE, meta, 0.0)
    valid = jnp.sum(marks, axis=1, keepdims=True)
    own = jnp.sum(marks * (lane - P_LANE).astype(F32), axis=1, keepdims=True)
    source = (rows_of(meta.shape) % ROWS // 2 * 4).astype(F32)
    spot = (lane.astype(F32) == source + own) & (valid > 0.5)
    return flags, spot


def slots_of(live):
    lane = lanes_of(live.shape)
    ids = (lane % HALF).astype(F32)
    low = jnp.min(jnp.where(live, ids, 1000.0), axis=1, keepdims=True)
    high = jnp.max(jnp.where(live, ids, -1.0), axis=1, keepdims=True)
    high = jnp.where(high > low, high, -1.0)
    return ids == low, ids == high, low < 999.0, high > -0.5


def correlate(rows_ref, table_ref, energy_ref, logits_ref, blocks_ref, acc_ref):
    total_rows = ROTATIONS * ROWS
    for b in range(TURNS):
        at = b % ROTATIONS * BLOCK
        blocks_ref[b * ROWS : (b + 1) * ROWS, :] = rows_ref[:, at : at + BLOCK]
    left = jnp.concatenate(
        [
            blocks_ref[4 * m * ROWS : 4 * m * ROWS + total_rows, :]
            for m in range(ROTATIONS // 4)
        ],
        axis=1,
    )
    acc_ref[...] = lax.dot_general(
        left, table_ref[...], (((1,), (1,)), ((), ())), preferred_element_type=F32
    )
    meta = rows_ref[:, FEATURES : FEATURES + LANES].astype(F32)
    lane = lanes_of((ROWS, LANES))
    quad = jnp.where(lane < HALF, meta, 0.0)
    norm = 0.5 * lax.dot_general(
        quad, energy_ref[...], (((1,), (1,)), ((), ())), precision=HIGH, preferred_element_type=F32
    )

    def tile(r, half):
        r = r % ROTATIONS
        return acc_ref[r * ROWS : (r + 1) * ROWS, half * LANES : (half + 1) * LANES]

    for r in range(ROTATIONS):
        mixed = jnp.where(lane < HALF, tile(r, 0), tile(r + 1, 0)) + jnp.where(
            lane < HALF, tile(r + 2, 1), tile(r + 3, 1)
        )
        logits_ref[r * ROWS : (r + 1) * ROWS, :] = mixed + pltpu.roll(mixed, HALF, 1) - norm


def cross_body(rows_ref, table_ref, energy_ref, logits_ref, stats_ref, blocks_ref, acc_ref):
    correlate(rows_ref, table_ref, energy_ref, logits_ref, blocks_ref, acc_ref)
    meta = rows_ref[:, FEATURES : FEATURES + LANES].astype(F32)
    lane = lanes_of((ROWS, LANES))
    live, spot = row_facts(meta)
    left = live & (lane < HALF)
    best = jnp.full((ROWS, LANES), NEGATIVE, F32)
    for r in range(ROTATIONS):
        value = logits_ref[r * ROWS : (r + 1) * ROWS, :]
        best = jnp.maximum(best, jnp.where(left, value, NEGATIVE))
    peak = jnp.max(best, axis=1, keepdims=True)
    total = jnp.zeros((ROWS, LANES), F32)
    for r in range(ROTATIONS):
        value = logits_ref[r * ROWS : (r + 1) * ROWS, :]
        total = total + jnp.where(left, jnp.exp(value - peak), 0.0)
    total = jnp.sum(total, axis=1, keepdims=True)
    peak_row = jnp.max(jnp.where(spot, peak, NEGATIVE), axis=0, keepdims=True)
    total_row = jnp.sum(jnp.where(spot, total, 0.0), axis=0, keepdims=True)
    for d in range(stats_ref.shape[0]):
        stats_ref[d, 0:1, :] = peak_row
        stats_ref[d, 1:2, :] = total_row


def share_body(one_ref, two_ref, one_logits_ref, two_logits_ref, mine_ref, theirs_ref):
    second = lax.axis_index("core") == 1
    pieces = []
    for b in range(ROTATIONS):
        for ref in (one_ref, two_ref):
            pieces.append(ref[:, b * BLOCK : (b + 1) * BLOCK])
    value = jnp.concatenate(pieces, axis=0).astype(F32)
    rolled = pltpu.roll(value, BLOCK - SLICE, 1)
    after = jnp.concatenate([rolled[2 * ROWS :, :], rolled[: 2 * ROWS, :]], axis=0)
    moved = jnp.where(lanes_of(value.shape) < BLOCK - SLICE, rolled, after)
    mine_ref[0:BLOCK, :] = jnp.where(second, moved, value).T.astype(BF16)
    theirs_ref[0:BLOCK, :] = jnp.where(second, value, moved).T.astype(BF16)
    columns = slice(FEATURES, FEATURES + LANES)
    meta = jnp.concatenate([one_ref[:, columns], two_ref[:, columns]], axis=0).astype(F32)
    lane = lanes_of(meta.shape)
    live, spot = row_facts(meta)
    first, other, has_first, has_other = slots_of(live)
    known = ((lane < ROTATIONS) & has_first) | (
        (lane >= ROTATIONS) & (lane < 2 * ROTATIONS) & has_other
    )
    quad = jnp.where(lane < HALF, meta, 0.0)
    quad = quad + pltpu.roll(quad, HALF, 1)
    one_mask = first & (lane < HALF)
    two_mask = other & (lane < HALF)
    compact = jnp.zeros(meta.shape, F32)
    for r in range(ROTATIONS):
        own = slice(r * ROWS, (r + 1) * ROWS)
        level = jnp.concatenate([one_logits_ref[own, :], two_logits_ref[own, :]], axis=0)
        one = jnp.sum(jnp.where(one_mask, level, 0.0), axis=1, keepdims=True)
        two = jnp.sum(jnp.where(two_mask, level, 0.0), axis=1, keepdims=True)
        compact = jnp.where(lane == r, one, jnp.where(lane == ROTATIONS + r, two, compact))
    high = compact.astype(BF16)
    left = compact - high.astype(F32)
    middle = left.astype(BF16)
    left = left - middle.astype(F32)
    for i, fact in enumerate((first, other, spot, known, quad, high, middle, left)):
        fact = fact.astype(F32).astype(BF16)
        for ref in (mine_ref, theirs_ref):
            ref[BLOCK:, i * LANES : (i + 1) * LANES] = fact
    for ref in (mine_ref, theirs_ref):
        ref[BLOCK:, 8 * LANES :] = jnp.zeros((2 * ROWS, DEPTH - 8 * LANES), BF16)


def settle_body(value_ref, out_ref):
    out_ref[...] = value_ref[...]


def sums_body(
    stats_ref, mine_ref, other_ref, out_any, evid_ref, pay_ref, table_a, table_b, sems
):
    core, near = lax.axis_index("core"), lax.axis_index("xl")
    tables = (table_a, table_b)
    lane = lanes_of((ROWS, LANES))
    on_left = lane < HALF
    weights, quads = [], []
    for g in range(4):
        facts_ref, table_ref = (mine_ref, other_ref)[g // 2], tables[g // 2]

        def fact(i):
            at = BLOCK + g % 2 * ROWS
            return facts_ref[at : at + ROWS, i * LANES : (i + 1) * LANES].astype(F32)

        at_core = core if g < 2 else 1 - core
        at_near = near if g % 2 == 0 else 1 - near
        stats = stats_ref[pl.ds((at_near * 2 + at_core) * 8, 8), :, :]
        peaks = stats[:, 0, :]
        totals = stats[:, 1, :]
        highest = jnp.max(peaks, axis=0, keepdims=True)
        total = jnp.sum(totals * jnp.exp(peaks - highest), axis=0, keepdims=True)
        evidence = highest + jnp.log(total)
        if g == 0:
            evid_ref[...] = evidence
        first, second = fact(0), fact(1)
        row_evidence = jnp.sum(
            jnp.where(fact(2) > 0.5, evidence, 0.0), axis=1, keepdims=True
        )
        logits = fact(5) + (fact(6) + fact(7))
        post = jnp.where(fact(3) > 0.5, jnp.exp(logits - row_evidence), 0.0)
        post = post.astype(BF16).astype(F32)
        total_one = jnp.sum(jnp.where(lane < ROTATIONS, post, 0.0), axis=1, keepdims=True)
        total_two = jnp.sum(jnp.where(lane < ROTATIONS, 0.0, post), axis=1, keepdims=True)
        weights.append(total_one * first + total_two * second)
        quads.append(fact(4))
        half = ROTATIONS // 2

        def spread(r):
            return (
                post[:, r : r + 1] * first + post[:, ROTATIONS + r : ROTATIONS + r + 1] * second
            )

        for r in range(half):
            here, there = spread(r), spread(r + half)
            for row, value in (
                (r, jnp.where(on_left, here, there)),
                (r + half, jnp.where(on_left, there, here)),
            ):
                value = value.astype(BF16)
                for turn in range(2):
                    at = ((turn * ROTATIONS + row) * 2 + g % 2) * ROWS
                    table_ref[at : at + ROWS, :] = value
    weight = jnp.concatenate(weights, axis=0)
    quad = jnp.concatenate(quads, axis=0)
    upper = weight.astype(BF16).astype(F32)
    parts = jnp.concatenate([upper, weight - upper], axis=0).T.astype(BF16)
    quad = jnp.concatenate([quad, quad], axis=0).astype(BF16)
    by_class = jnp.dot(parts, quad, preferred_element_type=F32)
    by_shell = by_class.T[0:HALF, :]
    tail = jnp.where(on_left, by_class[0:16, :], by_class[16:32, :]).astype(BF16)
    wide = lanes_of((HALF, LANES))
    spare = jnp.where(
        (wide >= CLASSES) & (wide < HALF),
        pltpu.roll(by_shell, CLASSES - 32, 1),
        jnp.where(wide >= HALF + CLASSES, pltpu.roll(by_shell, CLASSES - 46, 1), 0.0),
    ).astype(BF16)
    for d in range(TARGETS):
        pay_ref[d, 0:HALF, :] = spare
        pay_ref[d, PAY_ROWS : PAY_ROWS + 16, :] = tail
    copies = [
        pltpu.make_async_copy(pay_ref.at[d], out_any.at[d], sems.at[d]) for d in range(TARGETS)
    ]
    started = 0
    base = (ROTATIONS - CHUNKS * near) * 2 * ROWS
    for group in ((0, 1), (2, 3), (4, 5), (6, 7), (8,)):
        kept = {b: [i for i in range(16) if (16 * b + i) // CHUNKS % 2 == 0] for b in group}
        used = sorted(set(i for b in group for i in kept[b]))
        bands = []
        for i in used:
            if bands and bands[-1][1] == i:
                bands[-1][1] = i + 1
            else:
                bands.append([i, i + 1])
        left = jnp.concatenate(
            [
                jnp.concatenate([ref[16 * lo : 16 * hi, :] for lo, hi in bands], axis=0)
                for ref in (mine_ref, other_ref)
            ],
            axis=1,
        )
        columns = []
        for b in group:
            start = pl.multiple_of(base - b * 2 * ROWS, 2 * ROWS)
            columns.append(jnp.concatenate([ref[pl.ds(start, DEPTH), :] for ref in tables], axis=0))
        right = jnp.concatenate(columns, axis=1)
        out = jnp.dot(left, right, preferred_element_type=F32).astype(BF16)
        for c, b in enumerate(group):
            for i in kept[b]:
                n = used.index(i)
                for e in range(2):
                    q = b * 16 + i
                    d, j = e * 8 + q // CHUNKS // 2, q % CHUNKS
                    from_lane = c * LANES + e * HALF
                    piece = out[n * 16 : (n + 1) * 16, from_lane : from_lane + CLASSES]
                    if j < CHUNKS - 1:
                        at = j // 2 * 16
                        lo = j % 2 * HALF
                        pay_ref[d, at : at + 16, lo : lo + CLASSES] = piece
                    else:
                        pay_ref[d, PAY_ROWS - 8 : PAY_ROWS, 0:CLASSES] = piece[0:8, :]
                        pay_ref[d, PAY_ROWS - 8 : PAY_ROWS, HALF : HALF + CLASSES] = piece[8:16, :]
        finished = (16 * group[-1] + 16 + CHUNKS) // (2 * CHUNKS)
        for z in range(started, finished):
            copies[z].start()
            copies[8 + z].start()
        started = finished
    for copy in copies:
        copy.wait()


def final_body(parts_ref, sums_ref, weights_ref):
    acc = parts_ref[0, :, :].astype(F32)
    for g in range(1, TARGETS):
        acc = acc + parts_ref[g, :, :].astype(F32)
    pieces = []
    for j in range(CHUNKS - 1):
        lo = j % 2 * HALF
        pieces.append(acc[j // 2 * 16 : j // 2 * 16 + 16, lo : lo + HALF])
    pieces.append(acc[PAY_ROWS - 8 : PAY_ROWS, 0:HALF])
    pieces.append(acc[PAY_ROWS - 8 : PAY_ROWS, HALF:LANES])
    full = jnp.concatenate(pieces, axis=0)
    sums_ref[...] = full.T[0:CLASSES, :]
    weights_ref[0:16, :] = acc[PAY_ROWS : PAY_ROWS + 16, 0:HALF]
    weights_ref[16:32, :] = acc[PAY_ROWS : PAY_ROWS + 16, HALF:LANES]
    rest = acc[0:HALF, :].T
    weights_ref[32:46, :] = rest[CLASSES:HALF, :]
    weights_ref[46:CLASSES, :] = rest[HALF + CLASSES : HALF + CLASSES + 4, :]


def shards(images, ctf, inv_noise, classes, candidates):
    class_block = classes.shape[0]
    part = images.shape[0]
    my_index = lax.axis_index("cls")
    total_rows = ROTATIONS * ROWS
    width = FEATURES + LANES
    shape = jax.ShapeDtypeStruct
    vmem = pl.BlockSpec(memory_space=pltpu.VMEM)
    raw = pl.BlockSpec(memory_space=pltpu.HBM)

    def swap(value, axes):
        return lax.all_to_all(value, axes, split_axis=0, concat_axis=0, tiled=True)

    def flip(value, axis):
        return lax.ppermute(value, axis, [(0, 1), (1, 0)])

    def pack(*refs):
        pack_body(class_block, *refs)

    hbm = [
        pltpu.with_memory_space_constraint(value, pltpu.HBM)
        for value in (images, ctf, inv_noise.reshape(1, CYCLES), candidates.T)
    ]
    packed = call(
        pack,
        shape((8, 2, width), BF16),
        *hbm,
        in_specs=[raw] * 4,
        out_specs=raw,
        scratch=[
            pltpu.VMEM((part, FEATURES), BF16),
            pltpu.VMEM((part, CYCLES), F32),
            pltpu.VMEM((1, CYCLES), F32),
            pltpu.VMEM((2, part), jnp.int32),
            pltpu.VMEM((8, 2, width), BF16),
            pltpu.SemaphoreType.DMA((8,)),
        ],
    )
    rows = swap(packed, "cls").reshape(ROWS, width)
    table, energy = call(
        prep_body,
        (shape((BLOCK, ROTATIONS // 4 * BLOCK), BF16), shape((LANES, LANES), F32)),
        classes,
    )
    rows, table, energy = lax.optimization_barrier((rows, table, energy))
    beside = flip(rows, "xl")
    logits, stats = call(
        cross_body,
        (shape((total_rows, LANES), F32), shape((32, 2, LANES), F32)),
        rows,
        table,
        energy,
        scratch=[pltpu.VMEM((TURNS * ROWS, BLOCK), BF16), pltpu.VMEM((total_rows, BLOCK), F32)],
    )
    group_stats = swap(stats, ("xl", "core", "cls"))

    shared = shape((BLOCK + 2 * ROWS, DEPTH), BF16)

    def trade(one, two, one_logits):
        two_logits = call(
            correlate,
            shape((total_rows, LANES), F32),
            two,
            table,
            energy,
            scratch=[pltpu.VMEM((TURNS * ROWS, BLOCK), BF16), pltpu.VMEM((total_rows, BLOCK), F32)],
        )
        own, theirs = call(share_body, (shared, shared), one, two, one_logits, two_logits)
        return own, call(settle_body, shared, flip(theirs, "core"))

    def alone(one, two, one_logits):
        nothing = jnp.zeros(shared.shape, BF16)
        return nothing, nothing

    own_share, other_share = lax.cond(lax.axis_index("core") < 2, trade, alone, rows, beside, logits)
    pay, evidence = call(
        sums_body,
        (shape((TARGETS, PAY_ROWS + 16, LANES), BF16), shape((1, LANES), F32)),
        group_stats,
        own_share,
        other_share,
        out_specs=(raw, vmem),
        scratch=[
            pltpu.VMEM((TARGETS, PAY_ROWS + 16, LANES), BF16),
            pltpu.VMEM((2 * DEPTH, LANES), BF16),
            pltpu.VMEM((2 * DEPTH, LANES), BF16),
            pltpu.SemaphoreType.DMA((TARGETS,)),
        ],
    )
    parts = swap(pay, ("xh", "z"))
    sums, weight_sums = call(
        final_body, (shape((CLASSES, SLICE), F32), shape((CLASSES, CYCLES), F32)), parts
    )
    own = lax.dynamic_slice(evidence, (0, my_index * 4), (1, 4)).reshape(4)
    return sums.T, weight_sums, own


def solution(mesh):
    dom = ("xh", "xl", "z", "core")
    fine = Mesh(mesh.devices.reshape(2, 2, 8, 2, 8), dom + ("cls",))
    every = dom + ("cls",)
    in_specs = (P(every, None), P(every, None), P(), P("cls", None), P(every, None))
    out_specs = (P(dom, "cls"), P("cls", None), P(every))
    return jax.shard_map(shards, mesh=fine, in_specs=in_specs, out_specs=out_specs, check_vma=False)
```

```python
import jax
import jax.numpy as jnp
from jax import lax
from jax.experimental import pallas as pl
from jax.experimental.pallas import tpu as pltpu
from jax.sharding import Mesh, PartitionSpec as P

CYCLES = 64
ROTATIONS = 36
BLOCK = 256
FEATURES = ROTATIONS * BLOCK
LANES = 128
HALF = 64
ROWS = 16
TURNS = 2 * ROTATIONS - 4
GROUPS = 64
TARGETS = GROUPS // 4
DEPTH = 2 * ROTATIONS * ROWS
CLASSES = 50
SLICE = FEATURES // GROUPS
CHUNKS = SLICE // 16
PAY_ROWS = SLICE // 2
NEGATIVE = -1e30
P_LANE = 120
F32 = jnp.float32
BF16 = jnp.bfloat16
HIGH = lax.Precision.HIGHEST


def lanes_of(shape):
    return lax.broadcasted_iota(jnp.int32, shape, len(shape) - 1)


def rows_of(shape):
    return lax.broadcasted_iota(jnp.int32, shape, len(shape) - 2)


def call(body, outs, *args, in_specs=None, out_specs=None, scratch=()):
    more = {} if in_specs is None else {"in_specs": in_specs}
    if out_specs is not None:
        more["out_specs"] = out_specs
    return pl.pallas_call(
        body,
        out_shape=outs,
        scratch_shapes=list(scratch),
        compiler_params=pltpu.CompilerParams(vmem_limit_bytes=48 * 1024 * 1024),
        **more,
    )(*args)


def pack_body(class_block, images_any, ctf_any, noise_any, cands_any, out_any, images_ref, ctf_ref, noise_ref, cands_ref, out_ref, sems):
    copies = [
        pltpu.make_async_copy(source, target, sems.at[i])
        for i, (source, target) in enumerate(
            (
                (cands_any, cands_ref),
                (ctf_any, ctf_ref),
                (noise_any, noise_ref),
                (images_any, images_ref),
            )
        )
    ]
    for copy in copies:
        copy.start()
    for copy in copies[:3]:
        copy.wait()
    part = images_ref.shape[0]
    ctf = ctf_ref[...]
    noise = noise_ref[...]
    ctf_noise = ctf * noise
    factor = jnp.concatenate([ctf_noise, ctf_noise], axis=1)
    quad = (ctf * ctf * noise).astype(BF16)
    quad = jnp.concatenate([quad, quad], axis=1)
    cands = cands_ref[...]
    first = jnp.broadcast_to(cands[0:1, :], (ROWS, part))
    second = jnp.broadcast_to(cands[1:2, :], (ROWS, part))
    row = rows_of((ROWS, part))
    second_core = lax.axis_index("core") == 1
    owner = jnp.where(second_core, ROWS // 2 - 1 - row // 2, row // 2)
    low = owner * class_block
    hit = ((first >= low) & (first < low + class_block)) | (
        (second >= low) & (second < low + class_block)
    )
    hit = hit.astype(F32)
    taken = jnp.zeros((ROWS, 1), F32)
    columns = []
    slot = (rows_of((ROWS, 1)) % 2).astype(F32)
    for p in range(part):
        now = hit[:, p : p + 1]
        columns.append(now * (taken == slot).astype(F32))
        taken = taken + now
    packing = jnp.concatenate(columns, axis=1)
    valid = jnp.sum(packing, axis=1, keepdims=True)
    own = jnp.sum(packing * lanes_of((ROWS, part)).astype(F32), axis=1, keepdims=True)
    base = low[:, 0:1].astype(F32)
    id_a = jnp.sum(packing * first.astype(F32), axis=1, keepdims=True) - base
    id_b = jnp.sum(packing * second.astype(F32), axis=1, keepdims=True) - base
    lane = lanes_of((ROWS, LANES))
    klane = (lane - HALF).astype(F32)
    in_block = (lane >= HALF) & (lane < HALF + class_block)
    flags = (in_block & ((klane == id_a) | (klane == id_b))) | (
        (lane - P_LANE).astype(F32) == own
    )
    flags = flags.astype(F32) * (valid > 0.5).astype(F32)
    packing = packing.astype(BF16)

    def put(value, start, size):
        value = value.astype(BF16)
        for owner in range(ROWS // 2):
            out_ref[owner, :, start : start + size] = value[2 * owner : 2 * owner + 2, :]

    quad_rows = jnp.dot(packing, quad, preferred_element_type=F32)
    put(jnp.where(lane < HALF, quad_rows, flags), FEATURES, LANES)
    wide = jnp.concatenate([factor] * 4, axis=1)
    step = 4 * LANES
    copies[3].wait()
    sent = []

    def leave(start, size):
        piece = pl.ds(start, size)
        copy = pltpu.make_async_copy(
            out_ref.at[:, :, piece], out_any.at[:, :, piece], sems.at[4 + len(sent)]
        )
        copy.start()
        sent.append(copy)

    leave(FEATURES, LANES)
    for t in range(FEATURES // step):
        part_w = (images_ref[:, t * step : (t + 1) * step].astype(F32) * wide).astype(BF16)
        put(jnp.dot(packing, part_w, preferred_element_type=F32), t * step, step)
        if t % 6 == 5:
            leave((t - 5) * step, 6 * step)
    for copy in sent:
        copy.wait()


def prep_body(classes_ref, table_ref, energy_ref):
    count = classes_ref.shape[0]
    acc = jnp.zeros((count, LANES), F32)
    for b in range(ROTATIONS):
        block = classes_ref[:, b * BLOCK : (b + 1) * BLOCK]
        m, c = b // 4, b % 4
        table_ref[c * HALF : c * HALF + count, m * BLOCK : (m + 1) * BLOCK] = block
        wide = block.astype(F32)
        square = wide * wide
        acc = acc + square[:, :LANES] + square[:, LANES:]
    for c in range(4):
        table_ref[c * HALF + count : (c + 1) * HALF, :] = jnp.zeros(
            (HALF - count, ROTATIONS // 4 * BLOCK), BF16
        )
    acc = acc + pltpu.roll(acc, HALF, 1)
    energy_ref[...] = jnp.zeros((LANES, LANES), F32)
    energy_ref[0:count, :] = acc
    energy_ref[HALF : HALF + count, :] = acc


def row_facts(meta):
    lane = lanes_of(meta.shape)
    flags = jnp.where((lane >= HALF) & (lane < P_LANE), meta, 0.0)
    flags = (flags + pltpu.roll(flags, HALF, 1)) > 0.5
    marks = jnp.where(lane >= P_LANE, meta, 0.0)
    valid = jnp.sum(marks, axis=1, keepdims=True)
    own = jnp.sum(marks * (lane - P_LANE).astype(F32), axis=1, keepdims=True)
    source = rows_of(meta.shape) % ROWS // 2
    source = jnp.where(lax.axis_index("core") == 1, ROWS // 2 - 1 - source, source)
    source = (source * 4).astype(F32)
    spot = (lane.astype(F32) == source + own) & (valid > 0.5)
    return flags, spot


def slots_of(live):
    lane = lanes_of(live.shape)
    ids = (lane % HALF).astype(F32)
    low = jnp.min(jnp.where(live, ids, 1000.0), axis=1, keepdims=True)
    high = jnp.max(jnp.where(live, ids, -1.0), axis=1, keepdims=True)
    high = jnp.where(high > low, high, -1.0)
    return ids == low, ids == high, low < 999.0, high > -0.5


def correlate(rows_ref, table_ref, energy_ref, logits_ref, blocks_ref, acc_ref):
    total_rows = ROTATIONS * ROWS
    for b in range(TURNS):
        at = b % ROTATIONS * BLOCK
        blocks_ref[b * ROWS : (b + 1) * ROWS, :] = rows_ref[:, at : at + BLOCK]
    left = jnp.concatenate(
        [
            blocks_ref[4 * m * ROWS : 4 * m * ROWS + total_rows, :]
            for m in range(ROTATIONS // 4)
        ],
        axis=1,
    )
    acc_ref[...] = lax.dot_general(
        left, table_ref[...], (((1,), (1,)), ((), ())), preferred_element_type=F32
    )
    meta = rows_ref[:, FEATURES : FEATURES + LANES].astype(F32)
    lane = lanes_of((ROWS, LANES))
    quad = jnp.where(lane < HALF, meta, 0.0)
    norm = 0.5 * lax.dot_general(
        quad, energy_ref[...], (((1,), (1,)), ((), ())), precision=HIGH, preferred_element_type=F32
    )

    def tile(r, half):
        r = r % ROTATIONS
        return acc_ref[r * ROWS : (r + 1) * ROWS, half * LANES : (half + 1) * LANES]

    for r in range(ROTATIONS):
        mixed = jnp.where(lane < HALF, tile(r, 0), tile(r + 1, 0)) + jnp.where(
            lane < HALF, tile(r + 2, 1), tile(r + 3, 1)
        )
        logits_ref[r * ROWS : (r + 1) * ROWS, :] = mixed + pltpu.roll(mixed, HALF, 1) - norm


def cross_body(rows_ref, table_ref, energy_ref, logits_ref, stats_ref, blocks_ref, acc_ref):
    correlate(rows_ref, table_ref, energy_ref, logits_ref, blocks_ref, acc_ref)
    meta = rows_ref[:, FEATURES : FEATURES + LANES].astype(F32)
    lane = lanes_of((ROWS, LANES))
    live, spot = row_facts(meta)
    left = live & (lane < HALF)
    best = jnp.full((ROWS, LANES), NEGATIVE, F32)
    for r in range(ROTATIONS):
        value = logits_ref[r * ROWS : (r + 1) * ROWS, :]
        best = jnp.maximum(best, jnp.where(left, value, NEGATIVE))
    peak = jnp.max(best, axis=1, keepdims=True)
    total = jnp.zeros((ROWS, LANES), F32)
    for r in range(ROTATIONS):
        value = logits_ref[r * ROWS : (r + 1) * ROWS, :]
        total = total + jnp.where(left, jnp.exp(value - peak), 0.0)
    total = jnp.sum(total, axis=1, keepdims=True)
    peak_row = jnp.max(jnp.where(spot, peak, NEGATIVE), axis=0, keepdims=True)
    total_row = jnp.sum(jnp.where(spot, total, 0.0), axis=0, keepdims=True)
    for d in range(stats_ref.shape[0]):
        stats_ref[d, 0:1, :] = peak_row
        stats_ref[d, 1:2, :] = total_row


def share_body(one_ref, two_ref, one_logits_ref, two_logits_ref, mine_ref, theirs_ref):
    second = lax.axis_index("core") == 1
    pieces = []
    for b in range(ROTATIONS):
        for ref in (one_ref, two_ref):
            pieces.append(ref[:, b * BLOCK : (b + 1) * BLOCK])
    value = jnp.concatenate(pieces, axis=0).astype(F32)
    rolled = pltpu.roll(value, BLOCK - SLICE, 1)
    after = jnp.concatenate([rolled[2 * ROWS :, :], rolled[: 2 * ROWS, :]], axis=0)
    moved = jnp.where(lanes_of(value.shape) < BLOCK - SLICE, rolled, after)
    mine_ref[0:BLOCK, :] = jnp.where(second, moved, value).T.astype(BF16)
    theirs_ref[0:BLOCK, :] = jnp.where(second, value, moved).T.astype(BF16)
    columns = slice(FEATURES, FEATURES + LANES)
    meta = jnp.concatenate([one_ref[:, columns], two_ref[:, columns]], axis=0).astype(F32)
    lane = lanes_of(meta.shape)
    live, spot = row_facts(meta)
    first, other, has_first, has_other = slots_of(live)
    known = ((lane < ROTATIONS) & has_first) | (
        (lane >= ROTATIONS) & (lane < 2 * ROTATIONS) & has_other
    )
    quad = jnp.where(lane < HALF, meta, 0.0)
    quad = quad + pltpu.roll(quad, HALF, 1)
    one_mask = first & (lane < HALF)
    two_mask = other & (lane < HALF)
    compact = jnp.zeros(meta.shape, F32)
    for r in range(ROTATIONS):
        own = slice(r * ROWS, (r + 1) * ROWS)
        level = jnp.concatenate([one_logits_ref[own, :], two_logits_ref[own, :]], axis=0)
        one = jnp.sum(jnp.where(one_mask, level, 0.0), axis=1, keepdims=True)
        two = jnp.sum(jnp.where(two_mask, level, 0.0), axis=1, keepdims=True)
        compact = jnp.where(lane == r, one, jnp.where(lane == ROTATIONS + r, two, compact))
    high = compact.astype(BF16)
    left = compact - high.astype(F32)
    middle = left.astype(BF16)
    left = left - middle.astype(F32)
    for i, fact in enumerate((first, other, spot, known, quad, high, middle, left)):
        fact = fact.astype(F32).astype(BF16)
        for ref in (mine_ref, theirs_ref):
            ref[BLOCK:, i * LANES : (i + 1) * LANES] = fact
    for ref in (mine_ref, theirs_ref):
        ref[BLOCK:, 8 * LANES :] = jnp.zeros((2 * ROWS, DEPTH - 8 * LANES), BF16)


def settle_body(value_ref, out_ref):
    out_ref[...] = value_ref[...]


def sums_body(
    stats_ref, mine_ref, other_ref, out_any, evid_ref, pay_ref, table_a, table_b, sems
):
    core, near = lax.axis_index("core"), lax.axis_index("xl")
    tables = (table_a, table_b)
    lane = lanes_of((ROWS, LANES))
    on_left = lane < HALF
    weights, quads = [], []
    for g in range(4):
        facts_ref, table_ref = (mine_ref, other_ref)[g // 2], tables[g // 2]

        def fact(i):
            at = BLOCK + g % 2 * ROWS
            return facts_ref[at : at + ROWS, i * LANES : (i + 1) * LANES].astype(F32)

        at_core = core if g < 2 else 1 - core
        at_near = near if g % 2 == 0 else 1 - near
        stats = stats_ref[pl.ds((at_near * 2 + at_core) * 8, 8), :, :]
        peaks = stats[:, 0, :]
        totals = stats[:, 1, :]
        highest = jnp.max(peaks, axis=0, keepdims=True)
        total = jnp.sum(totals * jnp.exp(peaks - highest), axis=0, keepdims=True)
        evidence = highest + jnp.log(total)
        if g == 0:
            evid_ref[...] = evidence
        first, second = fact(0), fact(1)
        row_evidence = jnp.sum(
            jnp.where(fact(2) > 0.5, evidence, 0.0), axis=1, keepdims=True
        )
        logits = fact(5) + (fact(6) + fact(7))
        post = jnp.where(fact(3) > 0.5, jnp.exp(logits - row_evidence), 0.0)
        post = post.astype(BF16).astype(F32)
        total_one = jnp.sum(jnp.where(lane < ROTATIONS, post, 0.0), axis=1, keepdims=True)
        total_two = jnp.sum(jnp.where(lane < ROTATIONS, 0.0, post), axis=1, keepdims=True)
        weights.append(total_one * first + total_two * second)
        quads.append(fact(4))
        half = ROTATIONS // 2

        def spread(r):
            return (
                post[:, r : r + 1] * first + post[:, ROTATIONS + r : ROTATIONS + r + 1] * second
            )

        for r in range(half):
            here, there = spread(r), spread(r + half)
            for row, value in (
                (r, jnp.where(on_left, here, there)),
                (r + half, jnp.where(on_left, there, here)),
            ):
                value = value.astype(BF16)
                for turn in range(2):
                    at = ((turn * ROTATIONS + row) * 2 + g % 2) * ROWS
                    table_ref[at : at + ROWS, :] = value
    weight = jnp.concatenate(weights, axis=0)
    quad = jnp.concatenate(quads, axis=0)
    upper = weight.astype(BF16).astype(F32)
    parts = jnp.concatenate([upper, weight - upper], axis=0).T.astype(BF16)
    quad = jnp.concatenate([quad, quad], axis=0).astype(BF16)
    by_class = jnp.dot(parts, quad, preferred_element_type=F32)
    by_shell = by_class.T[0:HALF, :]
    tail = jnp.where(on_left, by_class[0:16, :], by_class[16:32, :]).astype(BF16)
    wide = lanes_of((HALF, LANES))
    spare = jnp.where(
        (wide >= CLASSES) & (wide < HALF),
        pltpu.roll(by_shell, CLASSES - 32, 1),
        jnp.where(wide >= HALF + CLASSES, pltpu.roll(by_shell, CLASSES - 46, 1), 0.0),
    ).astype(BF16)
    for d in range(TARGETS):
        pay_ref[d, 0:HALF, :] = spare
        pay_ref[d, PAY_ROWS : PAY_ROWS + 16, :] = tail
    copies = [
        pltpu.make_async_copy(
            pay_ref.at[d], out_any.at[jnp.where(core == 1, TARGETS - 1 - d, d)], sems.at[d]
        )
        for d in range(TARGETS)
    ]
    started = 0
    base = (ROTATIONS - CHUNKS * near) * 2 * ROWS
    for group in ((0, 1), (2, 3), (4, 5), (6, 7), (8,)):
        kept = {b: [i for i in range(16) if (16 * b + i) // CHUNKS % 2 == 0] for b in group}
        used = sorted(set(i for b in group for i in kept[b]))
        bands = []
        for i in used:
            if bands and bands[-1][1] == i:
                bands[-1][1] = i + 1
            else:
                bands.append([i, i + 1])
        left = jnp.concatenate(
            [
                jnp.concatenate([ref[16 * lo : 16 * hi, :] for lo, hi in bands], axis=0)
                for ref in (mine_ref, other_ref)
            ],
            axis=1,
        )
        columns = []
        for b in group:
            start = pl.multiple_of(base - b * 2 * ROWS, 2 * ROWS)
            columns.append(jnp.concatenate([ref[pl.ds(start, DEPTH), :] for ref in tables], axis=0))
        right = jnp.concatenate(columns, axis=1)
        out = jnp.dot(left, right, preferred_element_type=F32).astype(BF16)
        for c, b in enumerate(group):
            for i in kept[b]:
                n = used.index(i)
                for e in range(2):
                    q = b * 16 + i
                    d, j = e * 8 + q // CHUNKS // 2, q % CHUNKS
                    from_lane = c * LANES + e * HALF
                    piece = out[n * 16 : (n + 1) * 16, from_lane : from_lane + CLASSES]
                    if j < CHUNKS - 1:
                        at = j // 2 * 16
                        lo = j % 2 * HALF
                        pay_ref[d, at : at + 16, lo : lo + CLASSES] = piece
                    else:
                        pay_ref[d, PAY_ROWS - 8 : PAY_ROWS, 0:CLASSES] = piece[0:8, :]
                        pay_ref[d, PAY_ROWS - 8 : PAY_ROWS, HALF : HALF + CLASSES] = piece[8:16, :]
        finished = (16 * group[-1] + 16 + CHUNKS) // (2 * CHUNKS)
        for z in range(started, finished):
            copies[z].start()
            copies[8 + z].start()
        started = finished
    for copy in copies:
        copy.wait()


def final_body(parts_ref, sums_ref, weights_ref):
    acc = parts_ref[0, :, :].astype(F32)
    for g in range(1, TARGETS):
        acc = acc + parts_ref[g, :, :].astype(F32)
    pieces = []
    for j in range(CHUNKS - 1):
        lo = j % 2 * HALF
        pieces.append(acc[j // 2 * 16 : j // 2 * 16 + 16, lo : lo + HALF])
    pieces.append(acc[PAY_ROWS - 8 : PAY_ROWS, 0:HALF])
    pieces.append(acc[PAY_ROWS - 8 : PAY_ROWS, HALF:LANES])
    full = jnp.concatenate(pieces, axis=0)
    sums_ref[...] = full.T[0:CLASSES, :]
    weights_ref[0:16, :] = acc[PAY_ROWS : PAY_ROWS + 16, 0:HALF]
    weights_ref[16:32, :] = acc[PAY_ROWS : PAY_ROWS + 16, HALF:LANES]
    rest = acc[0:HALF, :].T
    weights_ref[32:46, :] = rest[CLASSES:HALF, :]
    weights_ref[46:CLASSES, :] = rest[HALF + CLASSES : HALF + CLASSES + 4, :]


def shards(images, ctf, inv_noise, classes, candidates):
    class_block = classes.shape[0]
    part = images.shape[0]
    my_index = lax.axis_index("cls")
    total_rows = ROTATIONS * ROWS
    width = FEATURES + LANES
    shape = jax.ShapeDtypeStruct
    vmem = pl.BlockSpec(memory_space=pltpu.VMEM)
    raw = pl.BlockSpec(memory_space=pltpu.HBM)

    def swap(value, axes):
        return lax.all_to_all(value, axes, split_axis=0, concat_axis=0, tiled=True)

    def swap_rows(value):
        groups = [list(range(8)), list(range(15, 7, -1))]
        return lax.all_to_all(value, ("core", "cls"), 0, 0, axis_index_groups=groups, tiled=True)

    def swap_both_ways(value, axes):
        count = value.shape[0]
        ahead = [2 * i for i in range(count)]
        groups = [ahead, [i + 1 for i in reversed(ahead)]]
        return lax.all_to_all(
            value, axes + ("core",), 0, 0, axis_index_groups=groups, tiled=True
        )

    def flip(value, axis):
        return lax.ppermute(value, axis, [(0, 1), (1, 0)])

    def pack(*refs):
        pack_body(class_block, *refs)

    hbm = [
        pltpu.with_memory_space_constraint(value, pltpu.HBM)
        for value in (images, ctf, inv_noise.reshape(1, CYCLES), candidates.T)
    ]
    packed = call(
        pack,
        shape((8, 2, width), BF16),
        *hbm,
        in_specs=[raw] * 4,
        out_specs=raw,
        scratch=[
            pltpu.VMEM((part, FEATURES), BF16),
            pltpu.VMEM((part, CYCLES), F32),
            pltpu.VMEM((1, CYCLES), F32),
            pltpu.VMEM((2, part), jnp.int32),
            pltpu.VMEM((8, 2, width), BF16),
            pltpu.SemaphoreType.DMA((8,)),
        ],
    )
    rows = swap_rows(packed).reshape(ROWS, width)
    table, energy = call(
        prep_body,
        (shape((BLOCK, ROTATIONS // 4 * BLOCK), BF16), shape((LANES, LANES), F32)),
        classes,
    )
    rows, table, energy = lax.optimization_barrier((rows, table, energy))
    beside = flip(rows, "xl")
    logits, stats = call(
        cross_body,
        (shape((total_rows, LANES), F32), shape((32, 2, LANES), F32)),
        rows,
        table,
        energy,
        scratch=[pltpu.VMEM((TURNS * ROWS, BLOCK), BF16), pltpu.VMEM((total_rows, BLOCK), F32)],
    )
    group_stats = swap(stats, ("xl", "core", "cls"))

    shared = shape((BLOCK + 2 * ROWS, DEPTH), BF16)

    def trade(one, two, one_logits):
        two_logits = call(
            correlate,
            shape((total_rows, LANES), F32),
            two,
            table,
            energy,
            scratch=[pltpu.VMEM((TURNS * ROWS, BLOCK), BF16), pltpu.VMEM((total_rows, BLOCK), F32)],
        )
        own, theirs = call(share_body, (shared, shared), one, two, one_logits, two_logits)
        return own, call(settle_body, shared, flip(theirs, "core"))

    def alone(one, two, one_logits):
        nothing = jnp.zeros(shared.shape, BF16)
        return nothing, nothing

    own_share, other_share = lax.cond(lax.axis_index("core") < 2, trade, alone, rows, beside, logits)
    pay, evidence = call(
        sums_body,
        (shape((TARGETS, PAY_ROWS + 16, LANES), BF16), shape((1, LANES), F32)),
        group_stats,
        own_share,
        other_share,
        out_specs=(raw, vmem),
        scratch=[
            pltpu.VMEM((TARGETS, PAY_ROWS + 16, LANES), BF16),
            pltpu.VMEM((2 * DEPTH, LANES), BF16),
            pltpu.VMEM((2 * DEPTH, LANES), BF16),
            pltpu.SemaphoreType.DMA((TARGETS,)),
        ],
    )
    parts = swap_both_ways(pay, ("xh", "z"))
    sums, weight_sums = call(
        final_body, (shape((CLASSES, SLICE), F32), shape((CLASSES, CYCLES), F32)), parts
    )
    own = lax.dynamic_slice(evidence, (0, my_index * 4), (1, 4)).reshape(4)
    return sums.T, weight_sums, own


def solution(mesh):
    dom = ("xh", "xl", "z", "core")
    fine = Mesh(mesh.devices.reshape(2, 2, 8, 2, 8), dom + ("cls",))
    every = dom + ("cls",)
    in_specs = (P(every, None), P(every, None), P(), P("cls", None), P(every, None))
    out_specs = (P(dom, "cls"), P("cls", None), P(every))
    return jax.shard_map(shards, mesh=fine, in_specs=in_specs, out_specs=out_specs, check_vma=False)
```

```python
import jax
import jax.numpy as jnp
from jax import lax
from jax.experimental import pallas as pl
from jax.experimental.pallas import tpu as pltpu
from jax.sharding import Mesh, PartitionSpec as P

CYCLES = 64
ROTATIONS = 36
BLOCK = 256
FEATURES = ROTATIONS * BLOCK
LANES = 128
HALF = 64
ROWS = 16
TURNS = 2 * ROTATIONS - 4
GROUPS = 64
TARGETS = GROUPS // 4
ROW_ORDER = ((1, 0), (7, 3))
SUM_ORDER = (
    [0, 1, 2, 3, 4, 5, 6, 7, 8, 9, 10, 11, 12, 13, 14, 15],
    [15, 14, 13, 12, 11, 10, 9, 8, 7, 6, 5, 4, 3, 2, 1, 0],
)
DEPTH = 2 * ROTATIONS * ROWS
CLASSES = 50
SLICE = FEATURES // GROUPS
CHUNKS = SLICE // 16
PAY_ROWS = SLICE // 2
NEGATIVE = -1e30
P_LANE = 120
F32 = jnp.float32
BF16 = jnp.bfloat16
HIGH = lax.Precision.HIGHEST


def lanes_of(shape):
    return lax.broadcasted_iota(jnp.int32, shape, len(shape) - 1)


def rows_of(shape):
    return lax.broadcasted_iota(jnp.int32, shape, len(shape) - 2)


def call(body, outs, *args, in_specs=None, out_specs=None, scratch=()):
    more = {} if in_specs is None else {"in_specs": in_specs}
    if out_specs is not None:
        more["out_specs"] = out_specs
    return pl.pallas_call(
        body,
        out_shape=outs,
        scratch_shapes=list(scratch),
        compiler_params=pltpu.CompilerParams(vmem_limit_bytes=48 * 1024 * 1024),
        **more,
    )(*args)


def pack_body(class_block, images_any, ctf_any, noise_any, cands_any, out_any, images_ref, ctf_ref, noise_ref, cands_ref, out_ref, sems):
    copies = [
        pltpu.make_async_copy(source, target, sems.at[i])
        for i, (source, target) in enumerate(
            (
                (cands_any, cands_ref),
                (ctf_any, ctf_ref),
                (noise_any, noise_ref),
                (images_any, images_ref),
            )
        )
    ]
    for copy in copies:
        copy.start()
    for copy in copies[:3]:
        copy.wait()
    part = images_ref.shape[0]
    ctf = ctf_ref[...]
    noise = noise_ref[...]
    ctf_noise = ctf * noise
    factor = jnp.concatenate([ctf_noise, ctf_noise], axis=1)
    quad = (ctf * ctf * noise).astype(BF16)
    quad = jnp.concatenate([quad, quad], axis=1)
    cands = cands_ref[...]
    first = jnp.broadcast_to(cands[0:1, :], (ROWS, part))
    second = jnp.broadcast_to(cands[1:2, :], (ROWS, part))
    row = rows_of((ROWS, part))
    second_core = lax.axis_index("core") == 1
    owner = (row // 2 * jnp.where(second_core, ROW_ORDER[1][0], ROW_ORDER[0][0]) + jnp.where(second_core, ROW_ORDER[1][1], ROW_ORDER[0][1])) % 8
    low = owner * class_block
    hit = ((first >= low) & (first < low + class_block)) | (
        (second >= low) & (second < low + class_block)
    )
    hit = hit.astype(F32)
    taken = jnp.zeros((ROWS, 1), F32)
    columns = []
    slot = (rows_of((ROWS, 1)) % 2).astype(F32)
    for p in range(part):
        now = hit[:, p : p + 1]
        columns.append(now * (taken == slot).astype(F32))
        taken = taken + now
    packing = jnp.concatenate(columns, axis=1)
    valid = jnp.sum(packing, axis=1, keepdims=True)
    own = jnp.sum(packing * lanes_of((ROWS, part)).astype(F32), axis=1, keepdims=True)
    base = low[:, 0:1].astype(F32)
    id_a = jnp.sum(packing * first.astype(F32), axis=1, keepdims=True) - base
    id_b = jnp.sum(packing * second.astype(F32), axis=1, keepdims=True) - base
    lane = lanes_of((ROWS, LANES))
    klane = (lane - HALF).astype(F32)
    in_block = (lane >= HALF) & (lane < HALF + class_block)
    flags = (in_block & ((klane == id_a) | (klane == id_b))) | (
        (lane - P_LANE).astype(F32) == own
    )
    flags = flags.astype(F32) * (valid > 0.5).astype(F32)
    packing = packing.astype(BF16)

    def put(value, start, size):
        value = value.astype(BF16)
        for owner in range(ROWS // 2):
            out_ref[owner, :, start : start + size] = value[2 * owner : 2 * owner + 2, :]

    quad_rows = jnp.dot(packing, quad, preferred_element_type=F32)
    put(jnp.where(lane < HALF, quad_rows, flags), FEATURES, LANES)
    wide = jnp.concatenate([factor] * 4, axis=1)
    step = 4 * LANES
    copies[3].wait()
    sent = []

    def leave(start, size):
        piece = pl.ds(start, size)
        copy = pltpu.make_async_copy(
            out_ref.at[:, :, piece], out_any.at[:, :, piece], sems.at[4 + len(sent)]
        )
        copy.start()
        sent.append(copy)

    leave(FEATURES, LANES)
    for t in range(FEATURES // step):
        part_w = (images_ref[:, t * step : (t + 1) * step].astype(F32) * wide).astype(BF16)
        put(jnp.dot(packing, part_w, preferred_element_type=F32), t * step, step)
        if t % 6 == 5:
            leave((t - 5) * step, 6 * step)
    for copy in sent:
        copy.wait()


def prep_body(classes_ref, table_ref, energy_ref):
    count = classes_ref.shape[0]
    acc = jnp.zeros((count, LANES), F32)
    for b in range(ROTATIONS):
        block = classes_ref[:, b * BLOCK : (b + 1) * BLOCK]
        m, c = b // 4, b % 4
        table_ref[c * HALF : c * HALF + count, m * BLOCK : (m + 1) * BLOCK] = block
        wide = block.astype(F32)
        square = wide * wide
        acc = acc + square[:, :LANES] + square[:, LANES:]
    for c in range(4):
        table_ref[c * HALF + count : (c + 1) * HALF, :] = jnp.zeros(
            (HALF - count, ROTATIONS // 4 * BLOCK), BF16
        )
    acc = acc + pltpu.roll(acc, HALF, 1)
    energy_ref[...] = jnp.zeros((LANES, LANES), F32)
    energy_ref[0:count, :] = acc
    energy_ref[HALF : HALF + count, :] = acc


def row_facts(meta):
    lane = lanes_of(meta.shape)
    flags = jnp.where((lane >= HALF) & (lane < P_LANE), meta, 0.0)
    flags = (flags + pltpu.roll(flags, HALF, 1)) > 0.5
    marks = jnp.where(lane >= P_LANE, meta, 0.0)
    valid = jnp.sum(marks, axis=1, keepdims=True)
    own = jnp.sum(marks * (lane - P_LANE).astype(F32), axis=1, keepdims=True)
    source = rows_of(meta.shape) % ROWS // 2
    second_core = lax.axis_index("core") == 1
    source = (source * jnp.where(second_core, ROW_ORDER[1][0], ROW_ORDER[0][0]) + jnp.where(second_core, ROW_ORDER[1][1], ROW_ORDER[0][1])) % 8
    source = (source * 4).astype(F32)
    spot = (lane.astype(F32) == source + own) & (valid > 0.5)
    return flags, spot


def slots_of(live):
    lane = lanes_of(live.shape)
    ids = (lane % HALF).astype(F32)
    low = jnp.min(jnp.where(live, ids, 1000.0), axis=1, keepdims=True)
    high = jnp.max(jnp.where(live, ids, -1.0), axis=1, keepdims=True)
    high = jnp.where(high > low, high, -1.0)
    return ids == low, ids == high, low < 999.0, high > -0.5


def correlate(rows_ref, table_ref, energy_ref, logits_ref, blocks_ref, acc_ref):
    total_rows = ROTATIONS * ROWS
    for b in range(TURNS):
        at = b % ROTATIONS * BLOCK
        blocks_ref[b * ROWS : (b + 1) * ROWS, :] = rows_ref[:, at : at + BLOCK]
    left = jnp.concatenate(
        [
            blocks_ref[4 * m * ROWS : 4 * m * ROWS + total_rows, :]
            for m in range(ROTATIONS // 4)
        ],
        axis=1,
    )
    acc_ref[...] = lax.dot_general(
        left, table_ref[...], (((1,), (1,)), ((), ())), preferred_element_type=F32
    )
    meta = rows_ref[:, FEATURES : FEATURES + LANES].astype(F32)
    lane = lanes_of((ROWS, LANES))
    quad = jnp.where(lane < HALF, meta, 0.0)
    norm = 0.5 * lax.dot_general(
        quad, energy_ref[...], (((1,), (1,)), ((), ())), precision=HIGH, preferred_element_type=F32
    )

    def tile(r, half):
        r = r % ROTATIONS
        return acc_ref[r * ROWS : (r + 1) * ROWS, half * LANES : (half + 1) * LANES]

    for r in range(ROTATIONS):
        mixed = jnp.where(lane < HALF, tile(r, 0), tile(r + 1, 0)) + jnp.where(
            lane < HALF, tile(r + 2, 1), tile(r + 3, 1)
        )
        logits_ref[r * ROWS : (r + 1) * ROWS, :] = mixed + pltpu.roll(mixed, HALF, 1) - norm


def cross_body(rows_ref, table_ref, energy_ref, logits_ref, stats_ref, blocks_ref, acc_ref):
    correlate(rows_ref, table_ref, energy_ref, logits_ref, blocks_ref, acc_ref)
    meta = rows_ref[:, FEATURES : FEATURES + LANES].astype(F32)
    lane = lanes_of((ROWS, LANES))
    live, spot = row_facts(meta)
    left = live & (lane < HALF)
    best = jnp.full((ROWS, LANES), NEGATIVE, F32)
    for r in range(ROTATIONS):
        value = logits_ref[r * ROWS : (r + 1) * ROWS, :]
        best = jnp.maximum(best, jnp.where(left, value, NEGATIVE))
    peak = jnp.max(best, axis=1, keepdims=True)
    total = jnp.zeros((ROWS, LANES), F32)
    for r in range(ROTATIONS):
        value = logits_ref[r * ROWS : (r + 1) * ROWS, :]
        total = total + jnp.where(left, jnp.exp(value - peak), 0.0)
    total = jnp.sum(total, axis=1, keepdims=True)
    peak_row = jnp.max(jnp.where(spot, peak, NEGATIVE), axis=0, keepdims=True)
    total_row = jnp.sum(jnp.where(spot, total, 0.0), axis=0, keepdims=True)
    for d in range(stats_ref.shape[0]):
        stats_ref[d, 0:1, :] = peak_row
        stats_ref[d, 1:2, :] = total_row


def share_body(one_ref, two_ref, one_logits_ref, two_logits_ref, mine_ref, theirs_ref):
    second = lax.axis_index("core") == 1
    pieces = []
    for b in range(ROTATIONS):
        for ref in (one_ref, two_ref):
            pieces.append(ref[:, b * BLOCK : (b + 1) * BLOCK])
    value = jnp.concatenate(pieces, axis=0).astype(F32)
    rolled = pltpu.roll(value, BLOCK - SLICE, 1)
    after = jnp.concatenate([rolled[2 * ROWS :, :], rolled[: 2 * ROWS, :]], axis=0)
    moved = jnp.where(lanes_of(value.shape) < BLOCK - SLICE, rolled, after)
    mine_ref[0:BLOCK, :] = jnp.where(second, moved, value).T.astype(BF16)
    theirs_ref[0:BLOCK, :] = jnp.where(second, value, moved).T.astype(BF16)
    columns = slice(FEATURES, FEATURES + LANES)
    meta = jnp.concatenate([one_ref[:, columns], two_ref[:, columns]], axis=0).astype(F32)
    lane = lanes_of(meta.shape)
    live, spot = row_facts(meta)
    first, other, has_first, has_other = slots_of(live)
    known = ((lane < ROTATIONS) & has_first) | (
        (lane >= ROTATIONS) & (lane < 2 * ROTATIONS) & has_other
    )
    quad = jnp.where(lane < HALF, meta, 0.0)
    quad = quad + pltpu.roll(quad, HALF, 1)
    one_mask = first & (lane < HALF)
    two_mask = other & (lane < HALF)
    compact = jnp.zeros(meta.shape, F32)
    for r in range(ROTATIONS):
        own = slice(r * ROWS, (r + 1) * ROWS)
        level = jnp.concatenate([one_logits_ref[own, :], two_logits_ref[own, :]], axis=0)
        one = jnp.sum(jnp.where(one_mask, level, 0.0), axis=1, keepdims=True)
        two = jnp.sum(jnp.where(two_mask, level, 0.0), axis=1, keepdims=True)
        compact = jnp.where(lane == r, one, jnp.where(lane == ROTATIONS + r, two, compact))
    high = compact.astype(BF16)
    left = compact - high.astype(F32)
    middle = left.astype(BF16)
    left = left - middle.astype(F32)
    for i, fact in enumerate((first, other, spot, known, quad, high, middle, left)):
        fact = fact.astype(F32).astype(BF16)
        for ref in (mine_ref, theirs_ref):
            ref[BLOCK:, i * LANES : (i + 1) * LANES] = fact
    for ref in (mine_ref, theirs_ref):
        ref[BLOCK:, 8 * LANES :] = jnp.zeros((2 * ROWS, DEPTH - 8 * LANES), BF16)


def settle_body(value_ref, out_ref):
    out_ref[...] = value_ref[...]


def sums_body(
    stats_ref, mine_ref, other_ref, out_any, evid_ref, pay_ref, table_a, table_b, sems
):
    core, near = lax.axis_index("core"), lax.axis_index("xl")
    tables = (table_a, table_b)
    lane = lanes_of((ROWS, LANES))
    on_left = lane < HALF
    weights, quads = [], []
    for g in range(4):
        facts_ref, table_ref = (mine_ref, other_ref)[g // 2], tables[g // 2]

        def fact(i):
            at = BLOCK + g % 2 * ROWS
            return facts_ref[at : at + ROWS, i * LANES : (i + 1) * LANES].astype(F32)

        at_core = core if g < 2 else 1 - core
        at_near = near if g % 2 == 0 else 1 - near
        stats = stats_ref[pl.ds((at_near * 2 + at_core) * 8, 8), :, :]
        peaks = stats[:, 0, :]
        totals = stats[:, 1, :]
        highest = jnp.max(peaks, axis=0, keepdims=True)
        total = jnp.sum(totals * jnp.exp(peaks - highest), axis=0, keepdims=True)
        evidence = highest + jnp.log(total)
        if g == 0:
            evid_ref[...] = evidence
        first, second = fact(0), fact(1)
        row_evidence = jnp.sum(
            jnp.where(fact(2) > 0.5, evidence, 0.0), axis=1, keepdims=True
        )
        logits = fact(5) + (fact(6) + fact(7))
        post = jnp.where(fact(3) > 0.5, jnp.exp(logits - row_evidence), 0.0)
        post = post.astype(BF16).astype(F32)
        total_one = jnp.sum(jnp.where(lane < ROTATIONS, post, 0.0), axis=1, keepdims=True)
        total_two = jnp.sum(jnp.where(lane < ROTATIONS, 0.0, post), axis=1, keepdims=True)
        weights.append(total_one * first + total_two * second)
        quads.append(fact(4))
        half = ROTATIONS // 2

        def spread(r):
            return (
                post[:, r : r + 1] * first + post[:, ROTATIONS + r : ROTATIONS + r + 1] * second
            )

        for r in range(half):
            here, there = spread(r), spread(r + half)
            for row, value in (
                (r, jnp.where(on_left, here, there)),
                (r + half, jnp.where(on_left, there, here)),
            ):
                value = value.astype(BF16)
                for turn in range(2):
                    at = ((turn * ROTATIONS + row) * 2 + g % 2) * ROWS
                    table_ref[at : at + ROWS, :] = value
    weight = jnp.concatenate(weights, axis=0)
    quad = jnp.concatenate(quads, axis=0)
    upper = weight.astype(BF16).astype(F32)
    parts = jnp.concatenate([upper, weight - upper], axis=0).T.astype(BF16)
    quad = jnp.concatenate([quad, quad], axis=0).astype(BF16)
    by_class = jnp.dot(parts, quad, preferred_element_type=F32)
    by_shell = by_class.T[0:HALF, :]
    tail = jnp.where(on_left, by_class[0:16, :], by_class[16:32, :]).astype(BF16)
    wide = lanes_of((HALF, LANES))
    spare = jnp.where(
        (wide >= CLASSES) & (wide < HALF),
        pltpu.roll(by_shell, CLASSES - 32, 1),
        jnp.where(wide >= HALF + CLASSES, pltpu.roll(by_shell, CLASSES - 46, 1), 0.0),
    ).astype(BF16)
    for d in range(TARGETS):
        pay_ref[d, 0:HALF, :] = spare
        pay_ref[d, PAY_ROWS : PAY_ROWS + 16, :] = tail
    copies = [
        pltpu.make_async_copy(
            pay_ref.at[d], out_any.at[jnp.where(core == 1, SUM_ORDER[1].index(d), SUM_ORDER[0].index(d))], sems.at[d]
        )
        for d in range(TARGETS)
    ]
    started = 0
    base = (ROTATIONS - CHUNKS * near) * 2 * ROWS
    for group in ((0, 1), (2, 3), (4, 5), (6, 7), (8,)):
        kept = {b: [i for i in range(16) if (16 * b + i) // CHUNKS % 2 == 0] for b in group}
        used = sorted(set(i for b in group for i in kept[b]))
        bands = []
        for i in used:
            if bands and bands[-1][1] == i:
                bands[-1][1] = i + 1
            else:
                bands.append([i, i + 1])
        left = jnp.concatenate(
            [
                jnp.concatenate([ref[16 * lo : 16 * hi, :] for lo, hi in bands], axis=0)
                for ref in (mine_ref, other_ref)
            ],
            axis=1,
        )
        columns = []
        for b in group:
            start = pl.multiple_of(base - b * 2 * ROWS, 2 * ROWS)
            columns.append(jnp.concatenate([ref[pl.ds(start, DEPTH), :] for ref in tables], axis=0))
        right = jnp.concatenate(columns, axis=1)
        out = jnp.dot(left, right, preferred_element_type=F32).astype(BF16)
        for c, b in enumerate(group):
            for i in kept[b]:
                n = used.index(i)
                for e in range(2):
                    q = b * 16 + i
                    d, j = e * 8 + q // CHUNKS // 2, q % CHUNKS
                    from_lane = c * LANES + e * HALF
                    piece = out[n * 16 : (n + 1) * 16, from_lane : from_lane + CLASSES]
                    if j < CHUNKS - 1:
                        at = j // 2 * 16
                        lo = j % 2 * HALF
                        pay_ref[d, at : at + 16, lo : lo + CLASSES] = piece
                    else:
                        pay_ref[d, PAY_ROWS - 8 : PAY_ROWS, 0:CLASSES] = piece[0:8, :]
                        pay_ref[d, PAY_ROWS - 8 : PAY_ROWS, HALF : HALF + CLASSES] = piece[8:16, :]
        finished = (16 * group[-1] + 16 + CHUNKS) // (2 * CHUNKS)
        for z in range(started, finished):
            copies[z].start()
            copies[8 + z].start()
        started = finished
    for copy in copies:
        copy.wait()


def final_body(parts_ref, sums_ref, weights_ref):
    acc = parts_ref[0, :, :].astype(F32)
    for g in range(1, TARGETS):
        acc = acc + parts_ref[g, :, :].astype(F32)
    pieces = []
    for j in range(CHUNKS - 1):
        lo = j % 2 * HALF
        pieces.append(acc[j // 2 * 16 : j // 2 * 16 + 16, lo : lo + HALF])
    pieces.append(acc[PAY_ROWS - 8 : PAY_ROWS, 0:HALF])
    pieces.append(acc[PAY_ROWS - 8 : PAY_ROWS, HALF:LANES])
    full = jnp.concatenate(pieces, axis=0)
    sums_ref[...] = full.T[0:CLASSES, :]
    weights_ref[0:16, :] = acc[PAY_ROWS : PAY_ROWS + 16, 0:HALF]
    weights_ref[16:32, :] = acc[PAY_ROWS : PAY_ROWS + 16, HALF:LANES]
    rest = acc[0:HALF, :].T
    weights_ref[32:46, :] = rest[CLASSES:HALF, :]
    weights_ref[46:CLASSES, :] = rest[HALF + CLASSES : HALF + CLASSES + 4, :]


def shards(images, ctf, inv_noise, classes, candidates):
    class_block = classes.shape[0]
    part = images.shape[0]
    my_index = lax.axis_index("cls")
    total_rows = ROTATIONS * ROWS
    width = FEATURES + LANES
    shape = jax.ShapeDtypeStruct
    vmem = pl.BlockSpec(memory_space=pltpu.VMEM)
    raw = pl.BlockSpec(memory_space=pltpu.HBM)

    def swap(value, axes):
        return lax.all_to_all(value, axes, split_axis=0, concat_axis=0, tiled=True)

    def swap_rows(value):
        groups = [[8 * c + (ROW_ORDER[c][0] * p + ROW_ORDER[c][1]) % 8 for p in range(8)] for c in range(2)]
        return lax.all_to_all(value, ("core", "cls"), 0, 0, axis_index_groups=groups, tiled=True)

    def swap_both_ways(value, axes):
        groups = [[2 * SUM_ORDER[c][p] + c for p in range(TARGETS)] for c in range(2)]
        return lax.all_to_all(
            value, axes + ("core",), 0, 0, axis_index_groups=groups, tiled=True
        )

    def flip(value, axis):
        return lax.ppermute(value, axis, [(0, 1), (1, 0)])

    def pack(*refs):
        pack_body(class_block, *refs)

    hbm = [
        pltpu.with_memory_space_constraint(value, pltpu.HBM)
        for value in (images, ctf, inv_noise.reshape(1, CYCLES), candidates.T)
    ]
    packed = call(
        pack,
        shape((8, 2, width), BF16),
        *hbm,
        in_specs=[raw] * 4,
        out_specs=raw,
        scratch=[
            pltpu.VMEM((part, FEATURES), BF16),
            pltpu.VMEM((part, CYCLES), F32),
            pltpu.VMEM((1, CYCLES), F32),
            pltpu.VMEM((2, part), jnp.int32),
            pltpu.VMEM((8, 2, width), BF16),
            pltpu.SemaphoreType.DMA((8,)),
        ],
    )
    rows = swap_rows(packed).reshape(ROWS, width)
    table, energy = call(
        prep_body,
        (shape((BLOCK, ROTATIONS // 4 * BLOCK), BF16), shape((LANES, LANES), F32)),
        classes,
    )
    rows, table, energy = lax.optimization_barrier((rows, table, energy))
    beside = flip(rows, "xl")
    logits, stats = call(
        cross_body,
        (shape((total_rows, LANES), F32), shape((32, 2, LANES), F32)),
        rows,
        table,
        energy,
        scratch=[pltpu.VMEM((TURNS * ROWS, BLOCK), BF16), pltpu.VMEM((total_rows, BLOCK), F32)],
    )
    group_stats = swap(stats, ("xl", "core", "cls"))

    shared = shape((BLOCK + 2 * ROWS, DEPTH), BF16)

    def trade(one, two, one_logits):
        two_logits = call(
            correlate,
            shape((total_rows, LANES), F32),
            two,
            table,
            energy,
            scratch=[pltpu.VMEM((TURNS * ROWS, BLOCK), BF16), pltpu.VMEM((total_rows, BLOCK), F32)],
        )
        own, theirs = call(share_body, (shared, shared), one, two, one_logits, two_logits)
        return own, call(settle_body, shared, flip(theirs, "core"))

    def alone(one, two, one_logits):
        nothing = jnp.zeros(shared.shape, BF16)
        return nothing, nothing

    own_share, other_share = lax.cond(lax.axis_index("core") < 2, trade, alone, rows, beside, logits)
    pay, evidence = call(
        sums_body,
        (shape((TARGETS, PAY_ROWS + 16, LANES), BF16), shape((1, LANES), F32)),
        group_stats,
        own_share,
        other_share,
        out_specs=(raw, vmem),
        scratch=[
            pltpu.VMEM((TARGETS, PAY_ROWS + 16, LANES), BF16),
            pltpu.VMEM((2 * DEPTH, LANES), BF16),
            pltpu.VMEM((2 * DEPTH, LANES), BF16),
            pltpu.SemaphoreType.DMA((TARGETS,)),
        ],
    )
    parts = swap_both_ways(pay, ("xh", "z"))
    sums, weight_sums = call(
        final_body, (shape((CLASSES, SLICE), F32), shape((CLASSES, CYCLES), F32)), parts
    )
    own = lax.dynamic_slice(evidence, (0, my_index * 4), (1, 4)).reshape(4)
    return sums.T, weight_sums, own


def solution(mesh):
    dom = ("xh", "xl", "z", "core")
    fine = Mesh(mesh.devices.reshape(2, 2, 8, 2, 8), dom + ("cls",))
    every = dom + ("cls",)
    in_specs = (P(every, None), P(every, None), P(), P("cls", None), P(every, None))
    out_specs = (P(dom, "cls"), P("cls", None), P(every))
    return jax.shard_map(shards, mesh=fine, in_specs=in_specs, out_specs=out_specs, check_vma=False)
```

```python
import jax
import jax.numpy as jnp
from jax import lax
from jax.experimental import pallas as pl
from jax.experimental.pallas import tpu as pltpu
from jax.sharding import Mesh, PartitionSpec as P

CYCLES = 64
ROTATIONS = 36
BLOCK = 256
FEATURES = ROTATIONS * BLOCK
LANES = 128
HALF = 64
ROWS = 16
TURNS = 2 * ROTATIONS - 4
GROUPS = 64
TARGETS = GROUPS // 4
DEPTH = 2 * ROTATIONS * ROWS
CLASSES = 50
SLICE = FEATURES // GROUPS
CHUNKS = SLICE // 16
PAY_ROWS = SLICE // 2
NEGATIVE = -1e30
P_LANE = 120
F32 = jnp.float32
BF16 = jnp.bfloat16
HIGH = lax.Precision.HIGHEST


def lanes_of(shape):
    return lax.broadcasted_iota(jnp.int32, shape, len(shape) - 1)


def rows_of(shape):
    return lax.broadcasted_iota(jnp.int32, shape, len(shape) - 2)


def call(body, outs, *args, in_specs=None, out_specs=None, scratch=()):
    more = {} if in_specs is None else {"in_specs": in_specs}
    if out_specs is not None:
        more["out_specs"] = out_specs
    return pl.pallas_call(
        body,
        out_shape=outs,
        scratch_shapes=list(scratch),
        compiler_params=pltpu.CompilerParams(vmem_limit_bytes=48 * 1024 * 1024),
        **more,
    )(*args)


def pack_body(class_block, images_any, ctf_any, noise_any, cands_any, out_any, images_ref, ctf_ref, noise_ref, cands_ref, out_ref, sems):
    copies = [
        pltpu.make_async_copy(source, target, sems.at[i])
        for i, (source, target) in enumerate(
            (
                (cands_any, cands_ref),
                (ctf_any, ctf_ref),
                (noise_any, noise_ref),
                (images_any, images_ref),
            )
        )
    ]
    for copy in copies:
        copy.start()
    for copy in copies[:3]:
        copy.wait()
    part = images_ref.shape[0]
    ctf = ctf_ref[...]
    noise = noise_ref[...]
    ctf_noise = ctf * noise
    factor = jnp.concatenate([ctf_noise, ctf_noise], axis=1)
    quad = (ctf * ctf * noise).astype(BF16)
    quad = jnp.concatenate([quad, quad], axis=1)
    cands = cands_ref[...]
    first = jnp.broadcast_to(cands[0:1, :], (ROWS, part))
    second = jnp.broadcast_to(cands[1:2, :], (ROWS, part))
    row = rows_of((ROWS, part))
    second_core = lax.axis_index("core") == 1
    owner = jnp.where(second_core, ROWS // 2 - 1 - row // 2, row // 2)
    low = owner * class_block
    hit = ((first >= low) & (first < low + class_block)) | (
        (second >= low) & (second < low + class_block)
    )
    hit = hit.astype(F32)
    taken = jnp.zeros((ROWS, 1), F32)
    columns = []
    slot = (rows_of((ROWS, 1)) % 2).astype(F32)
    for p in range(part):
        now = hit[:, p : p + 1]
        columns.append(now * (taken == slot).astype(F32))
        taken = taken + now
    packing = jnp.concatenate(columns, axis=1)
    valid = jnp.sum(packing, axis=1, keepdims=True)
    own = jnp.sum(packing * lanes_of((ROWS, part)).astype(F32), axis=1, keepdims=True)
    base = low[:, 0:1].astype(F32)
    id_a = jnp.sum(packing * first.astype(F32), axis=1, keepdims=True) - base
    id_b = jnp.sum(packing * second.astype(F32), axis=1, keepdims=True) - base
    lane = lanes_of((ROWS, LANES))
    klane = (lane - HALF).astype(F32)
    in_block = (lane >= HALF) & (lane < HALF + class_block)
    flags = (in_block & ((klane == id_a) | (klane == id_b))) | (
        (lane - P_LANE).astype(F32) == own
    )
    flags = flags.astype(F32) * (valid > 0.5).astype(F32)
    packing = packing.astype(BF16)

    def put(value, start, size):
        value = value.astype(BF16)
        for owner in range(ROWS // 2):
            out_ref[owner, :, start : start + size] = value[2 * owner : 2 * owner + 2, :]

    quad_rows = jnp.dot(packing, quad, preferred_element_type=F32)
    put(jnp.where(lane < HALF, quad_rows, flags), FEATURES, LANES)
    wide = jnp.concatenate([factor] * 4, axis=1)
    step = 4 * LANES
    copies[3].wait()
    sent = []

    def leave(start, size):
        piece = pl.ds(start, size)
        copy = pltpu.make_async_copy(
            out_ref.at[:, :, piece], out_any.at[:, :, piece], sems.at[4 + len(sent)]
        )
        copy.start()
        sent.append(copy)

    leave(FEATURES, LANES)
    for t in range(FEATURES // step):
        part_w = (images_ref[:, t * step : (t + 1) * step].astype(F32) * wide).astype(BF16)
        put(jnp.dot(packing, part_w, preferred_element_type=F32), t * step, step)
        if t % 3 == 2:
            leave((t - 2) * step, 3 * step)
    for copy in sent:
        copy.wait()


def prep_body(classes_ref, table_ref, energy_ref):
    count = classes_ref.shape[0]
    acc = jnp.zeros((count, LANES), F32)
    for b in range(ROTATIONS):
        block = classes_ref[:, b * BLOCK : (b + 1) * BLOCK]
        m, c = b // 4, b % 4
        table_ref[c * HALF : c * HALF + count, m * BLOCK : (m + 1) * BLOCK] = block
        wide = block.astype(F32)
        square = wide * wide
        acc = acc + square[:, :LANES] + square[:, LANES:]
    for c in range(4):
        table_ref[c * HALF + count : (c + 1) * HALF, :] = jnp.zeros(
            (HALF - count, ROTATIONS // 4 * BLOCK), BF16
        )
    acc = acc + pltpu.roll(acc, HALF, 1)
    energy_ref[...] = jnp.zeros((LANES, LANES), F32)
    energy_ref[0:count, :] = acc
    energy_ref[HALF : HALF + count, :] = acc


def row_facts(meta):
    lane = lanes_of(meta.shape)
    flags = jnp.where((lane >= HALF) & (lane < P_LANE), meta, 0.0)
    flags = (flags + pltpu.roll(flags, HALF, 1)) > 0.5
    marks = jnp.where(lane >= P_LANE, meta, 0.0)
    valid = jnp.sum(marks, axis=1, keepdims=True)
    own = jnp.sum(marks * (lane - P_LANE).astype(F32), axis=1, keepdims=True)
    source = rows_of(meta.shape) % ROWS // 2
    source = jnp.where(lax.axis_index("core") == 1, ROWS // 2 - 1 - source, source)
    source = (source * 4).astype(F32)
    spot = (lane.astype(F32) == source + own) & (valid > 0.5)
    return flags, spot


def slots_of(live):
    lane = lanes_of(live.shape)
    ids = (lane % HALF).astype(F32)
    low = jnp.min(jnp.where(live, ids, 1000.0), axis=1, keepdims=True)
    high = jnp.max(jnp.where(live, ids, -1.0), axis=1, keepdims=True)
    high = jnp.where(high > low, high, -1.0)
    return ids == low, ids == high, low < 999.0, high > -0.5


def correlate(rows_ref, table_ref, energy_ref, logits_ref, blocks_ref, acc_ref):
    total_rows = ROTATIONS * ROWS
    for b in range(TURNS):
        at = b % ROTATIONS * BLOCK
        blocks_ref[b * ROWS : (b + 1) * ROWS, :] = rows_ref[:, at : at + BLOCK]
    left = jnp.concatenate(
        [
            blocks_ref[4 * m * ROWS : 4 * m * ROWS + total_rows, :]
            for m in range(ROTATIONS // 4)
        ],
        axis=1,
    )
    acc_ref[...] = lax.dot_general(
        left, table_ref[...], (((1,), (1,)), ((), ())), preferred_element_type=F32
    )
    meta = rows_ref[:, FEATURES : FEATURES + LANES].astype(F32)
    lane = lanes_of((ROWS, LANES))
    quad = jnp.where(lane < HALF, meta, 0.0)
    norm = 0.5 * lax.dot_general(
        quad, energy_ref[...], (((1,), (1,)), ((), ())), precision=HIGH, preferred_element_type=F32
    )

    def tile(r, half):
        r = r % ROTATIONS
        return acc_ref[r * ROWS : (r + 1) * ROWS, half * LANES : (half + 1) * LANES]

    for r in range(ROTATIONS):
        mixed = jnp.where(lane < HALF, tile(r, 0), tile(r + 1, 0)) + jnp.where(
            lane < HALF, tile(r + 2, 1), tile(r + 3, 1)
        )
        logits_ref[r * ROWS : (r + 1) * ROWS, :] = mixed + pltpu.roll(mixed, HALF, 1) - norm


def cross_body(rows_ref, table_ref, energy_ref, logits_ref, stats_ref, blocks_ref, acc_ref):
    correlate(rows_ref, table_ref, energy_ref, logits_ref, blocks_ref, acc_ref)
    meta = rows_ref[:, FEATURES : FEATURES + LANES].astype(F32)
    lane = lanes_of((ROWS, LANES))
    live, spot = row_facts(meta)
    left = live & (lane < HALF)
    best = jnp.full((ROWS, LANES), NEGATIVE, F32)
    for r in range(ROTATIONS):
        value = logits_ref[r * ROWS : (r + 1) * ROWS, :]
        best = jnp.maximum(best, jnp.where(left, value, NEGATIVE))
    peak = jnp.max(best, axis=1, keepdims=True)
    total = jnp.zeros((ROWS, LANES), F32)
    for r in range(ROTATIONS):
        value = logits_ref[r * ROWS : (r + 1) * ROWS, :]
        total = total + jnp.where(left, jnp.exp(value - peak), 0.0)
    total = jnp.sum(total, axis=1, keepdims=True)
    peak_row = jnp.max(jnp.where(spot, peak, NEGATIVE), axis=0, keepdims=True)
    total_row = jnp.sum(jnp.where(spot, total, 0.0), axis=0, keepdims=True)
    for d in range(stats_ref.shape[0]):
        stats_ref[d, 0:1, :] = peak_row
        stats_ref[d, 1:2, :] = total_row


def share_body(one_ref, two_ref, one_logits_ref, two_logits_ref, mine_ref, theirs_ref):
    second = lax.axis_index("core") == 1
    pieces = []
    for b in range(ROTATIONS):
        for ref in (one_ref, two_ref):
            pieces.append(ref[:, b * BLOCK : (b + 1) * BLOCK])
    value = jnp.concatenate(pieces, axis=0).astype(F32)
    rolled = pltpu.roll(value, BLOCK - SLICE, 1)
    after = jnp.concatenate([rolled[2 * ROWS :, :], rolled[: 2 * ROWS, :]], axis=0)
    moved = jnp.where(lanes_of(value.shape) < BLOCK - SLICE, rolled, after)
    mine_ref[0:BLOCK, :] = jnp.where(second, moved, value).T.astype(BF16)
    theirs_ref[0:BLOCK, :] = jnp.where(second, value, moved).T.astype(BF16)
    columns = slice(FEATURES, FEATURES + LANES)
    meta = jnp.concatenate([one_ref[:, columns], two_ref[:, columns]], axis=0).astype(F32)
    lane = lanes_of(meta.shape)
    live, spot = row_facts(meta)
    first, other, has_first, has_other = slots_of(live)
    known = ((lane < ROTATIONS) & has_first) | (
        (lane >= ROTATIONS) & (lane < 2 * ROTATIONS) & has_other
    )
    quad = jnp.where(lane < HALF, meta, 0.0)
    quad = quad + pltpu.roll(quad, HALF, 1)
    one_mask = first & (lane < HALF)
    two_mask = other & (lane < HALF)
    compact = jnp.zeros(meta.shape, F32)
    for r in range(ROTATIONS):
        own = slice(r * ROWS, (r + 1) * ROWS)
        level = jnp.concatenate([one_logits_ref[own, :], two_logits_ref[own, :]], axis=0)
        one = jnp.sum(jnp.where(one_mask, level, 0.0), axis=1, keepdims=True)
        two = jnp.sum(jnp.where(two_mask, level, 0.0), axis=1, keepdims=True)
        compact = jnp.where(lane == r, one, jnp.where(lane == ROTATIONS + r, two, compact))
    high = compact.astype(BF16)
    left = compact - high.astype(F32)
    middle = left.astype(BF16)
    left = left - middle.astype(F32)
    for i, fact in enumerate((first, other, spot, known, quad, high, middle, left)):
        fact = fact.astype(F32).astype(BF16)
        for ref in (mine_ref, theirs_ref):
            ref[BLOCK:, i * LANES : (i + 1) * LANES] = fact
    for ref in (mine_ref, theirs_ref):
        ref[BLOCK:, 8 * LANES :] = jnp.zeros((2 * ROWS, DEPTH - 8 * LANES), BF16)


def settle_body(value_ref, out_ref):
    out_ref[...] = value_ref[...]


def sums_body(
    stats_ref, mine_ref, other_ref, out_any, evid_ref, pay_ref, table_a, table_b, sems
):
    core, near = lax.axis_index("core"), lax.axis_index("xl")
    tables = (table_a, table_b)
    lane = lanes_of((ROWS, LANES))
    on_left = lane < HALF
    weights, quads = [], []
    for g in range(4):
        facts_ref, table_ref = (mine_ref, other_ref)[g // 2], tables[g // 2]

        def fact(i):
            at = BLOCK + g % 2 * ROWS
            return facts_ref[at : at + ROWS, i * LANES : (i + 1) * LANES].astype(F32)

        at_core = core if g < 2 else 1 - core
        at_near = near if g % 2 == 0 else 1 - near
        stats = stats_ref[pl.ds((at_near * 2 + at_core) * 8, 8), :, :]
        peaks = stats[:, 0, :]
        totals = stats[:, 1, :]
        highest = jnp.max(peaks, axis=0, keepdims=True)
        total = jnp.sum(totals * jnp.exp(peaks - highest), axis=0, keepdims=True)
        evidence = highest + jnp.log(total)
        if g == 0:
            evid_ref[...] = evidence
        first, second = fact(0), fact(1)
        row_evidence = jnp.sum(
            jnp.where(fact(2) > 0.5, evidence, 0.0), axis=1, keepdims=True
        )
        logits = fact(5) + (fact(6) + fact(7))
        post = jnp.where(fact(3) > 0.5, jnp.exp(logits - row_evidence), 0.0)
        post = post.astype(BF16).astype(F32)
        total_one = jnp.sum(jnp.where(lane < ROTATIONS, post, 0.0), axis=1, keepdims=True)
        total_two = jnp.sum(jnp.where(lane < ROTATIONS, 0.0, post), axis=1, keepdims=True)
        weights.append(total_one * first + total_two * second)
        quads.append(fact(4))
        half = ROTATIONS // 2

        def spread(r):
            return (
                post[:, r : r + 1] * first + post[:, ROTATIONS + r : ROTATIONS + r + 1] * second
            )

        for r in range(half):
            here, there = spread(r), spread(r + half)
            for row, value in (
                (r, jnp.where(on_left, here, there)),
                (r + half, jnp.where(on_left, there, here)),
            ):
                value = value.astype(BF16)
                for turn in range(2):
                    at = ((turn * ROTATIONS + row) * 2 + g % 2) * ROWS
                    table_ref[at : at + ROWS, :] = value
    weight = jnp.concatenate(weights, axis=0)
    quad = jnp.concatenate(quads, axis=0)
    upper = weight.astype(BF16).astype(F32)
    parts = jnp.concatenate([upper, weight - upper], axis=0).T.astype(BF16)
    quad = jnp.concatenate([quad, quad], axis=0).astype(BF16)
    by_class = jnp.dot(parts, quad, preferred_element_type=F32)
    by_shell = by_class.T[0:HALF, :]
    tail = jnp.where(on_left, by_class[0:16, :], by_class[16:32, :]).astype(BF16)
    wide = lanes_of((HALF, LANES))
    spare = jnp.where(
        (wide >= CLASSES) & (wide < HALF),
        pltpu.roll(by_shell, CLASSES - 32, 1),
        jnp.where(wide >= HALF + CLASSES, pltpu.roll(by_shell, CLASSES - 46, 1), 0.0),
    ).astype(BF16)
    for d in range(TARGETS):
        pay_ref[d, 0:HALF, :] = spare
        pay_ref[d, PAY_ROWS : PAY_ROWS + 16, :] = tail
    copies = [
        pltpu.make_async_copy(
            pay_ref.at[d], out_any.at[jnp.where(core == 1, TARGETS - 1 - d, d)], sems.at[d]
        )
        for d in range(TARGETS)
    ]
    started = 0
    base = (ROTATIONS - CHUNKS * near) * 2 * ROWS
    for group in ((0, 1), (2, 3), (4, 5), (6, 7), (8,)):
        kept = {b: [i for i in range(16) if (16 * b + i) // CHUNKS % 2 == 0] for b in group}
        used = sorted(set(i for b in group for i in kept[b]))
        bands = []
        for i in used:
            if bands and bands[-1][1] == i:
                bands[-1][1] = i + 1
            else:
                bands.append([i, i + 1])
        left = jnp.concatenate(
            [
                jnp.concatenate([ref[16 * lo : 16 * hi, :] for lo, hi in bands], axis=0)
                for ref in (mine_ref, other_ref)
            ],
            axis=1,
        )
        columns = []
        for b in group:
            start = pl.multiple_of(base - b * 2 * ROWS, 2 * ROWS)
            columns.append(jnp.concatenate([ref[pl.ds(start, DEPTH), :] for ref in tables], axis=0))
        right = jnp.concatenate(columns, axis=1)
        out = jnp.dot(left, right, preferred_element_type=F32).astype(BF16)
        for c, b in enumerate(group):
            for i in kept[b]:
                n = used.index(i)
                for e in range(2):
                    q = b * 16 + i
                    d, j = e * 8 + q // CHUNKS // 2, q % CHUNKS
                    from_lane = c * LANES + e * HALF
                    piece = out[n * 16 : (n + 1) * 16, from_lane : from_lane + CLASSES]
                    if j < CHUNKS - 1:
                        at = j // 2 * 16
                        lo = j % 2 * HALF
                        pay_ref[d, at : at + 16, lo : lo + CLASSES] = piece
                    else:
                        pay_ref[d, PAY_ROWS - 8 : PAY_ROWS, 0:CLASSES] = piece[0:8, :]
                        pay_ref[d, PAY_ROWS - 8 : PAY_ROWS, HALF : HALF + CLASSES] = piece[8:16, :]
        finished = (16 * group[-1] + 16 + CHUNKS) // (2 * CHUNKS)
        for z in range(started, finished):
            copies[z].start()
            copies[8 + z].start()
        started = finished
    for copy in copies:
        copy.wait()


def final_body(parts_ref, sums_ref, weights_ref):
    acc = parts_ref[0, :, :].astype(F32)
    for g in range(1, TARGETS):
        acc = acc + parts_ref[g, :, :].astype(F32)
    pieces = []
    for j in range(CHUNKS - 1):
        lo = j % 2 * HALF
        pieces.append(acc[j // 2 * 16 : j // 2 * 16 + 16, lo : lo + HALF])
    pieces.append(acc[PAY_ROWS - 8 : PAY_ROWS, 0:HALF])
    pieces.append(acc[PAY_ROWS - 8 : PAY_ROWS, HALF:LANES])
    full = jnp.concatenate(pieces, axis=0)
    sums_ref[...] = full.T[0:CLASSES, :]
    weights_ref[0:16, :] = acc[PAY_ROWS : PAY_ROWS + 16, 0:HALF]
    weights_ref[16:32, :] = acc[PAY_ROWS : PAY_ROWS + 16, HALF:LANES]
    rest = acc[0:HALF, :].T
    weights_ref[32:46, :] = rest[CLASSES:HALF, :]
    weights_ref[46:CLASSES, :] = rest[HALF + CLASSES : HALF + CLASSES + 4, :]


def shards(images, ctf, inv_noise, classes, candidates):
    class_block = classes.shape[0]
    part = images.shape[0]
    my_index = lax.axis_index("cls")
    total_rows = ROTATIONS * ROWS
    width = FEATURES + LANES
    shape = jax.ShapeDtypeStruct
    vmem = pl.BlockSpec(memory_space=pltpu.VMEM)
    raw = pl.BlockSpec(memory_space=pltpu.HBM)

    def swap(value, axes):
        return lax.all_to_all(value, axes, split_axis=0, concat_axis=0, tiled=True)

    def swap_rows(value):
        groups = [list(range(8)), list(range(15, 7, -1))]
        return lax.all_to_all(value, ("core", "cls"), 0, 0, axis_index_groups=groups, tiled=True)

    def swap_both_ways(value, axes):
        count = value.shape[0]
        ahead = [2 * i for i in range(count)]
        groups = [ahead, [i + 1 for i in reversed(ahead)]]
        return lax.all_to_all(
            value, axes + ("core",), 0, 0, axis_index_groups=groups, tiled=True
        )

    def flip(value, axis):
        return lax.ppermute(value, axis, [(0, 1), (1, 0)])

    def pack(*refs):
        pack_body(class_block, *refs)

    hbm = [
        pltpu.with_memory_space_constraint(value, pltpu.HBM)
        for value in (images, ctf, inv_noise.reshape(1, CYCLES), candidates.T)
    ]
    packed = call(
        pack,
        shape((8, 2, width), BF16),
        *hbm,
        in_specs=[raw] * 4,
        out_specs=raw,
        scratch=[
            pltpu.VMEM((part, FEATURES), BF16),
            pltpu.VMEM((part, CYCLES), F32),
            pltpu.VMEM((1, CYCLES), F32),
            pltpu.VMEM((2, part), jnp.int32),
            pltpu.VMEM((8, 2, width), BF16),
            pltpu.SemaphoreType.DMA((11,)),
        ],
    )
    rows = swap_rows(packed).reshape(ROWS, width)
    table, energy = call(
        prep_body,
        (shape((BLOCK, ROTATIONS // 4 * BLOCK), BF16), shape((LANES, LANES), F32)),
        classes,
    )
    rows, table, energy = lax.optimization_barrier((rows, table, energy))
    beside = flip(rows, "xl")
    logits, stats = call(
        cross_body,
        (shape((total_rows, LANES), F32), shape((32, 2, LANES), F32)),
        rows,
        table,
        energy,
        scratch=[pltpu.VMEM((TURNS * ROWS, BLOCK), BF16), pltpu.VMEM((total_rows, BLOCK), F32)],
    )
    group_stats = swap(stats, ("xl", "core", "cls"))

    shared = shape((BLOCK + 2 * ROWS, DEPTH), BF16)

    def trade(one, two, one_logits):
        two_logits = call(
            correlate,
            shape((total_rows, LANES), F32),
            two,
            table,
            energy,
            scratch=[pltpu.VMEM((TURNS * ROWS, BLOCK), BF16), pltpu.VMEM((total_rows, BLOCK), F32)],
        )
        own, theirs = call(share_body, (shared, shared), one, two, one_logits, two_logits)
        return own, call(settle_body, shared, flip(theirs, "core"))

    def alone(one, two, one_logits):
        nothing = jnp.zeros(shared.shape, BF16)
        return nothing, nothing

    own_share, other_share = lax.cond(lax.axis_index("core") < 2, trade, alone, rows, beside, logits)
    pay, evidence = call(
        sums_body,
        (shape((TARGETS, PAY_ROWS + 16, LANES), BF16), shape((1, LANES), F32)),
        group_stats,
        own_share,
        other_share,
        out_specs=(raw, vmem),
        scratch=[
            pltpu.VMEM((TARGETS, PAY_ROWS + 16, LANES), BF16),
            pltpu.VMEM((2 * DEPTH, LANES), BF16),
            pltpu.VMEM((2 * DEPTH, LANES), BF16),
            pltpu.SemaphoreType.DMA((TARGETS,)),
        ],
    )
    parts = swap_both_ways(pay, ("xh", "z"))
    sums, weight_sums = call(
        final_body, (shape((CLASSES, SLICE), F32), shape((CLASSES, CYCLES), F32)), parts
    )
    own = lax.dynamic_slice(evidence, (0, my_index * 4), (1, 4)).reshape(4)
    return sums.T, weight_sums, own


def solution(mesh):
    dom = ("xh", "xl", "z", "core")
    fine = Mesh(mesh.devices.reshape(2, 2, 8, 2, 8), dom + ("cls",))
    every = dom + ("cls",)
    in_specs = (P(every, None), P(every, None), P(), P("cls", None), P(every, None))
    out_specs = (P(dom, "cls"), P("cls", None), P(every))
    return jax.shard_map(shards, mesh=fine, in_specs=in_specs, out_specs=out_specs, check_vma=False)
```
